512 devices in a mesh: seq: 128 (over z_hi, y, x, core), chan: 4 (over z_lo).
Axes of the slice: x: 4, y: 8, z: 8 (z_hi: 2, z_lo: 4; z = z_hi * 4 + z_lo), core: 2. Of those that a mesh axis runs over, the one named last changes fastest.
Arguments:
- residual: bfloat16 [16384, 8192], P('seq', 'chan'), may hold values from -64 to 64
- query_in: bfloat16 [16384, 8192], P('seq', 'chan'), may hold values from -6 to 6
- key_in: bfloat16 [16384, 8192], P('seq', 'chan'), may hold values from -6 to 6
- value_in: bfloat16 [16384, 8192], P('seq', 'chan'), may hold values from -6 to 6
- short_filter: float32 [3, 3, 8192], P(None, None, 'chan'), may hold values from -3.5 to 3.5
- decay_rate: float32 [16, 8192], P(None, 'chan'), may hold values from 0 to 1
- residue: float32 [16, 8192], P(None, 'chan'), may hold values from -1.5 to 1.5
- skip_gain: float32 [8192], P('chan'), may hold values from -3 to 3
- norm_gain: float32 [8192], P('chan'), may hold values from 0.1 to 1.9
Outputs:
- residual_out: bfloat16 [16384, 8192], P('seq', 'chan')
- normed: bfloat16 [16384, 8192], P('seq', 'chan')
The draws below stay inside these ranges and needn't reach their ends.
All inputs are finite; a program needn't handle non-finite values.
Results may differ from the reference program's by a relative error of at most 0.0055.
Values may be sent and summed in bfloat16 or wider, within the bound.
No kernel may reach another device: no remote copies, remote signals or barrier semaphores. Data moves between devices by JAX's collectives and lax.ppermute only.
A program may use at most 128 MiB of HBM per device.

```python
import math
import jax
import jax.numpy as jnp
from jax import lax

D = 8192
POLES = 16
SHORT = 3
SEQ_LEN = 16384


def draw_decay_rate(key, part):
    first = jax.random.fold_in(key, 0)
    lowest = math.log(0.3 / SEQ_LEN)
    highest = math.log(1.0 / 16.0)
    spread = jax.random.uniform(first, (POLES, D), jnp.float32, lowest, highest)
    return jnp.exp(spread).astype(jnp.float32)


def draw_residual(key, part):
    first, second, third = jax.random.split(key, 3)
    row_scale = jnp.exp(jax.random.uniform(first, (SEQ_LEN, 1), jnp.float32, math.log(0.3), math.log(3.0)))
    column_scale = jnp.exp(jax.random.uniform(second, (1, D), jnp.float32, math.log(0.3), math.log(3.0)))
    along = jnp.arange(D, dtype=jnp.float32)[None, :] / max(D - 1, 1)
    base = jnp.clip(jax.random.normal(third, (SEQ_LEN, D), jnp.float32), -4.0, 4.0)
    ramp = jnp.exp(0.5 * math.log(3.0) * along)
    return (base * row_scale * column_scale * ramp).astype(jnp.bfloat16)


def levels(key, dims, cuts, low, largest):
    def one(position, parts):
        draws = jax.random.uniform(jax.random.fold_in(jax.random.fold_in(key, 6), position), (parts,), jnp.float32, low / len(cuts), largest / len(cuts))
        return jnp.repeat(jnp.exp(draws), dims[position] // parts).reshape((-1,) + (1,) * (len(dims) - position - 1))

    gain = one(*cuts[0])
    for cut in cuts[1:]:
        gain = gain * one(*cut)
    return gain


def gaussian(own_key, dims, scale, bound, shards=(), kind=jnp.bfloat16):
    array = scale * jax.random.normal(own_key, dims, jnp.float32)
    if shards:
        array = array * levels(own_key, dims, shards, -0.22, 0.18)
    return jnp.clip(array, -bound, bound).astype(kind)


def setup_inputs(seed: int = 0) -> dict:
    key_of = jax.random.split(jax.random.key(seed), 10)
    return {
        "residual": draw_residual(jax.random.fold_in(key_of[9], 71), 0),
        "query_in": gaussian(key_of[1], (SEQ_LEN, D), 1.0, 6.0, ((0, 128), (1, 4))),
        "key_in": gaussian(key_of[2], (SEQ_LEN, D), 1.0, 6.0, ((0, 128), (1, 4))),
        "value_in": gaussian(key_of[3], (SEQ_LEN, D), 1.0, 6.0, ((0, 128), (1, 4))),
        "short_filter": gaussian(key_of[4], (3, SHORT, D), SHORT ** -0.5, 3.5, ((2, 4),), jnp.float32),
        "decay_rate": draw_decay_rate(jax.random.fold_in(key_of[9], 71), 0),
        "residue": gaussian(key_of[6], (POLES, D), 0.25, 1.5, ((1, 4),), jnp.float32),
        "skip_gain": gaussian(key_of[7], (D,), 0.5, 3.0, ((0, 4),), jnp.float32),
        "norm_gain": jnp.clip(1.0 + 0.18 * jax.random.normal(key_of[8], (D,), jnp.float32), 0.1, 1.9),
    }


def reference(residual, query_in, key_in, value_in, short_filter, decay_rate, residue, skip_gain, norm_gain):
    lag_rows = SHORT - 1
    filters = short_filter.astype(jnp.float32)
    decays = decay_rate.astype(jnp.float32)
    factor = jnp.exp(-decays)
    weights = residue.astype(jnp.float32) * jnp.sqrt(2.0 * decays)
    direct = skip_gain.astype(jnp.float32)
    gains = norm_gain.astype(jnp.float32)

    def advance(carried, inputs):
        previous, state = carried
        stream_row, query_row, key_row, value_row = inputs
        current = jnp.stack([query_row, key_row, value_row]).astype(jnp.float32)
        window = jnp.concatenate([current[:, None, :], previous], axis=1)
        features = lax.optimization_barrier(jnp.sum(filters * window, axis=1))
        mixed = features[1] * features[2]
        state = factor * state + mixed[None, :]
        convolved = lax.optimization_barrier(jnp.sum(weights * state, axis=0))
        gated = features[0] * (convolved + direct * mixed)
        summed = (stream_row.astype(jnp.float32) + gated).astype(jnp.bfloat16)
        widened = lax.optimization_barrier(summed).astype(jnp.float32)
        inverse_rms = lax.rsqrt(jnp.mean(widened * widened) + 1e-06)
        normed = (widened * inverse_rms * gains).astype(jnp.bfloat16)
        return ((window[:, :lag_rows, :], state), (summed, normed))
    initial = (jnp.zeros((3, lag_rows, D), jnp.float32), jnp.zeros((POLES, D), jnp.float32))
    _, outputs = lax.scan(advance, initial, (residual, query_in, key_in, value_in))
    return (outputs[0], outputs[1])
```

```python
import functools

import jax
import jax.numpy as jnp
from jax import lax
from jax.experimental import pallas as pl
from jax.experimental.pallas import tpu as pltpu
from jax.sharding import PartitionSpec as P

D = 8192
EPSILON = 1e-06
LANES = 128
SUBLANES = 8
MINOR = 8
MIDDLE = 8
MAJOR = 2
STEP = 6

f32 = jnp.float32
bf16 = jnp.bfloat16


def call(kernel, out_shape, name, scratch=(), **extra):
    return pl.pallas_call(
        kernel,
        out_shape=out_shape,
        scratch_shapes=scratch,
        compiler_params=pltpu.CompilerParams(vmem_limit_bytes=14 << 20),
        name=name,
        **extra,
    )


def spread(source, target, first=0):
    items, chans = source.shape
    groups = chans // LANES
    for j in range(groups):
        target[pl.ds(first * groups + j, items, stride=groups), :] = source[
            :, j * LANES : (j + 1) * LANES
        ].astype(f32)


def tile(ref, item, half, groups):
    start = item * groups + half * SUBLANES
    if not isinstance(start, int):
        start = pl.multiple_of(start, SUBLANES)
    return ref[pl.ds(start, SUBLANES), :]


def put(ref, item, half, groups, value):
    start = item * groups + half * SUBLANES
    if not isinstance(start, int):
        start = pl.multiple_of(start, SUBLANES)
    ref[pl.ds(start, SUBLANES), :] = value


def taps_of(taps_ref, which, half, groups):
    return [tile(taps_ref, which * 3 + lag, half, groups) for lag in range(3)]


def fir(taps, now, last, older):
    return taps[0] * now + taps[1] * last + taps[2] * older


def tails_kernel(query_in, key_in, value_in, tails):
    last = [x[...].astype(f32)[-2:] for x in (query_in, key_in, value_in)]
    tails[...] = jnp.concatenate(last, axis=0).astype(bf16)


def first_kernel(
    key_in, value_in, filters, decay_rate, mixed, heads, taps, rates, partial, keys, values
):
    tokens, chans = key_in.shape
    groups = chans // LANES
    poles = decay_rate.shape[0]
    spread(decay_rate, rates)
    for which in range(3):
        spread(filters.at[which], taps, 3 * which)
    spread(key_in, keys)
    spread(value_in, values)
    heads[: 2 * groups, :] = keys[: 2 * groups, :]
    heads[2 * groups :, :] = values[: 2 * groups, :]
    for half in range(groups // SUBLANES):
        key_taps = taps_of(taps, 1, half, groups)
        value_taps = taps_of(taps, 2, half, groups)
        factor = [jnp.exp(-tile(rates, n, half, groups)) for n in range(poles)]

        def turn(i, carry):
            k1, k2, v1, v2, *state = carry
            for u in range(STEP):
                t = 2 + i * STEP + u
                k0 = tile(keys, t, half, groups)
                v0 = tile(values, t, half, groups)
                m = fir(key_taps, k0, k1, k2) * fir(value_taps, v0, v1, v2)
                put(mixed, t, half, groups, m)
                state = [factor[n] * state[n] + m for n in range(poles)]
                k1, k2, v1, v2 = k0, k1, v0, v1
            return (k1, k2, v1, v2, *state)

        begin = (
            tile(keys, 1, half, groups),
            tile(keys, 0, half, groups),
            tile(values, 1, half, groups),
            tile(values, 0, half, groups),
        ) + (jnp.zeros((SUBLANES, LANES), f32),) * poles
        end = lax.fori_loop(0, (tokens - 2) // STEP, turn, begin)
        for n in range(poles):
            put(partial, n, half, groups, end[4 + n])
        for t in range(2):
            put(mixed, t, half, groups, jnp.zeros((SUBLANES, LANES), f32))


def state_kernel(tokens, tails, heads, taps, rates, partial, state, opening, before):
    groups = tails.shape[1] // LANES
    poles = rates.shape[0] // groups
    spread(tails, before)
    for half in range(groups // SUBLANES):
        m = []
        for t in range(2):
            pair = []
            for side in range(2):
                line = [tile(before, 2 * side + 2 + r, half, groups) for r in range(2)]
                line += [tile(heads, 2 * side + r, half, groups) for r in range(2)]
                tap = taps_of(taps, 1 + side, half, groups)
                pair.append(fir(tap, line[t + 2], line[t + 1], line[t]))
            m.append(pair[0] * pair[1])
            put(opening, t, half, groups, m[t])
        for n in range(poles):
            rate = tile(rates, n, half, groups)
            total = (
                tile(partial, n, half, groups)
                + jnp.exp(-rate * (tokens - 1.0)) * m[0]
                + jnp.exp(-rate * (tokens - 2.0)) * m[1]
            )
            put(before, n, half, groups, total)
    state[...] = before[...].astype(bf16)


def inner_kernel(
    query_in, tails, taps, rates, residue, skip, mixed, opening, base, query, lead, rows, weights
):
    tokens, chans = query_in.shape
    groups = chans // LANES
    poles = residue.shape[0]
    spread(residue, weights)
    spread(tails, rows)
    spread(query_in, rows, 2)
    for half in range(groups // SUBLANES):
        query_taps = taps_of(taps, 0, half, groups)
        factor, weight = [], []
        for n in range(poles):
            rate = tile(rates, n, half, groups)
            factor.append(jnp.exp(-rate))
            weight.append(tile(weights, n, half, groups) * jnp.sqrt(2.0 * rate))
            put(lead, n, half, groups, weight[n] * factor[n])
        direct = tile(skip, 0, half, groups)

        def follow(state, m):
            state = [factor[n] * state[n] + m for n in range(poles)]
            parts = [direct * m, weight[0] * state[0]]
            for n in range(1, poles):
                parts[n % 2] = parts[n % 2] + weight[n] * state[n]
            return state, parts[0] + parts[1]

        state = [jnp.zeros((SUBLANES, LANES), f32)] * poles
        for t in range(2):
            state, out = follow(state, tile(opening, t, half, groups))
            put(base, t, half, groups, out)

        def turn(i, state):
            for u in range(STEP):
                t = 2 + i * STEP + u
                state, out = follow(state, tile(mixed, t, half, groups))
                put(base, t, half, groups, out)
            return tuple(state)

        lax.fori_loop(0, (tokens - 2) // STEP, turn, tuple(state))

        def filtered(i, carry):
            q1, q2 = carry
            for u in range(8):
                t = i * 8 + u
                q0 = tile(rows, t + 2, half, groups)
                put(query, t, half, groups, fir(query_taps, q0, q1, q2))
                q1, q2 = q0, q1
            return q1, q2

        lax.fori_loop(
            0, tokens // 8, filtered, (tile(rows, 1, half, groups), tile(rows, 0, half, groups))
        )


def pair_rates(rates, place, rows):
    return rates[pl.ds(pl.multiple_of(place * rows, SUBLANES), rows), :]


def minor_kernel(block, place, arrived, rates, sums, prefix):
    rows = arrived.shape[0] // MINOR
    decay = jnp.exp(-pair_rates(rates, place[0] % MINOR, rows) * block)
    total = jnp.zeros((rows, LANES), f32)
    for b in range(MINOR):
        prefix[b * rows : (b + 1) * rows, :] = total
        total = decay * total + arrived[b * rows : (b + 1) * rows, :].astype(f32)
    total = total.astype(bf16)
    for other in range(MIDDLE):
        sums[other * rows : (other + 1) * rows, :] = total


def middle_kernel(block, place, arrived, rates, prefix, carries):
    rows = arrived.shape[0] // MIDDLE
    rate = pair_rates(rates, place[0] % MINOR, rows)
    mine = (place[0] // MINOR) % MIDDLE
    lower = place[0] < MINOR * MIDDLE
    decay = jnp.exp(-rate * block)
    line_decay = jnp.exp(-rate * (block * MINOR))
    before = jnp.zeros((rows, LANES), f32)
    whole = jnp.zeros((rows, LANES), f32)
    for other in range(MIDDLE):
        piece = arrived[other * rows : (other + 1) * rows, :].astype(f32)
        whole = line_decay * whole + piece
        before = jnp.where(other < mine, whole, before)
    onward = jnp.exp(-rate * (mine.astype(f32) * (block * MINOR))) * whole
    half_rows = MINOR * rows
    for b in range(MINOR):
        here = before + prefix[b * rows : (b + 1) * rows, :]
        carries[b * rows : (b + 1) * rows, :] = jnp.where(lower, here, 0.0).astype(bf16)
        carries[half_rows + b * rows : half_rows + (b + 1) * rows, :] = jnp.where(
            lower, onward, here
        ).astype(bf16)
        before = decay * before
        onward = decay * onward


def outer_kernel(carries, rates, lead, base, query, residual, summed, squares, gated):
    tokens, chans = residual.shape
    groups = chans // LANES
    poles = rates.shape[0] // groups
    for half in range(groups // SUBLANES):
        factor, state = [], []
        for n in range(poles):
            factor.append(jnp.exp(-tile(rates, n, half, groups)))
            start = n * groups + half * SUBLANES
            carried = carries[start : start + SUBLANES, :].astype(f32)
            start += poles * groups
            carried = carried + carries[start : start + SUBLANES, :].astype(f32)
            state.append(tile(lead, n, half, groups) * carried)

        def turn(i, state):
            for u in range(8):
                t = i * 8 + u
                parts = [tile(base, t, half, groups) + state[0], state[1]]
                for n in range(2, poles):
                    parts[n % 2] = parts[n % 2] + state[n]
                put(
                    gated, t, half, groups, tile(query, t, half, groups) * (parts[0] + parts[1])
                )
                state = [factor[n] * state[n] for n in range(poles)]
            return tuple(state)

        lax.fori_loop(0, tokens // 8, turn, tuple(state))
    total = jnp.zeros((tokens, LANES), f32)
    for j in range(groups):
        columns = slice(j * LANES, (j + 1) * LANES)
        value = residual[:, columns].astype(f32) + gated[pl.ds(j, tokens, stride=groups), :]
        value = value.astype(bf16)
        summed[:, columns] = value
        value = value.astype(f32)
        total = total + value * value
    squares[...] = jnp.broadcast_to(
        jnp.sum(total.T, axis=0, keepdims=True), squares.shape
    )


def norm_kernel(summed, squares, gain, normed):
    tokens, chans = summed.shape
    mean = jnp.sum(squares[...], axis=0, keepdims=True) / D
    inverse = jnp.broadcast_to(lax.rsqrt(mean + EPSILON), (LANES, tokens)).T
    for j in range(chans // LANES):
        columns = slice(j * LANES, (j + 1) * LANES)
        normed[:, columns] = (
            summed[:, columns].astype(f32) * inverse * gain[j : j + 1, :]
        ).astype(bf16)


def body(
    residual, query_in, key_in, value_in, short_filter, decay_rate, residue, skip_gain, norm_gain
):
    tokens, chans = residual.shape
    poles = decay_rate.shape[0]
    groups = chans // LANES
    count = MINOR * MIDDLE * MAJOR

    def rows(items, kind=f32):
        return jax.ShapeDtypeStruct((items * groups, LANES), kind)

    def hold(items):
        return pltpu.VMEM((items * groups, LANES), f32)

    tail_spec = pl.BlockSpec((16, chans), lambda i: (tokens // 16 - 1, 0))
    tails = call(
        tails_kernel,
        jax.ShapeDtypeStruct((6, chans), bf16),
        "tails",
        grid=(1,),
        in_specs=[tail_spec] * 3,
        out_specs=pl.BlockSpec((6, chans), lambda i: (0, 0)),
    )(query_in, key_in, value_in)
    tails = lax.ppermute(tails, "seq", [(i, i + 1) for i in range(count - 1)])

    mixed, heads, taps, rates, partial = call(
        first_kernel,
        (rows(tokens), rows(4), rows(9), rows(poles), rows(poles)),
        "first",
        scratch=[hold(tokens), hold(tokens)],
    )(key_in, value_in, short_filter, decay_rate)
    state, opening = call(
        functools.partial(state_kernel, float(tokens)),
        (rows(poles, bf16), rows(2)),
        "state",
        scratch=[hold(poles)],
    )(tails, heads, taps, rates, partial)

    place = lax.axis_index("seq").astype(jnp.int32).reshape(1)
    smem = pl.BlockSpec(memory_space=pltpu.SMEM)
    vmem = pl.BlockSpec(memory_space=pltpu.VMEM)
    lines = [[g * MINOR + j for j in range(MINOR)] for g in range(MIDDLE * MAJOR)]
    planes = [
        [(z * MIDDLE + y) * MINOR + j for y in range(MIDDLE)]
        for z in range(MAJOR)
        for j in range(MINOR)
    ]
    pairs = [
        [(z * MIDDLE + y) * MINOR + j for z in range(MAJOR) for j in range(MINOR)]
        for y in range(MIDDLE)
    ]

    def exchange(x, members):
        return lax.all_to_all(x, "seq", 0, 0, axis_index_groups=members, tiled=True)

    arrived = exchange(state, lines)
    base, query, lead = call(
        inner_kernel,
        (rows(tokens), rows(tokens), rows(poles)),
        "inner",
        scratch=[hold(tokens + 4), hold(poles)],
    )(
        query_in,
        tails,
        taps,
        rates,
        residue,
        skip_gain.reshape(groups, LANES),
        mixed,
        opening,
    )
    sums, prefix = call(
        functools.partial(minor_kernel, float(tokens)),
        (rows(poles, bf16), rows(poles)),
        "minor",
        in_specs=[smem, vmem, vmem],
    )(place, arrived, rates)
    arrived = exchange(sums, planes)
    carries = call(
        functools.partial(middle_kernel, float(tokens)),
        rows(MAJOR * poles, bf16),
        "middle",
        in_specs=[smem, vmem, vmem, vmem],
    )(place, arrived, rates, prefix)
    carries = exchange(carries, pairs)
    members = lax.axis_size("chan")
    summed, squares = call(
        outer_kernel,
        (
            jax.ShapeDtypeStruct((tokens, chans), bf16),
            jax.ShapeDtypeStruct((members, tokens), f32),
        ),
        "outer",
        scratch=[hold(tokens)],
    )(carries, rates, lead, base, query, residual)
    squares = lax.all_to_all(squares, "chan", 0, 0, tiled=True)
    normed = call(norm_kernel, jax.ShapeDtypeStruct((tokens, chans), bf16), "norm")(
        summed, squares, norm_gain.reshape(groups, LANES)
    )
    return (summed, normed)


def solution(mesh):
    whole = P("seq", "chan")
    in_specs = (whole, whole, whole, whole, P(None, None, "chan"))
    in_specs += (P(None, "chan"), P(None, "chan"), P("chan"), P("chan"))
    return jax.shard_map(
        body, mesh=mesh, in_specs=in_specs, out_specs=(whole, whole), check_vma=False
    )
```

```python
import functools

import jax
import jax.numpy as jnp
from jax import lax
from jax.experimental import pallas as pl
from jax.experimental.pallas import tpu as pltpu
from jax.sharding import PartitionSpec as P


D = 8192
EPSILON = 1e-06
LANES = 128
SUBLANES = 8
MINOR = 8
MIDDLE = 8
MAJOR = 2
STEP = 6
HALO = 2
RAW = 8

f32 = jnp.float32
bf16 = jnp.bfloat16

POLES = 16


def call(kernel, out_shape, scratch=(), room=50, **extra):
    limit = int((64 - room) * 1024) << 10
    return pl.pallas_call(
        kernel,
        out_shape=out_shape,
        scratch_shapes=scratch,
        compiler_params=pltpu.CompilerParams(vmem_limit_bytes=limit),
        **extra,
    )


def spread(source, target, first, columns, groups):
    items = source.shape[0]
    for g in columns:
        target[pl.ds(first * groups + g, items, stride=groups), :] = source[
            :, g * LANES : (g + 1) * LANES
        ].astype(f32)


def start_of(item, half, groups):
    start = item * groups + half * SUBLANES
    return start if isinstance(start, int) else pl.multiple_of(start, SUBLANES)


def tile(ref, item, half, groups):
    return ref[pl.ds(start_of(item, half, groups), SUBLANES), :]


def put(ref, item, half, groups, value):
    ref[pl.ds(start_of(item, half, groups), SUBLANES), :] = value


def poled(item, half, stride=POLES):
    return pl.ds(half * SUBLANES * stride + item, SUBLANES, stride=stride)


def halves_of(tables):
    rows = tables.shape[0] // 2
    return tables.at[:rows], tables.at[rows:]


def taps_of(taps, which, half):
    return [taps[poled(which * 3 + lag, half), :] for lag in range(3)]


def fir(taps, now, last, older):
    return taps[0] * now + taps[1] * last + taps[2] * older


def first_kernel(
    query_in, key_in, value_in, filters_in, decay_in, parcel, tails, tables,
    key, value, query, filters, decay, keys, values, states, sem,
):
    tokens, chans = key.shape
    groups = chans // LANES
    halves = groups // SUBLANES
    width = SUBLANES * LANES

    def part(source, target, half, slot):
        columns = slice(half * width, (half + 1) * width)
        return pltpu.make_async_copy(source.at[:, columns], target.at[:, columns], sem.at[slot])

    small = [
        pltpu.make_async_copy(decay_in, decay, sem.at[0]),
        pltpu.make_async_copy(filters_in, filters, sem.at[1]),
        pltpu.make_async_copy(query_in.at[tokens - 8 : tokens, :], query, sem.at[2]),
    ]
    large = [
        (part(key_in, key, h, 3 + 2 * h), part(value_in, value, h, 4 + 2 * h))
        for h in range(halves)
    ]
    small[0].start()
    small[1].start()
    for pair in large:
        pair[0].start()
        pair[1].start()
    small[2].start()
    small[0].wait()
    small[1].wait()
    rates, taps = halves_of(tables)
    for g in range(groups):
        columns = slice(g * LANES, (g + 1) * LANES)
        rates[g * POLES : (g + 1) * POLES, :] = decay[:, columns]
        for which in range(3):
            start = g * POLES + 3 * which
            taps[start : start + 3, :] = filters[which, :, columns]
        taps[g * POLES + 9 : (g + 1) * POLES, :] = jnp.zeros((POLES - 9, LANES), f32)
    for half in range(halves):
        factor = [jnp.exp(-rates[poled(n, half), :]) for n in range(POLES)]
        key_taps = taps_of(taps, 1, half)
        value_taps = taps_of(taps, 2, half)
        for copy in large[half]:
            copy.wait()
        columns = range(half * SUBLANES, (half + 1) * SUBLANES)
        spread(key, keys, 0, columns, groups)
        spread(value, values, 0, columns, groups)

        def turn(i, carry):
            k1, k2, v1, v2, *state = carry
            for u in range(STEP):
                t = HALO + i * STEP + u
                k0 = tile(keys, t, half, groups)
                v0 = tile(values, t, half, groups)
                m = fir(key_taps, k0, k1, k2) * fir(value_taps, v0, v1, v2)
                state = [factor[n] * state[n] + m for n in range(POLES)]
                k1, k2, v1, v2 = k0, k1, v0, v1
            return (k1, k2, v1, v2, *state)

        begin = tuple(tile(x, t, half, groups) for x in (keys, values) for t in (1, 0))
        begin += (jnp.zeros((SUBLANES, LANES), f32),) * POLES
        end = lax.fori_loop(0, (tokens - HALO) // STEP, turn, begin)
        for n in range(POLES):
            states[poled(n, half), :] = end[4 + n]
    small[2].wait()
    ends = [(x[:16, :].astype(f32)[:2], x[tokens - 16 :, :].astype(f32)[-2:]) for x in (key, value)]
    raw = jnp.concatenate([*ends[0], *ends[1]], axis=0)
    tails[...] = jnp.concatenate(
        [query[...].astype(f32)[-2:], ends[0][1], ends[1][1]], axis=0
    ).astype(bf16)
    each = groups // MINOR
    rows = each * (POLES + RAW)
    for j in range(MINOR):
        pieces = [raw[:, g * LANES : (g + 1) * LANES] for g in range(each * j, each * (j + 1))]
        parcel[j * rows : j * rows + each * POLES, :] = states[
            each * POLES * j : each * POLES * (j + 1), :
        ].astype(bf16)
        parcel[j * rows + each * POLES : (j + 1) * rows, :] = jnp.concatenate(
            pieces, axis=0
        ).astype(bf16)


def opening_of(tap, head, tail):
    result = [[], []]
    for g in range(head.shape[0] // RAW):
        pair = [[], []]
        for side in range(2):
            weight = [
                tap[g * POLES + 3 + 3 * side + lag : g * POLES + 4 + 3 * side + lag, :]
                for lag in range(3)
            ]
            at = g * RAW + 4 * side
            line = [tail[at + 2 + r : at + 3 + r, :] for r in range(2)]
            line += [head[at + r : at + 1 + r, :] for r in range(2)]
            for t in range(2):
                pair[t].append(fir(weight, line[t + 2], line[t + 1], line[t]))
        for t in range(2):
            m = pair[t][0] * pair[t][1]
            result[t].append(jnp.broadcast_to(m, (POLES, LANES)))
    return [jnp.concatenate(x, axis=0) for x in result]


def piece_of(ref, place, rows):
    return ref[pl.ds(pl.multiple_of((place[0] % MINOR) * rows, SUBLANES), rows), :]


def is_head(shape):
    return (lax.broadcasted_iota(jnp.int32, shape, 0) & 2) == 0


def minor_kernel(block, place, arrived, tables, sums, prefix):
    rates, taps = halves_of(tables)
    size = arrived.shape[0] // MINOR
    rows = rates.shape[0] // MINOR
    rate = piece_of(rates, place, rows)
    tap = piece_of(taps, place, rows)
    decay = jnp.exp(-rate * block)
    late = [jnp.exp(-rate * (block - 1.0)), jnp.exp(-rate * (block - 2.0))]
    total = jnp.zeros((rows, LANES), f32)
    raw = []
    for b in range(MINOR):
        prefix[b * rows : (b + 1) * rows, :] = total
        total = decay * total + arrived[b * size : b * size + rows, :].astype(f32)
        raw.append(arrived[b * size + rows : (b + 1) * size, :].astype(f32))
        if b:
            m = opening_of(tap, raw[b], raw[b - 1])
            total = total + (late[0] * m[0] + late[1] * m[1])
    ends = jnp.where(is_head(raw[0].shape), raw[0], raw[-1]).astype(bf16)
    total = total.astype(bf16)
    for other in range(MIDDLE):
        sums[other * size : other * size + rows, :] = total
        sums[other * size + rows : (other + 1) * size, :] = ends


def middle_kernel(block, place, arrived, tables, prefix, carries):
    rates, taps = halves_of(tables)
    size = arrived.shape[0] // MIDDLE
    rows = rates.shape[0] // MINOR
    rate = piece_of(rates, place, rows)
    tap = piece_of(taps, place, rows)
    mine = (place[0] // MINOR) % MIDDLE
    lower = place[0] < MINOR * MIDDLE
    decay = jnp.exp(-rate * block)
    line_decay = jnp.exp(-rate * (block * MINOR))
    rest_decay = jnp.exp(-rate * (block * (MINOR - 1)))
    late = [jnp.exp(-rate * (block - 1.0)), jnp.exp(-rate * (block - 2.0))]
    before = jnp.zeros((rows, LANES), f32)
    whole = jnp.zeros((rows, LANES), f32)
    own = jnp.zeros((rows, LANES), f32)
    raw = []
    for other in range(MIDDLE):
        raw.append(arrived[other * size + rows : (other + 1) * size, :].astype(f32))
        last = raw[other - 1] if other else jnp.zeros_like(raw[0])
        m = opening_of(tap, raw[other], last)
        opening = late[0] * m[0] + late[1] * m[1]
        if not other:
            opening = jnp.where(lower, opening, 0.0)
        piece = arrived[other * size : other * size + rows, :].astype(f32)
        whole = line_decay * whole + (piece + rest_decay * opening)
        before = jnp.where(other < mine, whole, before)
        own = jnp.where(other == mine, opening, own)
    onward = jnp.exp(-rate * (mine.astype(f32) * (block * MINOR))) * whole
    head = is_head(raw[0].shape)
    ends = jnp.where(
        lower, jnp.where(head, 0.0, raw[-1]), jnp.where(head, raw[0], 0.0)
    )
    half = MINOR * size
    for b in range(MINOR):
        here = before + prefix[b * rows : (b + 1) * rows, :]
        if b:
            here = here + own
            own = decay * own
        send = jnp.where(mine + b > 0, ends, 0.0)
        at = b * size
        carries[at : at + rows, :] = jnp.where(lower, here, 0.0).astype(bf16)
        carries[at + rows : at + size, :] = jnp.zeros((size - rows, LANES), bf16)
        at += half
        carries[at : at + rows, :] = jnp.where(lower, onward, here).astype(bf16)
        carries[at + rows : at + size, :] = send.astype(bf16)
        before = decay * before
        onward = decay * onward


def inner_kernel(
    query_hbm, key_hbm, value_hbm, residual_hbm, residue_hbm, tails, tables, skip,
    base, query, lead, query_in, key_in, value_in, residual, residue,
    queries, keys, values, streams, weights, sem,
):
    tokens, chans = query_in.shape
    groups = chans // LANES
    every = range(groups)
    rates, taps = halves_of(tables)
    sources = (query_hbm, key_hbm, value_hbm, residual_hbm, residue_hbm)
    targets = (query_in, key_in, value_in, residual, residue)
    copies = [
        pltpu.make_async_copy(source, target, sem.at[i])
        for i, (source, target) in enumerate(zip(sources, targets, strict=True))
    ]
    for copy in copies:
        copy.start()
    for copy in copies:
        copy.wait()
    ends = tails[...].astype(f32)
    for which, (source, target) in enumerate(
        ((query_in, queries), (key_in, keys), (value_in, values))
    ):
        spread(ends[2 * which : 2 * which + 2], target, 0, every, groups)
        spread(source, target, HALO, every, groups)
    spread(residual, streams, 0, every, groups)
    for g in every:
        weights[g * POLES : (g + 1) * POLES, :] = residue[:, g * LANES : (g + 1) * LANES]
    for half in range(groups // SUBLANES):
        taps_here = [taps_of(taps, which, half) for which in range(3)]
        sources = (queries, keys, values)

        def filtered(i, carry):
            carry = list(carry)
            for u in range(4):
                t = i * 4 + u
                now = [tile(x, t + HALO, half, groups) for x in sources]
                out = [fir(taps_here[w], now[w], carry[2 * w], carry[2 * w + 1]) for w in range(3)]
                put(query, t, half, groups, out[0])
                put(keys, t, half, groups, out[1] * out[2])
                for w in range(3):
                    carry[2 * w + 1], carry[2 * w] = carry[2 * w], now[w]
            return tuple(carry)

        begin = tuple(tile(x, t, half, groups) for x in sources for t in (1, 0))
        lax.fori_loop(0, tokens // 4, filtered, begin)

        factor, weight = [], []
        for n in range(POLES):
            rate = rates[poled(n, half), :]
            factor.append(jnp.exp(-rate))
            weight.append(weights[poled(n, half), :] * jnp.sqrt(2.0 * rate))
            put(lead, n, half, groups, weight[n] * factor[n])
        direct = tile(skip, 0, half, groups)

        def turn(i, state):
            for u in range(8):
                t = i * 8 + u
                m = tile(keys, t, half, groups)
                state = [factor[n] * state[n] + m for n in range(POLES)]
                parts = [direct * m, weight[0] * state[0]]
                for n in range(1, POLES):
                    parts[n % 2] = parts[n % 2] + weight[n] * state[n]
                gated = tile(query, t, half, groups) * (parts[0] + parts[1])
                put(base, t, half, groups, tile(streams, t, half, groups) + gated)
            return tuple(state)

        lax.fori_loop(0, tokens // 8, turn, (jnp.zeros((SUBLANES, LANES), f32),) * POLES)


def outer_kernel(
    block, place, carries, tables, lead, query_hbm, base_hbm, summed, squares,
    carried, raw, query, gated, sem,
):
    tokens, chans = summed.shape
    groups = chans // LANES
    each = groups // MINOR
    size = each * (POLES + RAW)
    rows = each * POLES
    rates, taps = halves_of(tables)
    parts = sem.shape[0] // 2
    span = tokens // parts
    copies = []
    for p in range(parts):
        part = slice(p * span * groups, (p + 1) * span * groups)
        for i, (source, target) in enumerate(((query_hbm, query), (base_hbm, gated))):
            copies.append(
                pltpu.make_async_copy(source.at[part, :], target.at[part, :], sem.at[2 * p + i])
            )
            copies[-1].start()
    for j in range(MINOR):
        at, more = j * size, (MINOR + j) * size
        both = carries[at : at + size, :].astype(f32) + carries[more : more + size, :].astype(f32)
        carried[j * rows : (j + 1) * rows, :] = both[:rows]
        raw[j * each * RAW : (j + 1) * each * RAW, :] = both[rows:]
    away = (place[0] % (MINOR * MIDDLE)).astype(f32) * block - 2.0
    for half in range(groups // SUBLANES):
        pair = [[], []]
        for side in range(2):
            weight = taps_of(taps, 1 + side, half)
            line = [raw[poled(4 * side + r, half, RAW), :] for r in (2, 3, 0, 1)]
            for t in range(2):
                pair[t].append(fir(weight, line[t + 2], line[t + 1], line[t]))
        opening = [p[0] * p[1] for p in pair]
        factor, state = [], []
        for n in range(POLES):
            rate = rates[poled(n, half), :]
            factor.append(jnp.exp(-rate))
            entering = carried[poled(n, half), :] + jnp.exp(-rate * away) * (
                factor[n] * opening[0] + opening[1]
            )
            state.append(tile(lead, n, half, groups) * entering)

        def turn(i, state):
            for u in range(8):
                t = i * 8 + u
                sums = [state[0], state[1]]
                for n in range(2, POLES):
                    sums[n % 2] = sums[n % 2] + state[n]
                added = tile(query, t, half, groups) * (sums[0] + sums[1])
                put(gated, t, half, groups, tile(gated, t, half, groups) + added)
                state = [factor[n] * state[n] for n in range(POLES)]
            return tuple(state)

        state = tuple(state)
        for p in range(parts):
            if half == 0:
                copies[2 * p].wait()
                copies[2 * p + 1].wait()
            state = lax.fori_loop(p * span // 8, (p + 1) * span // 8, turn, state)
    total = jnp.zeros((tokens, LANES), f32)
    for g in range(groups):
        value = gated[pl.ds(g, tokens, stride=groups), :].astype(bf16)
        summed[:, g * LANES : (g + 1) * LANES] = value
        value = value.astype(f32)
        total = total + value * value
    squares[...] = jnp.broadcast_to(jnp.sum(total.T, axis=0, keepdims=True), squares.shape)


def norm_kernel(summed, squares, gain, stream_out, normed_out, normed, sem):
    tokens, chans = summed.shape
    parts = 4
    width = chans // parts
    stream = pltpu.make_async_copy(summed, stream_out, sem.at[parts])
    stream.start()
    mean = jnp.sum(squares[...], axis=0, keepdims=True) / D
    inverse = jnp.broadcast_to(lax.rsqrt(mean + EPSILON), (LANES, tokens)).T
    copies = []
    for part in range(parts):
        for g in range(part * width // LANES, (part + 1) * width // LANES):
            columns = slice(g * LANES, (g + 1) * LANES)
            normed[:, columns] = (
                summed[:, columns].astype(f32) * inverse * gain[g : g + 1, :]
            ).astype(bf16)
        columns = slice(part * width, (part + 1) * width)
        copies.append(
            pltpu.make_async_copy(normed.at[:, columns], normed_out.at[:, columns], sem.at[part])
        )
        copies[part].start()
    for copy in copies:
        copy.wait()
    stream.wait()


def layer(
    residual, query_in, key_in, value_in, short_filter, decay_rate, residue, skip_gain, norm_gain
):
    tokens, chans = residual.shape
    groups = chans // LANES
    count = MINOR * MIDDLE * MAJOR
    block = float(tokens)

    def shape(rows, kind=f32):
        return jax.ShapeDtypeStruct((rows, LANES), kind)

    def hold(rows):
        return pltpu.VMEM((rows, LANES), f32)

    smem = pl.BlockSpec(memory_space=pltpu.SMEM)
    vmem = pl.BlockSpec(memory_space=pltpu.VMEM)
    hbm = pl.BlockSpec(memory_space=pltpu.HBM)
    wide = pltpu.VMEM((tokens, chans), bf16)
    poled_rows = POLES * groups
    parcel_rows = (POLES + RAW) * groups

    parcel, tails, tables = call(
        first_kernel,
        (
            shape(parcel_rows, bf16),
            jax.ShapeDtypeStruct((6, chans), bf16),
            shape(2 * poled_rows),
        ),
        room=10.25,
        in_specs=[hbm] * 5,
        scratch=[
            wide,
            wide,
            pltpu.VMEM((8, chans), bf16),
            pltpu.VMEM(short_filter.shape, f32),
            pltpu.VMEM(decay_rate.shape, f32),
            hold(tokens * groups),
            hold(tokens * groups),
            hold(poled_rows),
            pltpu.SemaphoreType.DMA((3 + 2 * (groups // SUBLANES),)),
        ],
    )(query_in, key_in, value_in, short_filter, decay_rate)

    place = lax.axis_index("seq").astype(jnp.int32).reshape(1)
    lines = [[g * MINOR + j for j in range(MINOR)] for g in range(MIDDLE * MAJOR)]
    planes = [
        [(z * MIDDLE + y) * MINOR + j for y in range(MIDDLE)]
        for z in range(MAJOR)
        for j in range(MINOR)
    ]
    pairs = [
        [(z * MIDDLE + y) * MINOR + j for z in range(MAJOR) for j in range(MINOR)]
        for y in range(MIDDLE)
    ]

    def exchange(x, members):
        return lax.all_to_all(x, "seq", 0, 0, axis_index_groups=members, tiled=True)

    arrived = exchange(parcel, lines)
    tails = lax.ppermute(tails, "seq", [(i, i + 1) for i in range(count - 1)])
    sums, prefix = call(
        functools.partial(minor_kernel, block),
        (shape(parcel_rows, bf16), shape(poled_rows)),
        in_specs=[smem, vmem, vmem],
    )(place, arrived, tables)
    arrived = exchange(sums, planes)
    carries = call(
        functools.partial(middle_kernel, block),
        shape(MAJOR * parcel_rows, bf16),
        in_specs=[smem, vmem, vmem, vmem],
    )(place, arrived, tables, prefix)
    base, query, lead = call(
        inner_kernel,
        (shape(tokens * groups),) * 2 + (shape(poled_rows),),
        room=11.5,
        in_specs=[hbm] * 5 + [vmem] * 3,
        scratch=[
            wide,
            wide,
            wide,
            wide,
            pltpu.VMEM(residue.shape, f32),
            hold((tokens + HALO) * groups),
            hold((tokens + HALO) * groups),
            hold((tokens + HALO) * groups),
            hold(tokens * groups),
            hold(poled_rows),
            pltpu.SemaphoreType.DMA((5,)),
        ],
    )(
        query_in,
        key_in,
        value_in,
        residual,
        residue,
        tails,
        tables,
        skip_gain.reshape(groups, LANES),
    )
    carries = exchange(carries, pairs)
    members = lax.axis_size("chan")
    summed, squares = call(
        functools.partial(outer_kernel, block),
        (
            jax.ShapeDtypeStruct((tokens, chans), bf16),
            jax.ShapeDtypeStruct((members, tokens), f32),
        ),
        room=11.5,
        in_specs=[smem] + [vmem] * 3 + [hbm] * 2,
        scratch=[
            hold(poled_rows),
            hold(RAW * groups),
            hold(tokens * groups),
            hold(tokens * groups),
            pltpu.SemaphoreType.DMA((8,)),
        ],
    )(place, carries, tables, lead, query, base)
    squares = lax.all_to_all(squares, "chan", 0, 0, tiled=True)
    whole = jax.ShapeDtypeStruct((tokens, chans), bf16)
    return call(
        norm_kernel,
        (whole, whole),
        in_specs=[vmem] * 3,
        out_specs=(hbm, hbm),
        scratch=[wide, pltpu.SemaphoreType.DMA((5,))],
    )(summed, squares, norm_gain.reshape(groups, LANES))


def solution(mesh):
    whole = P("seq", "chan")
    in_specs = (whole, whole, whole, whole, P(None, None, "chan"))
    in_specs += (P(None, "chan"), P(None, "chan"), P("chan"), P("chan"))
    return jax.shard_map(
        layer, mesh=mesh, in_specs=in_specs, out_specs=(whole, whole), check_vma=False
    )
```

```python
import functools

import jax
import jax.numpy as jnp
from jax import lax
from jax.experimental import pallas as pl
from jax.experimental.pallas import tpu as pltpu
from jax.sharding import PartitionSpec as P


D = 8192
EPSILON = 1e-06
LANES = 128
SUBLANES = 8
MINOR = 8
MIDDLE = 8
MAJOR = 2
STEP = 6
HALO = 2
RAW = 8

f32 = jnp.float32
bf16 = jnp.bfloat16

POLES = 16


def call(kernel, out_shape, scratch=(), room=50, **extra):
    limit = int((64 - room) * 1024) << 10
    return pl.pallas_call(
        kernel,
        out_shape=out_shape,
        scratch_shapes=scratch,
        compiler_params=pltpu.CompilerParams(vmem_limit_bytes=limit),
        **extra,
    )


def spread(source, target, first, columns, groups):
    items = source.shape[0]
    for g in columns:
        target[pl.ds(first * groups + g, items, stride=groups), :] = source[
            :, g * LANES : (g + 1) * LANES
        ].astype(f32)


def start_of(item, half, groups):
    start = item * groups + half * SUBLANES
    return start if isinstance(start, int) else pl.multiple_of(start, SUBLANES)


def tile(ref, item, half, groups):
    return ref[pl.ds(start_of(item, half, groups), SUBLANES), :]


def put(ref, item, half, groups, value):
    ref[pl.ds(start_of(item, half, groups), SUBLANES), :] = value


def poled(item, half, stride=POLES):
    return pl.ds(half * SUBLANES * stride + item, SUBLANES, stride=stride)


def halves_of(tables):
    rows = tables.shape[0] // 2
    return tables.at[:rows], tables.at[rows:]


def taps_of(taps, which, half):
    return [taps[poled(which * 3 + lag, half), :] for lag in range(3)]


def fir(taps, now, last, older):
    return taps[0] * now + taps[1] * last + taps[2] * older


def fill_tables(filters, decay, rates, taps):
    groups = decay.shape[1] // LANES
    for g in range(groups):
        columns = slice(g * LANES, (g + 1) * LANES)
        rates[g * POLES : (g + 1) * POLES, :] = decay[:, columns]
        for which in range(3):
            start = g * POLES + 3 * which
            taps[start : start + 3, :] = filters[which, :, columns]
        taps[g * POLES + 9 : (g + 1) * POLES, :] = jnp.zeros((POLES - 9, LANES), f32)


def first_kernel(
    query_in, key_in, value_in, filters_in, decay_in, parcel, tails,
    key, value, query, filters, decay, keys, values, states, rates, taps, sem,
):
    tokens, chans = key.shape
    groups = chans // LANES
    halves = groups // SUBLANES
    width = SUBLANES * LANES

    def part(source, target, half, slot):
        columns = slice(half * width, (half + 1) * width)
        return pltpu.make_async_copy(source.at[:, columns], target.at[:, columns], sem.at[slot])

    small = [
        pltpu.make_async_copy(decay_in, decay, sem.at[0]),
        pltpu.make_async_copy(filters_in, filters, sem.at[1]),
        pltpu.make_async_copy(query_in.at[tokens - 8 : tokens, :], query, sem.at[2]),
    ]
    large = [
        (part(key_in, key, h, 3 + 2 * h), part(value_in, value, h, 4 + 2 * h))
        for h in range(halves)
    ]
    small[0].start()
    small[1].start()
    for pair in large:
        pair[0].start()
        pair[1].start()
    small[2].start()
    small[0].wait()
    small[1].wait()
    fill_tables(filters, decay, rates, taps)
    for half in range(halves):
        factor = [jnp.exp(-rates[poled(n, half), :]) for n in range(POLES)]
        key_taps = taps_of(taps, 1, half)
        value_taps = taps_of(taps, 2, half)
        for copy in large[half]:
            copy.wait()
        columns = range(half * SUBLANES, (half + 1) * SUBLANES)
        spread(key, keys, 0, columns, groups)
        spread(value, values, 0, columns, groups)

        def turn(i, carry):
            k1, k2, v1, v2, *state = carry
            for u in range(STEP):
                t = HALO + i * STEP + u
                k0 = tile(keys, t, half, groups)
                v0 = tile(values, t, half, groups)
                m = fir(key_taps, k0, k1, k2) * fir(value_taps, v0, v1, v2)
                state = [factor[n] * state[n] + m for n in range(POLES)]
                k1, k2, v1, v2 = k0, k1, v0, v1
            return (k1, k2, v1, v2, *state)

        begin = tuple(tile(x, t, half, groups) for x in (keys, values) for t in (1, 0))
        begin += (jnp.zeros((SUBLANES, LANES), f32),) * POLES
        end = lax.fori_loop(0, (tokens - HALO) // STEP, turn, begin)
        for n in range(POLES):
            states[poled(n, half), :] = end[4 + n]
    small[2].wait()
    ends = [(x[:16, :].astype(f32)[:2], x[tokens - 16 :, :].astype(f32)[-2:]) for x in (key, value)]
    raw = jnp.concatenate([*ends[0], *ends[1]], axis=0)
    tails[...] = jnp.concatenate(
        [query[...].astype(f32)[-2:], ends[0][1], ends[1][1]], axis=0
    ).astype(bf16)
    each = groups // MINOR
    rows = each * (POLES + RAW)
    for j in range(MINOR):
        pieces = [raw[:, g * LANES : (g + 1) * LANES] for g in range(each * j, each * (j + 1))]
        parcel[j * rows : j * rows + each * POLES, :] = states[
            each * POLES * j : each * POLES * (j + 1), :
        ].astype(bf16)
        parcel[j * rows + each * POLES : (j + 1) * rows, :] = jnp.concatenate(
            pieces, axis=0
        ).astype(bf16)


def opening_of(tap, head, tail):
    result = [[], []]
    for g in range(head.shape[0] // RAW):
        pair = [[], []]
        for side in range(2):
            weight = [
                tap[g * POLES + 3 + 3 * side + lag : g * POLES + 4 + 3 * side + lag, :]
                for lag in range(3)
            ]
            at = g * RAW + 4 * side
            line = [tail[at + 2 + r : at + 3 + r, :] for r in range(2)]
            line += [head[at + r : at + 1 + r, :] for r in range(2)]
            for t in range(2):
                pair[t].append(fir(weight, line[t + 2], line[t + 1], line[t]))
        for t in range(2):
            m = pair[t][0] * pair[t][1]
            result[t].append(jnp.broadcast_to(m, (POLES, LANES)))
    return [jnp.concatenate(x, axis=0) for x in result]


def piece_of(ref, place, rows):
    return ref[pl.ds(pl.multiple_of((place[0] % MINOR) * rows, SUBLANES), rows), :]


def is_head(shape):
    return (lax.broadcasted_iota(jnp.int32, shape, 0) & 2) == 0


def minor_kernel(block, place, arrived, tables, sums, prefix):
    rates, taps = halves_of(tables)
    size = arrived.shape[0] // MINOR
    rows = rates.shape[0] // MINOR
    rate = piece_of(rates, place, rows)
    tap = piece_of(taps, place, rows)
    decay = jnp.exp(-rate * block)
    late = [jnp.exp(-rate * (block - 1.0)), jnp.exp(-rate * (block - 2.0))]
    total = jnp.zeros((rows, LANES), f32)
    raw = []
    for b in range(MINOR):
        prefix[b * rows : (b + 1) * rows, :] = total
        total = decay * total + arrived[b * size : b * size + rows, :].astype(f32)
        raw.append(arrived[b * size + rows : (b + 1) * size, :].astype(f32))
        if b:
            m = opening_of(tap, raw[b], raw[b - 1])
            total = total + (late[0] * m[0] + late[1] * m[1])
    ends = jnp.where(is_head(raw[0].shape), raw[0], raw[-1]).astype(bf16)
    total = total.astype(bf16)
    for other in range(MIDDLE):
        sums[other * size : other * size + rows, :] = total
        sums[other * size + rows : (other + 1) * size, :] = ends


def middle_kernel(block, place, arrived, tables, prefix, carries):
    rates, taps = halves_of(tables)
    size = arrived.shape[0] // MIDDLE
    rows = rates.shape[0] // MINOR
    rate = piece_of(rates, place, rows)
    tap = piece_of(taps, place, rows)
    mine = (place[0] // MINOR) % MIDDLE
    lower = place[0] < MINOR * MIDDLE
    decay = jnp.exp(-rate * block)
    line_decay = jnp.exp(-rate * (block * MINOR))
    rest_decay = jnp.exp(-rate * (block * (MINOR - 1)))
    late = [jnp.exp(-rate * (block - 1.0)), jnp.exp(-rate * (block - 2.0))]
    before = jnp.zeros((rows, LANES), f32)
    whole = jnp.zeros((rows, LANES), f32)
    own = jnp.zeros((rows, LANES), f32)
    raw = []
    for other in range(MIDDLE):
        raw.append(arrived[other * size + rows : (other + 1) * size, :].astype(f32))
        last = raw[other - 1] if other else jnp.zeros_like(raw[0])
        m = opening_of(tap, raw[other], last)
        opening = late[0] * m[0] + late[1] * m[1]
        if not other:
            opening = jnp.where(lower, opening, 0.0)
        piece = arrived[other * size : other * size + rows, :].astype(f32)
        whole = line_decay * whole + (piece + rest_decay * opening)
        before = jnp.where(other < mine, whole, before)
        own = jnp.where(other == mine, opening, own)
    onward = jnp.exp(-rate * (mine.astype(f32) * (block * MINOR))) * whole
    head = is_head(raw[0].shape)
    ends = jnp.where(
        lower, jnp.where(head, 0.0, raw[-1]), jnp.where(head, raw[0], 0.0)
    )
    half = MINOR * size
    for b in range(MINOR):
        here = before + prefix[b * rows : (b + 1) * rows, :]
        if b:
            here = here + own
            own = decay * own
        send = jnp.where(mine + b > 0, ends, 0.0)
        at = b * size
        carries[at : at + rows, :] = jnp.where(lower, here, 0.0).astype(bf16)
        carries[at + rows : at + size, :] = jnp.zeros((size - rows, LANES), bf16)
        at += half
        carries[at : at + rows, :] = jnp.where(lower, onward, here).astype(bf16)
        carries[at + rows : at + size, :] = send.astype(bf16)
        before = decay * before
        onward = decay * onward


def features_kernel(
    query_hbm, key_hbm, value_hbm, tails, tables, query, mixed,
    query_in, key_in, value_in, queries, keys, values, sem,
):
    tokens, chans = query_in.shape
    groups = chans // LANES
    _, taps = halves_of(tables)
    halves = groups // SUBLANES
    width = SUBLANES * LANES
    lanes = (
        (query_hbm, query_in, queries),
        (key_hbm, key_in, keys),
        (value_hbm, value_in, values),
    )
    copies = []
    for half in range(halves):
        columns = slice(half * width, (half + 1) * width)
        for i, (source, target, _) in enumerate(lanes):
            copies.append(
                pltpu.make_async_copy(
                    source.at[:, columns], target.at[:, columns], sem.at[3 * half + i]
                )
            )
            copies[-1].start()
    ends = tails[...].astype(f32)
    for half in range(halves):
        columns = range(half * SUBLANES, (half + 1) * SUBLANES)
        for i, (_, source, target) in enumerate(lanes):
            spread(ends[2 * i : 2 * i + 2], target, 0, columns, groups)
            copies[3 * half + i].wait()
            spread(source, target, HALO, columns, groups)
        taps_here = [taps_of(taps, which, half) for which in range(3)]
        sources = (queries, keys, values)

        def turn(i, carry):
            carry = list(carry)
            for u in range(4):
                t = i * 4 + u
                now = [tile(x, t + HALO, half, groups) for x in sources]
                out = [fir(taps_here[w], now[w], carry[2 * w], carry[2 * w + 1]) for w in range(3)]
                put(query, t, half, groups, out[0])
                put(mixed, t, half, groups, out[1] * out[2])
                for w in range(3):
                    carry[2 * w + 1], carry[2 * w] = carry[2 * w], now[w]
            return tuple(carry)

        begin = tuple(tile(x, t, half, groups) for x in sources for t in (1, 0))
        lax.fori_loop(0, tokens // 4, turn, begin)


def inner_kernel(
    query_hbm, mixed_hbm, residual_hbm, residue_hbm, tables, skip, base, lead,
    query, mixed, residual, residue, streams, weights, sem,
):
    tokens, chans = residual.shape
    groups = chans // LANES
    rates, _ = halves_of(tables)
    parts = (sem.shape[0] - 2) // 2
    span = tokens // parts
    small = [
        pltpu.make_async_copy(residue_hbm, residue, sem.at[0]),
        pltpu.make_async_copy(residual_hbm, residual, sem.at[1]),
    ]
    for copy in small:
        copy.start()
    copies = []
    for p in range(parts):
        part = slice(p * span * groups, (p + 1) * span * groups)
        for i, (source, target) in enumerate(((query_hbm, query), (mixed_hbm, mixed))):
            copies.append(
                pltpu.make_async_copy(source.at[part, :], target.at[part, :], sem.at[2 + 2 * p + i])
            )
            copies[-1].start()
    for copy in small:
        copy.wait()
    for g in range(groups):
        weights[g * POLES : (g + 1) * POLES, :] = residue[:, g * LANES : (g + 1) * LANES]
    spread(residual, streams, 0, range(groups), groups)
    for half in range(groups // SUBLANES):
        factor, weight = [], []
        for n in range(POLES):
            rate = rates[poled(n, half), :]
            factor.append(jnp.exp(-rate))
            weight.append(weights[poled(n, half), :] * jnp.sqrt(2.0 * rate))
            put(lead, n, half, groups, weight[n] * factor[n])
        direct = tile(skip, 0, half, groups)

        def turn(i, state):
            for u in range(8):
                t = i * 8 + u
                m = tile(mixed, t, half, groups)
                state = [factor[n] * state[n] + m for n in range(POLES)]
                sums = [direct * m, weight[0] * state[0]]
                for n in range(1, POLES):
                    sums[n % 2] = sums[n % 2] + weight[n] * state[n]
                gated = tile(query, t, half, groups) * (sums[0] + sums[1])
                put(base, t, half, groups, tile(streams, t, half, groups) + gated)
            return tuple(state)

        state = (jnp.zeros((SUBLANES, LANES), f32),) * POLES
        for p in range(parts):
            if half == 0:
                copies[2 * p].wait()
                copies[2 * p + 1].wait()
            state = lax.fori_loop(p * span // 8, (p + 1) * span // 8, turn, state)


def tables_kernel(filters, decay, tables):
    rates, taps = halves_of(tables)
    fill_tables(filters, decay, rates, taps)


def outer_kernel(
    block, place, carries, tables, lead, query_hbm, base_hbm, summed, squares,
    carried, raw, query, gated, sem,
):
    tokens, chans = summed.shape
    groups = chans // LANES
    each = groups // MINOR
    size = each * (POLES + RAW)
    rows = each * POLES
    rates, taps = halves_of(tables)
    parts = sem.shape[0] // 2
    span = tokens // parts
    copies = []
    for p in range(parts):
        part = slice(p * span * groups, (p + 1) * span * groups)
        for i, (source, target) in enumerate(((query_hbm, query), (base_hbm, gated))):
            copies.append(
                pltpu.make_async_copy(source.at[part, :], target.at[part, :], sem.at[2 * p + i])
            )
            copies[-1].start()
    for j in range(MINOR):
        at, more = j * size, (MINOR + j) * size
        both = carries[at : at + size, :].astype(f32) + carries[more : more + size, :].astype(f32)
        carried[j * rows : (j + 1) * rows, :] = both[:rows]
        raw[j * each * RAW : (j + 1) * each * RAW, :] = both[rows:]
    away = (place[0] % (MINOR * MIDDLE)).astype(f32) * block - 2.0
    for half in range(groups // SUBLANES):
        pair = [[], []]
        for side in range(2):
            weight = taps_of(taps, 1 + side, half)
            line = [raw[poled(4 * side + r, half, RAW), :] for r in (2, 3, 0, 1)]
            for t in range(2):
                pair[t].append(fir(weight, line[t + 2], line[t + 1], line[t]))
        opening = [p[0] * p[1] for p in pair]
        factor, state = [], []
        for n in range(POLES):
            rate = rates[poled(n, half), :]
            factor.append(jnp.exp(-rate))
            entering = carried[poled(n, half), :] + jnp.exp(-rate * away) * (
                factor[n] * opening[0] + opening[1]
            )
            state.append(tile(lead, n, half, groups) * entering)

        def turn(i, state):
            for u in range(8):
                t = i * 8 + u
                sums = [state[0], state[1]]
                for n in range(2, POLES):
                    sums[n % 2] = sums[n % 2] + state[n]
                added = tile(query, t, half, groups) * (sums[0] + sums[1])
                put(gated, t, half, groups, tile(gated, t, half, groups) + added)
                state = [factor[n] * state[n] for n in range(POLES)]
            return tuple(state)

        state = tuple(state)
        for p in range(parts):
            if half == 0:
                copies[2 * p].wait()
                copies[2 * p + 1].wait()
            state = lax.fori_loop(p * span // 8, (p + 1) * span // 8, turn, state)
    total = jnp.zeros((tokens, LANES), f32)
    for g in range(groups):
        value = gated[pl.ds(g, tokens, stride=groups), :].astype(bf16)
        summed[:, g * LANES : (g + 1) * LANES] = value
        value = value.astype(f32)
        total = total + value * value
    squares[...] = jnp.broadcast_to(jnp.sum(total.T, axis=0, keepdims=True), squares.shape)


def norm_kernel(summed, squares, gain, stream_out, normed_out, normed, sem):
    tokens, chans = summed.shape
    parts = 4
    width = chans // parts
    stream = pltpu.make_async_copy(summed, stream_out, sem.at[parts])
    stream.start()
    mean = jnp.sum(squares[...], axis=0, keepdims=True) / D
    inverse = jnp.broadcast_to(lax.rsqrt(mean + EPSILON), (LANES, tokens)).T
    copies = []
    for part in range(parts):
        for g in range(part * width // LANES, (part + 1) * width // LANES):
            columns = slice(g * LANES, (g + 1) * LANES)
            normed[:, columns] = (
                summed[:, columns].astype(f32) * inverse * gain[g : g + 1, :]
            ).astype(bf16)
        columns = slice(part * width, (part + 1) * width)
        copies.append(
            pltpu.make_async_copy(normed.at[:, columns], normed_out.at[:, columns], sem.at[part])
        )
        copies[part].start()
    for copy in copies:
        copy.wait()
    stream.wait()


def layer(
    residual, query_in, key_in, value_in, short_filter, decay_rate, residue, skip_gain, norm_gain
):
    tokens, chans = residual.shape
    groups = chans // LANES
    count = MINOR * MIDDLE * MAJOR
    block = float(tokens)

    def shape(rows, kind=f32):
        return jax.ShapeDtypeStruct((rows, LANES), kind)

    def hold(rows):
        return pltpu.VMEM((rows, LANES), f32)

    smem = pl.BlockSpec(memory_space=pltpu.SMEM)
    vmem = pl.BlockSpec(memory_space=pltpu.VMEM)
    hbm = pl.BlockSpec(memory_space=pltpu.HBM)
    wide = pltpu.VMEM((tokens, chans), bf16)
    poled_rows = POLES * groups
    parcel_rows = (POLES + RAW) * groups

    parcel, tails = call(
        first_kernel,
        (
            shape(parcel_rows, bf16),
            jax.ShapeDtypeStruct((6, chans), bf16),
        ),
        room=10.25,
        in_specs=[hbm] * 5,
        scratch=[
            wide,
            wide,
            pltpu.VMEM((8, chans), bf16),
            pltpu.VMEM(short_filter.shape, f32),
            pltpu.VMEM(decay_rate.shape, f32),
            hold(tokens * groups),
            hold(tokens * groups),
            hold(poled_rows),
            hold(poled_rows),
            hold(poled_rows),
            pltpu.SemaphoreType.DMA((3 + 2 * (groups // SUBLANES),)),
        ],
    )(query_in, key_in, value_in, short_filter, decay_rate)

    place = lax.axis_index("seq").astype(jnp.int32).reshape(1)
    lines = [[g * MINOR + j for j in range(MINOR)] for g in range(MIDDLE * MAJOR)]
    planes = [
        [(z * MIDDLE + y) * MINOR + j for y in range(MIDDLE)]
        for z in range(MAJOR)
        for j in range(MINOR)
    ]
    pairs = [
        [(z * MIDDLE + y) * MINOR + j for z in range(MAJOR) for j in range(MINOR)]
        for y in range(MIDDLE)
    ]

    def exchange(x, members):
        return lax.all_to_all(x, "seq", 0, 0, axis_index_groups=members, tiled=True)

    arrived = exchange(parcel, lines)
    tails = lax.ppermute(tails, "seq", [(i, i + 1) for i in range(count - 1)])
    tables = call(tables_kernel, shape(2 * poled_rows))(short_filter, decay_rate)
    sums, prefix = call(
        functools.partial(minor_kernel, block),
        (shape(parcel_rows, bf16), shape(poled_rows)),
        in_specs=[smem, vmem, vmem],
    )(place, arrived, tables)
    arrived = exchange(sums, planes)
    query, mixed = call(
        features_kernel,
        (shape(tokens * groups),) * 2,
        room=11.5,
        in_specs=[hbm] * 3 + [vmem] * 2,
        scratch=[
            wide,
            wide,
            wide,
            hold((tokens + HALO) * groups),
            hold((tokens + HALO) * groups),
            hold((tokens + HALO) * groups),
            pltpu.SemaphoreType.DMA((3 * (groups // SUBLANES),)),
        ],
    )(query_in, key_in, value_in, tails, tables)
    carries = call(
        functools.partial(middle_kernel, block),
        shape(MAJOR * parcel_rows, bf16),
        in_specs=[smem, vmem, vmem, vmem],
    )(place, arrived, tables, prefix)
    base, lead = call(
        inner_kernel,
        (shape(tokens * groups), shape(poled_rows)),
        room=11.5,
        in_specs=[hbm] * 4 + [vmem] * 2,
        scratch=[
            hold(tokens * groups),
            hold(tokens * groups),
            wide,
            pltpu.VMEM(residue.shape, f32),
            hold(tokens * groups),
            hold(poled_rows),
            pltpu.SemaphoreType.DMA((10,)),
        ],
    )(query, mixed, residual, residue, tables, skip_gain.reshape(groups, LANES))
    carries = exchange(carries, pairs)
    members = lax.axis_size("chan")
    summed, squares = call(
        functools.partial(outer_kernel, block),
        (
            jax.ShapeDtypeStruct((tokens, chans), bf16),
            jax.ShapeDtypeStruct((members, tokens), f32),
        ),
        room=11.5,
        in_specs=[smem] + [vmem] * 3 + [hbm] * 2,
        scratch=[
            hold(poled_rows),
            hold(RAW * groups),
            hold(tokens * groups),
            hold(tokens * groups),
            pltpu.SemaphoreType.DMA((8,)),
        ],
    )(place, carries, tables, lead, query, base)
    squares = lax.all_to_all(squares, "chan", 0, 0, tiled=True)
    whole = jax.ShapeDtypeStruct((tokens, chans), bf16)
    return call(
        norm_kernel,
        (whole, whole),
        in_specs=[vmem] * 3,
        out_specs=(hbm, hbm),
        scratch=[wide, pltpu.SemaphoreType.DMA((5,))],
    )(summed, squares, norm_gain.reshape(groups, LANES))


def solution(mesh):
    whole = P("seq", "chan")
    in_specs = (whole, whole, whole, whole, P(None, None, "chan"))
    in_specs += (P(None, "chan"), P(None, "chan"), P("chan"), P("chan"))
    return jax.shard_map(
        layer, mesh=mesh, in_specs=in_specs, out_specs=(whole, whole), check_vma=False
    )
```

```python
import functools

import jax
import jax.numpy as jnp
from jax import lax
from jax.experimental import pallas as pl
from jax.experimental.pallas import tpu as pltpu
from jax.sharding import PartitionSpec as P


D = 8192
EPSILON = 1e-06
LANES = 128
SUBLANES = 8
MINOR = 8
MIDDLE = 8
MAJOR = 2
STEP = 6
HALO = 2
RAW = 8

f32 = jnp.float32
bf16 = jnp.bfloat16

POLES = 16


def call(kernel, out_shape, scratch=(), room=50, **extra):
    limit = int((64 - room) * 1024) << 10
    return pl.pallas_call(
        kernel,
        out_shape=out_shape,
        scratch_shapes=scratch,
        compiler_params=pltpu.CompilerParams(vmem_limit_bytes=limit),
        **extra,
    )


def spread(source, target, first, columns, groups):
    items = source.shape[0]
    for g in columns:
        target[pl.ds(first * groups + g, items, stride=groups), :] = source[
            :, g * LANES : (g + 1) * LANES
        ].astype(f32)


def start_of(item, half, groups):
    start = item * groups + half * SUBLANES
    return start if isinstance(start, int) else pl.multiple_of(start, SUBLANES)


def tile(ref, item, half, groups):
    return ref[pl.ds(start_of(item, half, groups), SUBLANES), :]


def put(ref, item, half, groups, value):
    ref[pl.ds(start_of(item, half, groups), SUBLANES), :] = value


def poled(item, half, stride=POLES):
    return pl.ds(half * SUBLANES * stride + item, SUBLANES, stride=stride)


def halves_of(tables):
    rows = tables.shape[0] // 2
    return tables.at[:rows], tables.at[rows:]


def taps_of(taps, which, half):
    return [taps[poled(which * 3 + lag, half), :] for lag in range(3)]


def fir(taps, now, last, older):
    return taps[0] * now + taps[1] * last + taps[2] * older


def fill_tables(filters, decay, rates, taps):
    groups = decay.shape[1] // LANES
    for g in range(groups):
        columns = slice(g * LANES, (g + 1) * LANES)
        rates[g * POLES : (g + 1) * POLES, :] = decay[:, columns]
        for which in range(3):
            start = g * POLES + 3 * which
            taps[start : start + 3, :] = filters[which, :, columns]
        taps[g * POLES + 9 : (g + 1) * POLES, :] = jnp.zeros((POLES - 9, LANES), f32)


def first_kernel(
    query_in, key_in, value_in, filters_in, decay_in, parcel, tails,
    key, value, query, filters, decay, keys, values, states, rates, taps, sem,
):
    tokens, chans = key.shape
    groups = chans // LANES
    halves = groups // SUBLANES
    width = SUBLANES * LANES

    def part(source, target, half, slot):
        columns = slice(half * width, (half + 1) * width)
        return pltpu.make_async_copy(source.at[:, columns], target.at[:, columns], sem.at[slot])

    small = [
        pltpu.make_async_copy(decay_in, decay, sem.at[0]),
        pltpu.make_async_copy(filters_in, filters, sem.at[1]),
        pltpu.make_async_copy(query_in.at[tokens - 8 : tokens, :], query, sem.at[2]),
    ]
    large = [
        (part(key_in, key, h, 3 + 2 * h), part(value_in, value, h, 4 + 2 * h))
        for h in range(halves)
    ]
    small[0].start()
    small[1].start()
    for pair in large:
        pair[0].start()
        pair[1].start()
    small[2].start()
    small[0].wait()
    small[1].wait()
    fill_tables(filters, decay, rates, taps)
    for half in range(halves):
        factor = [jnp.exp(-rates[poled(n, half), :]) for n in range(POLES)]
        key_taps = taps_of(taps, 1, half)
        value_taps = taps_of(taps, 2, half)
        for copy in large[half]:
            copy.wait()
        columns = range(half * SUBLANES, (half + 1) * SUBLANES)
        spread(key, keys, 0, columns, groups)
        spread(value, values, 0, columns, groups)

        def turn(i, carry):
            k1, k2, v1, v2, *state = carry
            for u in range(STEP):
                t = HALO + i * STEP + u
                k0 = tile(keys, t, half, groups)
                v0 = tile(values, t, half, groups)
                m = fir(key_taps, k0, k1, k2) * fir(value_taps, v0, v1, v2)
                state = [factor[n] * state[n] + m for n in range(POLES)]
                k1, k2, v1, v2 = k0, k1, v0, v1
            return (k1, k2, v1, v2, *state)

        begin = tuple(tile(x, t, half, groups) for x in (keys, values) for t in (1, 0))
        begin += (jnp.zeros((SUBLANES, LANES), f32),) * POLES
        end = lax.fori_loop(0, (tokens - HALO) // STEP, turn, begin)
        for n in range(POLES):
            states[poled(n, half), :] = end[4 + n]
    small[2].wait()
    ends = [(x[:16, :].astype(f32)[:2], x[tokens - 16 :, :].astype(f32)[-2:]) for x in (key, value)]
    raw = jnp.concatenate([*ends[0], *ends[1]], axis=0)
    tails[...] = jnp.concatenate(
        [query[...].astype(f32)[-2:], ends[0][1], ends[1][1]], axis=0
    ).astype(bf16)
    each = groups // MINOR
    rows = each * (POLES + RAW)
    for j in range(MINOR):
        pieces = [raw[:, g * LANES : (g + 1) * LANES] for g in range(each * j, each * (j + 1))]
        parcel[j * rows : j * rows + each * POLES, :] = states[
            each * POLES * j : each * POLES * (j + 1), :
        ].astype(bf16)
        parcel[j * rows + each * POLES : (j + 1) * rows, :] = jnp.concatenate(
            pieces, axis=0
        ).astype(bf16)


def opening_of(tap, head, tail):
    result = [[], []]
    for g in range(head.shape[0] // RAW):
        pair = [[], []]
        for side in range(2):
            weight = [
                tap[g * POLES + 3 + 3 * side + lag : g * POLES + 4 + 3 * side + lag, :]
                for lag in range(3)
            ]
            at = g * RAW + 4 * side
            line = [tail[at + 2 + r : at + 3 + r, :] for r in range(2)]
            line += [head[at + r : at + 1 + r, :] for r in range(2)]
            for t in range(2):
                pair[t].append(fir(weight, line[t + 2], line[t + 1], line[t]))
        for t in range(2):
            m = pair[t][0] * pair[t][1]
            result[t].append(jnp.broadcast_to(m, (POLES, LANES)))
    return [jnp.concatenate(x, axis=0) for x in result]


def piece_of(place, filters, decay):
    chans = decay.shape[1] // MINOR
    start = pl.multiple_of((place[0] % MINOR) * chans, LANES)
    rates = decay[:, pl.ds(start, chans)]
    taps = jnp.concatenate([filters[which, :, pl.ds(start, chans)] for which in range(3)], axis=0)
    taps = jnp.concatenate([taps, jnp.zeros((POLES - 9, chans), f32)], axis=0)
    return [
        jnp.concatenate([x[:, g : g + LANES] for g in range(0, chans, LANES)], axis=0)
        for x in (rates, taps)
    ]


def is_head(shape):
    return (lax.broadcasted_iota(jnp.int32, shape, 0) & 2) == 0


def minor_kernel(block, place, arrived, filters, decay_rate, sums, prefix):
    rate, tap = piece_of(place, filters, decay_rate)
    size = arrived.shape[0] // MINOR
    rows = rate.shape[0]
    decay = jnp.exp(-rate * block)
    late = [jnp.exp(-rate * (block - 1.0)), jnp.exp(-rate * (block - 2.0))]
    total = jnp.zeros((rows, LANES), f32)
    raw = []
    for b in range(MINOR):
        prefix[b * rows : (b + 1) * rows, :] = total
        total = decay * total + arrived[b * size : b * size + rows, :].astype(f32)
        raw.append(arrived[b * size + rows : (b + 1) * size, :].astype(f32))
        if b:
            m = opening_of(tap, raw[b], raw[b - 1])
            total = total + (late[0] * m[0] + late[1] * m[1])
    ends = jnp.where(is_head(raw[0].shape), raw[0], raw[-1]).astype(bf16)
    total = total.astype(bf16)
    for other in range(MIDDLE):
        sums[other * size : other * size + rows, :] = total
        sums[other * size + rows : (other + 1) * size, :] = ends


def lines_of(block, rate, tap, arrived, state, tail):
    size = arrived.shape[0] // MIDDLE
    rows = rate.shape[0]
    line_decay = jnp.exp(-rate * (block * MINOR))
    rest_decay = jnp.exp(-rate * (block * (MINOR - 1)))
    late = [jnp.exp(-rate * (block - 1.0)), jnp.exp(-rate * (block - 2.0))]
    entering, openings = [], []
    for line in range(MIDDLE):
        raw = arrived[line * size + rows : (line + 1) * size, :].astype(f32)
        m = opening_of(tap, raw, tail)
        openings.append(late[0] * m[0] + late[1] * m[1])
        entering.append(state)
        piece = arrived[line * size : line * size + rows, :].astype(f32)
        state = line_decay * state + (piece + rest_decay * openings[-1])
        tail = raw
    return entering, openings, state, tail


def ahead_kernel(block, place, arrived, filters, decay_rate, ahead):
    rate, tap = piece_of(place, filters, decay_rate)
    rows = rate.shape[0]
    begin = jnp.zeros((rows, LANES), f32), jnp.zeros((ahead.shape[0] - rows, LANES), f32)
    _, _, state, tail = lines_of(block, rate, tap, arrived, *begin)
    ahead[:rows, :] = state.astype(bf16)
    ahead[rows:, :] = tail.astype(bf16)


def middle_kernel(block, place, arrived, ahead, prefix, filters, decay_rate, carries):
    rate, tap = piece_of(place, filters, decay_rate)
    rows = rate.shape[0]
    mine = (place[0] // MINOR) % MIDDLE
    begin = ahead[:rows, :].astype(f32), ahead[rows:, :].astype(f32)
    entering, openings, _, _ = lines_of(block, rate, tap, arrived, *begin)
    before, own = entering[0], openings[0]
    for line in range(1, MIDDLE):
        before = jnp.where(mine == line, entering[line], before)
        own = jnp.where(mine == line, openings[line], own)
    decay = jnp.exp(-rate * block)
    for b in range(MINOR):
        here = before + prefix[b * rows : (b + 1) * rows, :]
        if b:
            here = here + own
            own = decay * own
        carries[b * rows : (b + 1) * rows, :] = here.astype(bf16)
        before = decay * before


def features_kernel(
    query_hbm, key_hbm, value_hbm, filters, decay, query, mixed, tables,
    query_in, key_in, value_in, queries, keys, values, sem,
):
    tokens, chans = query_in.shape
    groups = chans // LANES
    rates, taps = halves_of(tables)
    halves = groups // SUBLANES
    width = SUBLANES * LANES
    lanes = (
        (query_hbm, query_in, queries),
        (key_hbm, key_in, keys),
        (value_hbm, value_in, values),
    )
    copies = []
    for half in range(halves):
        columns = slice(half * width, (half + 1) * width)
        for i, (source, target, _) in enumerate(lanes):
            copies.append(
                pltpu.make_async_copy(
                    source.at[:, columns], target.at[:, columns], sem.at[3 * half + i]
                )
            )
            copies[-1].start()
    fill_tables(filters, decay, rates, taps)
    for half in range(halves):
        columns = range(half * SUBLANES, (half + 1) * SUBLANES)
        for i, (_, source, target) in enumerate(lanes):
            copies[3 * half + i].wait()
            spread(source, target, 0, columns, groups)
        taps_here = [taps_of(taps, which, half) for which in range(3)]
        sources = (queries, keys, values)

        def turn(i, carry):
            carry = list(carry)
            for u in range(4):
                t = i * 4 + u
                now = [tile(x, t, half, groups) for x in sources]
                out = [fir(taps_here[w], now[w], carry[2 * w], carry[2 * w + 1]) for w in range(3)]
                put(query, t, half, groups, out[0])
                put(mixed, t, half, groups, out[1] * out[2])
                for w in range(3):
                    carry[2 * w + 1], carry[2 * w] = carry[2 * w], now[w]
            return tuple(carry)

        begin = (jnp.zeros((SUBLANES, LANES), f32),) * 6
        lax.fori_loop(0, tokens // 4, turn, begin)


def inner_kernel(
    query_hbm, mixed_hbm, residual_hbm, residue_hbm, query_in, key_in, value_in, tails, tables, skip,
    base, lead, opening, query, mixed, residual, residue, heads, edges, streams, weights, sem,
):
    tokens, chans = residual.shape
    groups = chans // LANES
    rates, taps = halves_of(tables)
    parts = (sem.shape[0] - 5) // 2
    span = tokens // parts
    small = [
        pltpu.make_async_copy(residue_hbm, residue, sem.at[0]),
        pltpu.make_async_copy(residual_hbm, residual, sem.at[1]),
    ]
    first_rows = heads.shape[0] // 3
    for i, source in enumerate((query_in, key_in, value_in)):
        small.append(
            pltpu.make_async_copy(
                source.at[:first_rows, :],
                heads.at[first_rows * i : first_rows * (i + 1), :],
                sem.at[2 + i],
            )
        )
    for copy in small:
        copy.start()
    copies = []
    for p in range(parts):
        part = slice(p * span * groups, (p + 1) * span * groups)
        for i, (source, target) in enumerate(((query_hbm, query), (mixed_hbm, mixed))):
            copies.append(
                pltpu.make_async_copy(source.at[part, :], target.at[part, :], sem.at[5 + 2 * p + i])
            )
            copies[-1].start()
    for copy in small:
        copy.wait()
    for g in range(groups):
        weights[g * POLES : (g + 1) * POLES, :] = residue[:, g * LANES : (g + 1) * LANES]
    spread(residual, streams, 0, range(groups), groups)
    ends = tails[...].astype(f32)
    begins = heads[...].astype(f32)
    for i in range(3):
        spread(ends[2 * i : 2 * i + 2], edges, 4 * i, range(groups), groups)
        spread(begins[first_rows * i : first_rows * i + 2], edges, 4 * i + 2, range(groups), groups)
    for half in range(groups // SUBLANES):
        factor, weight = [], []
        for n in range(POLES):
            rate = rates[poled(n, half), :]
            factor.append(jnp.exp(-rate))
            weight.append(weights[poled(n, half), :] * jnp.sqrt(2.0 * rate))
            put(lead, n, half, groups, weight[n] * factor[n])
        direct = tile(skip, 0, half, groups)

        def turn(i, state):
            for u in range(8):
                t = i * 8 + u
                m = tile(mixed, t, half, groups)
                state = [factor[n] * state[n] + m for n in range(POLES)]
                sums = [direct * m, weight[0] * state[0]]
                for n in range(1, POLES):
                    sums[n % 2] = sums[n % 2] + weight[n] * state[n]
                gated = tile(query, t, half, groups) * (sums[0] + sums[1])
                put(base, t, half, groups, tile(streams, t, half, groups) + gated)
            return tuple(state)

        state = (jnp.zeros((SUBLANES, LANES), f32),) * POLES
        for p in range(parts):
            if half == 0:
                copies[2 * p].wait()
                copies[2 * p + 1].wait()
            if p == 0:
                for t in range(HALO):
                    out = []
                    for i in range(3):
                        now = [tile(edges, 4 * i + 2 + t - lag, half, groups) for lag in range(3)]
                        out.append(fir(taps_of(taps, i, half), *now))
                    put(query, t, half, groups, out[0])
                    put(opening, t, half, groups, out[0])
                    put(mixed, t, half, groups, out[1] * out[2])
            state = lax.fori_loop(p * span // 8, (p + 1) * span // 8, turn, state)


def outer_kernel(
    carries, tables, lead, opening, query_hbm, base_hbm, summed, squares,
    carried, query, gated, sem,
):
    tokens, chans = summed.shape
    groups = chans // LANES
    rates, _ = halves_of(tables)
    parts = sem.shape[0] // 2
    span = tokens // parts
    copies = []
    for p in range(parts):
        part = slice(p * span * groups, (p + 1) * span * groups)
        for i, (source, target) in enumerate(((query_hbm, query), (base_hbm, gated))):
            copies.append(
                pltpu.make_async_copy(source.at[part, :], target.at[part, :], sem.at[2 * p + i])
            )
            copies[-1].start()
    carried[...] = carries[...].astype(f32)
    for half in range(groups // SUBLANES):
        factor, state = [], []
        for n in range(POLES):
            factor.append(jnp.exp(-rates[poled(n, half), :]))
            entering = carried[poled(n, half), :]
            state.append(tile(lead, n, half, groups) * entering)

        def turn(i, state):
            for u in range(8):
                t = i * 8 + u
                sums = [state[0], state[1]]
                for n in range(2, POLES):
                    sums[n % 2] = sums[n % 2] + state[n]
                added = tile(query, t, half, groups) * (sums[0] + sums[1])
                put(gated, t, half, groups, tile(gated, t, half, groups) + added)
                state = [factor[n] * state[n] for n in range(POLES)]
            return tuple(state)

        state = tuple(state)
        for p in range(parts):
            if half == 0:
                copies[2 * p].wait()
                copies[2 * p + 1].wait()
            if p == 0:
                for t in range(HALO):
                    put(query, t, half, groups, tile(opening, t, half, groups))
            state = lax.fori_loop(p * span // 8, (p + 1) * span // 8, turn, state)
    total = jnp.zeros((tokens, LANES), f32)
    for g in range(groups):
        value = gated[pl.ds(g, tokens, stride=groups), :].astype(bf16)
        summed[:, g * LANES : (g + 1) * LANES] = value
        value = value.astype(f32)
        total = total + value * value
    squares[...] = jnp.broadcast_to(jnp.sum(total.T, axis=0, keepdims=True), squares.shape)


def norm_kernel(summed, squares, gain, stream_out, normed_out, normed, sem):
    tokens, chans = summed.shape
    parts = 4
    width = chans // parts
    stream = pltpu.make_async_copy(summed, stream_out, sem.at[parts])
    stream.start()
    mean = jnp.sum(squares[...], axis=0, keepdims=True) / D
    inverse = jnp.broadcast_to(lax.rsqrt(mean + EPSILON), (LANES, tokens)).T
    copies = []
    for part in range(parts):
        for g in range(part * width // LANES, (part + 1) * width // LANES):
            columns = slice(g * LANES, (g + 1) * LANES)
            normed[:, columns] = (
                summed[:, columns].astype(f32) * inverse * gain[g : g + 1, :]
            ).astype(bf16)
        columns = slice(part * width, (part + 1) * width)
        copies.append(
            pltpu.make_async_copy(normed.at[:, columns], normed_out.at[:, columns], sem.at[part])
        )
        copies[part].start()
    for copy in copies:
        copy.wait()
    stream.wait()


def layer(
    residual, query_in, key_in, value_in, short_filter, decay_rate, residue, skip_gain, norm_gain
):
    tokens, chans = residual.shape
    groups = chans // LANES
    count = MINOR * MIDDLE * MAJOR
    block = float(tokens)

    def shape(rows, kind=f32):
        return jax.ShapeDtypeStruct((rows, LANES), kind)

    def hold(rows):
        return pltpu.VMEM((rows, LANES), f32)

    smem = pl.BlockSpec(memory_space=pltpu.SMEM)
    vmem = pl.BlockSpec(memory_space=pltpu.VMEM)
    hbm = pl.BlockSpec(memory_space=pltpu.HBM)
    wide = pltpu.VMEM((tokens, chans), bf16)
    poled_rows = POLES * groups
    parcel_rows = (POLES + RAW) * groups

    parcel, tails = call(
        first_kernel,
        (
            shape(parcel_rows, bf16),
            jax.ShapeDtypeStruct((6, chans), bf16),
        ),
        room=10.25,
        in_specs=[hbm] * 5,
        scratch=[
            wide,
            wide,
            pltpu.VMEM((8, chans), bf16),
            pltpu.VMEM(short_filter.shape, f32),
            pltpu.VMEM(decay_rate.shape, f32),
            hold(tokens * groups),
            hold(tokens * groups),
            hold(poled_rows),
            hold(poled_rows),
            hold(poled_rows),
            pltpu.SemaphoreType.DMA((3 + 2 * (groups // SUBLANES),)),
        ],
    )(query_in, key_in, value_in, short_filter, decay_rate)

    place = lax.axis_index("seq").astype(jnp.int32).reshape(1)
    lines = [[g * MINOR + j for j in range(MINOR)] for g in range(MIDDLE * MAJOR)]
    planes = [
        [(z * MIDDLE + y) * MINOR + j for y in range(MIDDLE)]
        for z in range(MAJOR)
        for j in range(MINOR)
    ]

    def exchange(x, members):
        return lax.all_to_all(x, "seq", 0, 0, axis_index_groups=members, tiled=True)

    tables_in = (short_filter, decay_rate)
    parcel, place = lax.optimization_barrier((parcel, place))
    arrived = exchange(parcel, lines)
    sums, prefix = call(
        functools.partial(minor_kernel, block),
        (shape(parcel_rows, bf16), shape(poled_rows)),
        in_specs=[smem, vmem, vmem, vmem],
    )(place, arrived, *tables_in)
    arrived = exchange(sums, planes)
    tails = lax.ppermute(tails, "seq", [(i, i + 1) for i in range(count - 1)])
    query, mixed, tables = call(
        features_kernel,
        (shape(tokens * groups),) * 2 + (shape(2 * poled_rows),),
        room=11.5,
        in_specs=[hbm] * 3 + [vmem] * 2,
        scratch=[
            wide,
            wide,
            wide,
            hold(tokens * groups),
            hold(tokens * groups),
            hold(tokens * groups),
            pltpu.SemaphoreType.DMA((3 * (groups // SUBLANES),)),
        ],
    )(query_in, key_in, value_in, *tables_in)
    ahead = call(
        functools.partial(ahead_kernel, block),
        shape(parcel_rows // MINOR, bf16),
        in_specs=[smem, vmem, vmem, vmem],
    )(place, arrived, *tables_in)
    ahead = lax.ppermute(ahead, "seq", [(i, i + count // 2) for i in range(count // 2)])
    base, lead, opening = call(
        inner_kernel,
        (shape(tokens * groups), shape(poled_rows), shape(HALO * groups)),
        room=11.5,
        in_specs=[hbm] * 7 + [vmem] * 3,
        scratch=[
            hold(tokens * groups),
            hold(tokens * groups),
            wide,
            pltpu.VMEM(residue.shape, f32),
            pltpu.VMEM((48, chans), bf16),
            hold(12 * groups),
            hold(tokens * groups),
            hold(poled_rows),
            pltpu.SemaphoreType.DMA((13,)),
        ],
    )(
        query,
        mixed,
        residual,
        residue,
        query_in,
        key_in,
        value_in,
        tails,
        tables,
        skip_gain.reshape(groups, LANES),
    )
    carries = call(
        functools.partial(middle_kernel, block),
        shape(poled_rows, bf16),
        in_specs=[smem] + [vmem] * 5,
    )(place, arrived, ahead, prefix, *tables_in)
    carries = exchange(carries, lines)
    members = lax.axis_size("chan")
    summed, squares = call(
        outer_kernel,
        (
            jax.ShapeDtypeStruct((tokens, chans), bf16),
            jax.ShapeDtypeStruct((members, tokens), f32),
        ),
        room=11.5,
        in_specs=[vmem] * 4 + [hbm] * 2,
        scratch=[
            hold(poled_rows),
            hold(tokens * groups),
            hold(tokens * groups),
            pltpu.SemaphoreType.DMA((8,)),
        ],
    )(carries, tables, lead, opening, query, base)
    squares = lax.all_to_all(squares, "chan", 0, 0, tiled=True)
    whole = jax.ShapeDtypeStruct((tokens, chans), bf16)
    return call(
        norm_kernel,
        (whole, whole),
        in_specs=[vmem] * 3,
        out_specs=(hbm, hbm),
        scratch=[wide, pltpu.SemaphoreType.DMA((5,))],
    )(summed, squares, norm_gain.reshape(groups, LANES))


def solution(mesh):
    whole = P("seq", "chan")
    in_specs = (whole, whole, whole, whole, P(None, None, "chan"))
    in_specs += (P(None, "chan"), P(None, "chan"), P("chan"), P("chan"))
    return jax.shard_map(
        layer, mesh=mesh, in_specs=in_specs, out_specs=(whole, whole), check_vma=False
    )
```

```python
import functools

import jax
import jax.numpy as jnp
from jax import lax
from jax.experimental import pallas as pl
from jax.experimental.pallas import tpu as pltpu
from jax.sharding import PartitionSpec as P


D = 8192
EPSILON = 1e-06
LANES = 128
SUBLANES = 8
MINOR = 8
MIDDLE = 8
MAJOR = 2
STEP = 6
HALO = 2
RAW = 8
EXTRA = 8

f32 = jnp.float32
bf16 = jnp.bfloat16

POLES = 16


def call(kernel, out_shape, scratch=(), room=50, **extra):
    limit = int((64 - room) * 1024) << 10
    return pl.pallas_call(
        kernel,
        out_shape=out_shape,
        scratch_shapes=scratch,
        compiler_params=pltpu.CompilerParams(vmem_limit_bytes=limit),
        **extra,
    )


def spread(source, target, first, columns, groups):
    items = source.shape[0]
    for g in columns:
        target[pl.ds(first * groups + g, items, stride=groups), :] = source[
            :, g * LANES : (g + 1) * LANES
        ].astype(f32)


def start_of(item, half, groups):
    start = item * groups + half * SUBLANES
    return start if isinstance(start, int) else pl.multiple_of(start, SUBLANES)


def tile(ref, item, half, groups):
    return ref[pl.ds(start_of(item, half, groups), SUBLANES), :]


def put(ref, item, half, groups, value):
    ref[pl.ds(start_of(item, half, groups), SUBLANES), :] = value


def poled(item, half, stride=POLES):
    return pl.ds(half * SUBLANES * stride + item, SUBLANES, stride=stride)


def taps_of(taps, which, half):
    return [taps[poled(which * 3 + lag, half), :] for lag in range(3)]


def fir(taps, now, last, older):
    return taps[0] * now + taps[1] * last + taps[2] * older


def fill_tables(filters, decay, rates, taps):
    groups = decay.shape[1] // LANES
    for g in range(groups):
        columns = slice(g * LANES, (g + 1) * LANES)
        rates[g * POLES : (g + 1) * POLES, :] = decay[:, columns]
        for which in range(3):
            start = g * POLES + 3 * which
            taps[start : start + 3, :] = filters[which, :, columns]
        taps[g * POLES + 9 : (g + 1) * POLES, :] = jnp.zeros((POLES - 9, LANES), f32)


def first_kernel(
    query_in, key_in, value_in, filters_in, decay_in, parcel,
    key, value, query, filters, decay, keys, values, states, rates, taps, sem,
):
    tokens, chans = key.shape
    groups = chans // LANES
    halves = groups // SUBLANES
    width = SUBLANES * LANES

    def part(source, target, half, slot):
        columns = slice(half * width, (half + 1) * width)
        return pltpu.make_async_copy(source.at[:, columns], target.at[:, columns], sem.at[slot])

    small = [
        pltpu.make_async_copy(decay_in, decay, sem.at[0]),
        pltpu.make_async_copy(filters_in, filters, sem.at[1]),
        pltpu.make_async_copy(query_in.at[tokens - 8 : tokens, :], query, sem.at[2]),
    ]
    large = [
        (part(key_in, key, h, 3 + 2 * h), part(value_in, value, h, 4 + 2 * h))
        for h in range(halves)
    ]
    small[0].start()
    small[1].start()
    for pair in large:
        pair[0].start()
        pair[1].start()
    small[2].start()
    small[0].wait()
    small[1].wait()
    fill_tables(filters, decay, rates, taps)
    for half in range(halves):
        factor = [jnp.exp(-rates[poled(n, half), :]) for n in range(POLES)]
        key_taps = taps_of(taps, 1, half)
        value_taps = taps_of(taps, 2, half)
        for copy in large[half]:
            copy.wait()
        columns = range(half * SUBLANES, (half + 1) * SUBLANES)
        spread(key, keys, 0, columns, groups)
        spread(value, values, 0, columns, groups)

        def turn(i, carry):
            k1, k2, v1, v2, *state = carry
            for u in range(STEP):
                t = HALO + i * STEP + u
                k0 = tile(keys, t, half, groups)
                v0 = tile(values, t, half, groups)
                m = fir(key_taps, k0, k1, k2) * fir(value_taps, v0, v1, v2)
                state = [factor[n] * state[n] + m for n in range(POLES)]
                k1, k2, v1, v2 = k0, k1, v0, v1
            return (k1, k2, v1, v2, *state)

        begin = tuple(tile(x, t, half, groups) for x in (keys, values) for t in (1, 0))
        begin += (jnp.zeros((SUBLANES, LANES), f32),) * POLES
        end = lax.fori_loop(0, (tokens - HALO) // STEP, turn, begin)
        for n in range(POLES):
            states[poled(n, half), :] = end[4 + n]
    small[2].wait()
    ends = [(x[:16, :].astype(f32)[:2], x[tokens - 16 :, :].astype(f32)[-2:]) for x in (key, value)]
    raw = jnp.concatenate([*ends[0], *ends[1]], axis=0)
    last = query[...].astype(f32)[-2:]
    each = groups // MINOR
    rows = each * POLES
    size = rows + each * RAW + EXTRA
    for j in range(MINOR):
        lanes = [slice(g * LANES, (g + 1) * LANES) for g in range(each * j, each * (j + 1))]
        parcel[j * size : j * size + rows, :] = states[rows * j : rows * (j + 1), :].astype(bf16)
        pieces = [raw[:, x] for x in lanes] + [last[:, x] for x in lanes]
        pieces.append(jnp.zeros((EXTRA - 2 * each, LANES), f32))
        parcel[j * size + rows : (j + 1) * size, :] = jnp.concatenate(pieces, axis=0).astype(bf16)


def opening_of(tap, head, tail):
    result = [[], []]
    for g in range(head.shape[0] // RAW):
        pair = [[], []]
        for side in range(2):
            weight = [
                tap[g * POLES + 3 + 3 * side + lag : g * POLES + 4 + 3 * side + lag, :]
                for lag in range(3)
            ]
            at = g * RAW + 4 * side
            line = [tail[at + 2 + r : at + 3 + r, :] for r in range(2)]
            line += [head[at + r : at + 1 + r, :] for r in range(2)]
            for t in range(2):
                pair[t].append(fir(weight, line[t + 2], line[t + 1], line[t]))
        for t in range(2):
            m = pair[t][0] * pair[t][1]
            result[t].append(jnp.broadcast_to(m, (POLES, LANES)))
    return [jnp.concatenate(x, axis=0) for x in result]


def piece_of(place, filters, decay):
    chans = decay.shape[1] // MINOR
    start = pl.multiple_of((place[0] % MINOR) * chans, LANES)
    rates = decay[:, pl.ds(start, chans)]
    taps = jnp.concatenate([filters[which, :, pl.ds(start, chans)] for which in range(3)], axis=0)
    taps = jnp.concatenate([taps, jnp.zeros((POLES - 9, chans), f32)], axis=0)
    return [
        jnp.concatenate([x[:, g : g + LANES] for g in range(0, chans, LANES)], axis=0)
        for x in (rates, taps)
    ]


def is_head(shape):
    return (lax.broadcasted_iota(jnp.int32, shape, 0) & 2) == 0


def not_extra(shape):
    return lax.broadcasted_iota(jnp.int32, shape, 0) < shape[0] - EXTRA


def minor_kernel(block, place, arrived, filters, decay_rate, sums, prefix):
    rate, tap = piece_of(place, filters, decay_rate)
    size = arrived.shape[0] // MINOR
    rows = rate.shape[0]
    decay = jnp.exp(-rate * block)
    late = [jnp.exp(-rate * (block - 1.0)), jnp.exp(-rate * (block - 2.0))]
    total = jnp.zeros((rows, LANES), f32)
    raw = []
    for b in range(MINOR):
        prefix[b * rows : (b + 1) * rows, :] = total
        total = decay * total + arrived[b * size : b * size + rows, :].astype(f32)
        raw.append(arrived[b * size + rows : (b + 1) * size, :].astype(f32))
        if b:
            m = opening_of(tap, raw[b][:-EXTRA], raw[b - 1])
            total = total + (late[0] * m[0] + late[1] * m[1])
    head = is_head(raw[0].shape) & not_extra(raw[0].shape)
    ends = jnp.where(head, raw[0], raw[-1]).astype(bf16)
    total = total.astype(bf16)
    for other in range(MIDDLE):
        sums[other * size : other * size + rows, :] = total
        sums[other * size + rows : (other + 1) * size, :] = ends


def lines_of(block, rate, tap, arrived, state, tail):
    size = arrived.shape[0] // MIDDLE
    rows = rate.shape[0]
    line_decay = jnp.exp(-rate * (block * MINOR))
    rest_decay = jnp.exp(-rate * (block * (MINOR - 1)))
    late = [jnp.exp(-rate * (block - 1.0)), jnp.exp(-rate * (block - 2.0))]
    entering, openings, tails = [], [], []
    for line in range(MIDDLE):
        raw = arrived[line * size + rows : (line + 1) * size, :].astype(f32)
        m = opening_of(tap, raw[:-EXTRA], tail)
        tails.append(tail)
        openings.append(late[0] * m[0] + late[1] * m[1])
        entering.append(state)
        piece = arrived[line * size : line * size + rows, :].astype(f32)
        state = line_decay * state + (piece + rest_decay * openings[-1])
        tail = raw
    return entering, openings, tails, state, tail


def ahead_kernel(block, place, arrived, filters, decay_rate, ahead):
    rate, tap = piece_of(place, filters, decay_rate)
    rows = rate.shape[0]
    begin = jnp.zeros((rows, LANES), f32), jnp.zeros((ahead.shape[0] - rows, LANES), f32)
    *_, state, tail = lines_of(block, rate, tap, arrived, *begin)
    ahead[:rows, :] = state.astype(bf16)
    ahead[rows:, :] = tail.astype(bf16)


def tail_rows(raw):
    at = raw.shape[0] - EXTRA
    rows = []
    for g in range(at // RAW):
        rows += [raw[g * RAW + 2 : g * RAW + 4], raw[g * RAW + 6 : g * RAW + 8]]
        rows += [raw[at + 2 * g : at + 2 * g + 2], jnp.zeros((2, LANES), f32)]
    return jnp.concatenate(rows, axis=0)


def middle_kernel(block, place, line, arrived, ahead, prefix, filters, decay_rate, carries):
    rate, tap = piece_of(place, filters, decay_rate)
    rows = rate.shape[0]
    mine = (place[0] // MINOR) % MIDDLE
    begin = ahead[:rows, :].astype(f32), ahead[rows:, :].astype(f32)
    entering, openings, tails, *_ = lines_of(block, rate, tap, arrived, *begin)
    before, own, tail = entering[0], openings[0], tails[0]
    for other in range(1, MIDDLE):
        before = jnp.where(mine == other, entering[other], before)
        own = jnp.where(mine == other, openings[other], own)
        tail = jnp.where(mine == other, tails[other], tail)
    decay = jnp.exp(-rate * block)
    size = line.shape[0] // MINOR
    out = carries.shape[0] // MINOR
    for b in range(MINOR):
        here = before + prefix[b * rows : (b + 1) * rows, :]
        if b:
            here = here + own
            own = decay * own
            tail = line[(b - 1) * size + rows : b * size, :].astype(f32)
        carries[b * out : b * out + rows, :] = here.astype(bf16)
        carries[b * out + rows : (b + 1) * out, :] = tail_rows(tail).astype(bf16)
        before = decay * before


def inner_kernel(
    upper, place, query_hbm, key_hbm, value_hbm, residual_hbm, residue_hbm, filters, decay, skip,
    base_hbm, feature_hbm, lead, heads,
    query_in, key_in, value_in, residual, residue, queries, keys, values, streams, feature,
    weights, rates, taps, sem, out_sem,
):
    tokens, chans = query_in.shape
    groups = chans // LANES
    halves = groups // SUBLANES
    width = SUBLANES * LANES
    lanes = (
        (query_hbm, query_in, queries),
        (key_hbm, key_in, keys),
        (value_hbm, value_in, values),
        (residual_hbm, residual, streams),
    )
    parts = out_sem.shape[0] // 2
    span = tokens * groups // parts

    @pl.when((place[0] >= MINOR * MIDDLE) == upper)
    def _():
        small = pltpu.make_async_copy(residue_hbm, residue, sem.at[0])
        small.start()
        copies = []
        for half in range(halves):
            columns = slice(half * width, (half + 1) * width)
            for i, (source, target, _) in enumerate(lanes):
                copies.append(
                    pltpu.make_async_copy(
                        source.at[:, columns], target.at[:, columns], sem.at[1 + 4 * half + i]
                    )
                )
                copies[-1].start()
        fill_tables(filters, decay, rates, taps)
        small.wait()
        for g in range(groups):
            weights[g * POLES : (g + 1) * POLES, :] = residue[:, g * LANES : (g + 1) * LANES]
        outward = []
        for half in range(halves):
            for i, (_, source, target) in enumerate(lanes):
                copies[4 * half + i].wait()
                columns = range(half * SUBLANES, (half + 1) * SUBLANES)
                spread(source, target, 0, columns, groups)
            for i in range(3):
                for t in range(HALO):
                    put(heads, HALO * i + t, half, groups, tile(lanes[i][2], t, half, groups))
            taps_here = [taps_of(taps, which, half) for which in range(3)]

            def filtered(i, carry):
                carry = list(carry)
                for u in range(STEP):
                    t = HALO + i * STEP + u
                    now = [tile(lanes[w][2], t, half, groups) for w in range(3)]
                    out = [
                        fir(taps_here[w], now[w], carry[2 * w], carry[2 * w + 1]) for w in range(3)
                    ]
                    put(feature, t, half, groups, out[0])
                    put(keys, t, half, groups, out[1] * out[2])
                    for w in range(3):
                        carry[2 * w + 1], carry[2 * w] = carry[2 * w], now[w]
                return tuple(carry)

            begin = tuple(tile(lanes[w][2], t, half, groups) for w in range(3) for t in (1, 0))
            lax.fori_loop(0, (tokens - HALO) // STEP, filtered, begin)
            for t in range(HALO):
                put(feature, t, half, groups, jnp.zeros((SUBLANES, LANES), f32))

            factor, weight = [], []
            for n in range(POLES):
                rate = rates[poled(n, half), :]
                factor.append(jnp.exp(-rate))
                weight.append(weights[poled(n, half), :] * jnp.sqrt(2.0 * rate))
                put(lead, n, half, groups, weight[n])
            direct = tile(skip, 0, half, groups)

            def turn(i, state):
                for u in range(STEP):
                    t = HALO + i * STEP + u
                    m = tile(keys, t, half, groups)
                    state = [factor[n] * state[n] + m for n in range(POLES)]
                    sums = [direct * m, weight[0] * state[0]]
                    for n in range(1, POLES):
                        sums[n % 2] = sums[n % 2] + weight[n] * state[n]
                    gated = tile(feature, t, half, groups) * (sums[0] + sums[1])
                    put(streams, t, half, groups, tile(streams, t, half, groups) + gated)
                return tuple(state)

            state = (jnp.zeros((SUBLANES, LANES), f32),) * POLES
            turns = (tokens - HALO) // STEP
            done = 0
            for p in range(parts):
                last = min(turns, -((HALO - (p + 1) * tokens // parts) // STEP))
                state = lax.fori_loop(done, last, turn, state)
                done = last
                if half == halves - 1:
                    rows = slice(span * p, span * (p + 1))
                    for i, (source, target) in enumerate(
                        ((streams, base_hbm), (feature, feature_hbm))
                    ):
                        outward.append(
                            pltpu.make_async_copy(
                                source.at[rows, :], target.at[rows, :], out_sem.at[2 * p + i]
                            )
                        )
                        outward[-1].start()
        for copy in outward:
            copy.wait()


def outer_kernel(
    place, carries, filters, decay, skip, lead_low, heads_low, lead_high, heads_high,
    base_low, feature_low, base_high, feature_high, summed, squares,
    carried, before, rates, taps, query, gated, sem,
):
    tokens, chans = summed.shape
    groups = chans // LANES
    lower = place[0] < MINOR * MIDDLE
    parts = sem.shape[0] // 2
    span = tokens // parts

    def copies_from(feature, base):
        copies = []
        for p in range(parts):
            part = slice(p * span * groups, (p + 1) * span * groups)
            for i, (source, target) in enumerate(((feature, query), (base, gated))):
                copies.append(
                    pltpu.make_async_copy(
                        source.at[part, :], target.at[part, :], sem.at[2 * p + i]
                    )
                )
        return copies

    copies = copies_from(feature_low, base_low)

    @pl.when(lower)
    def _():
        for copy in copies:
            copy.start()

    @pl.when(jnp.logical_not(lower))
    def _():
        for copy in copies_from(feature_high, base_high):
            copy.start()

    fill_tables(filters, decay, rates, taps)
    size = carries.shape[0] // MINOR
    rows = groups // MINOR * POLES
    for j in range(MINOR):
        piece = carries[j * size : (j + 1) * size, :].astype(f32)
        carried[j * rows : (j + 1) * rows, :] = piece[:rows]
        before[j * (size - rows) : (j + 1) * (size - rows), :] = piece[rows:]

    def chosen(low, high, item, half):
        return jnp.where(lower, tile(low, item, half, groups), tile(high, item, half, groups))

    for half in range(groups // SUBLANES):
        opening = []
        for i, at in enumerate((4, 0, 2)):
            line = [before[poled(at + r, half, RAW), :] for r in range(2)]
            line += [chosen(heads_low, heads_high, HALO * i + r, half) for r in range(2)]
            weight = taps_of(taps, i, half)
            opening.append([fir(weight, line[t + 2], line[t + 1], line[t]) for t in range(2)])
        mixed = [opening[1][t] * opening[2][t] for t in range(2)]
        factor, state, weight = [], [], []
        for n in range(POLES):
            factor.append(jnp.exp(-rates[poled(n, half), :]))
            weight.append(chosen(lead_low, lead_high, n, half))
            state.append(weight[n] * (factor[n] * carried[poled(n, half), :] + mixed[0]))
        direct = tile(skip, 0, half, groups)

        def total_of(state, first):
            sums = [state[0] if first is None else first + state[0], state[1]]
            for n in range(2, POLES):
                sums[n % 2] = sums[n % 2] + state[n]
            return sums[0] + sums[1]

        start = []
        for t in range(HALO):
            if t:
                state = [factor[n] * state[n] + weight[n] * mixed[t] for n in range(POLES)]
            start.append(opening[0][t] * total_of(state, direct * mixed[t]))
        state = tuple(factor[n] * state[n] for n in range(POLES))

        def turn(i, state):
            for u in range(STEP):
                t = HALO + i * STEP + u
                added = tile(query, t, half, groups) * total_of(state, None)
                put(gated, t, half, groups, tile(gated, t, half, groups) + added)
                state = tuple(factor[n] * state[n] for n in range(POLES))
            return state

        turns = (tokens - HALO) // STEP
        done = 0
        for p in range(parts):
            if half == 0:
                copies[2 * p].wait()
                copies[2 * p + 1].wait()
            if p == 0:
                for t in range(HALO):
                    put(gated, t, half, groups, tile(gated, t, half, groups) + start[t])
            last = turns if p == parts - 1 else ((p + 1) * span - HALO) // STEP
            state = lax.fori_loop(done, last, turn, state)
            done = last
    total = jnp.zeros((tokens, LANES), f32)
    for g in range(groups):
        value = gated[pl.ds(g, tokens, stride=groups), :].astype(bf16)
        summed[:, g * LANES : (g + 1) * LANES] = value
        value = value.astype(f32)
        total = total + value * value
    squares[...] = jnp.broadcast_to(jnp.sum(total.T, axis=0, keepdims=True), squares.shape)


def norm_kernel(summed, squares, gain, stream_out, normed_out, normed, sem):
    tokens, chans = summed.shape
    parts = 4
    width = chans // parts
    stream = pltpu.make_async_copy(summed, stream_out, sem.at[parts])
    stream.start()
    mean = jnp.sum(squares[...], axis=0, keepdims=True) / D
    inverse = jnp.broadcast_to(lax.rsqrt(mean + EPSILON), (LANES, tokens)).T
    copies = []
    for part in range(parts):
        for g in range(part * width // LANES, (part + 1) * width // LANES):
            columns = slice(g * LANES, (g + 1) * LANES)
            normed[:, columns] = (
                summed[:, columns].astype(f32) * inverse * gain[g : g + 1, :]
            ).astype(bf16)
        columns = slice(part * width, (part + 1) * width)
        copies.append(
            pltpu.make_async_copy(normed.at[:, columns], normed_out.at[:, columns], sem.at[part])
        )
        copies[part].start()
    for copy in copies:
        copy.wait()
    stream.wait()


def layer(
    residual, query_in, key_in, value_in, short_filter, decay_rate, residue, skip_gain, norm_gain
):
    tokens, chans = residual.shape
    groups = chans // LANES
    count = MINOR * MIDDLE * MAJOR
    block = float(tokens)

    def shape(rows, kind=f32):
        return jax.ShapeDtypeStruct((rows, LANES), kind)

    def hold(rows):
        return pltpu.VMEM((rows, LANES), f32)

    smem = pl.BlockSpec(memory_space=pltpu.SMEM)
    vmem = pl.BlockSpec(memory_space=pltpu.VMEM)
    hbm = pl.BlockSpec(memory_space=pltpu.HBM)
    wide = pltpu.VMEM((tokens, chans), bf16)
    poled_rows = POLES * groups
    parcel_rows = (POLES + RAW) * groups + EXTRA * MINOR

    parcel = call(
        first_kernel,
        shape(parcel_rows, bf16),
        room=10.1,
        in_specs=[hbm] * 5,
        scratch=[
            wide,
            wide,
            pltpu.VMEM((8, chans), bf16),
            pltpu.VMEM(short_filter.shape, f32),
            pltpu.VMEM(decay_rate.shape, f32),
            hold(tokens * groups),
            hold(tokens * groups),
            hold(poled_rows),
            hold(poled_rows),
            hold(poled_rows),
            pltpu.SemaphoreType.DMA((3 + 2 * (groups // SUBLANES),)),
        ],
    )(query_in, key_in, value_in, short_filter, decay_rate)

    place = lax.axis_index("seq").astype(jnp.int32).reshape(1)
    lines = [[g * MINOR + j for j in range(MINOR)] for g in range(MIDDLE * MAJOR)]
    planes = [
        [(z * MIDDLE + y) * MINOR + j for y in range(MIDDLE)]
        for z in range(MAJOR)
        for j in range(MINOR)
    ]

    def exchange(x, members):
        return lax.all_to_all(x, "seq", 0, 0, axis_index_groups=members, tiled=True)

    tables_in = (short_filter, decay_rate)
    parcel, place = lax.optimization_barrier((parcel, place))
    arrived = exchange(parcel, lines)
    sums, prefix = call(
        functools.partial(minor_kernel, block),
        (shape(parcel_rows, bf16), shape(poled_rows)),
        in_specs=[smem, vmem, vmem, vmem],
    )(place, arrived, *tables_in)
    line = arrived
    arrived = exchange(sums, planes)
    ahead = call(
        functools.partial(ahead_kernel, block),
        shape(parcel_rows // MINOR, bf16),
        in_specs=[smem, vmem, vmem, vmem],
    )(place, arrived, *tables_in)
    skip = skip_gain.reshape(groups, LANES)

    def inner(upper, place):
        return call(
            functools.partial(inner_kernel, upper),
            (
                shape(tokens * groups),
                shape(tokens * groups),
                shape(poled_rows),
                shape(3 * HALO * groups),
            ),
            room=11.5,
            in_specs=[smem] + [hbm] * 5 + [vmem] * 3,
            out_specs=(hbm, hbm, vmem, vmem),
            scratch=[wide] * 4
            + [pltpu.VMEM(residue.shape, f32)]
            + [hold(tokens * groups)] * 5
            + [hold(poled_rows)] * 3
            + [pltpu.SemaphoreType.DMA((1 + 4 * (groups // SUBLANES),))]
            + [pltpu.SemaphoreType.DMA((8,))],
        )(place, query_in, key_in, value_in, residual, residue, *tables_in, skip)

    place, ahead = lax.optimization_barrier((place, ahead))
    low = inner(False, place)
    *low, ahead = lax.optimization_barrier((*low, ahead))
    ahead = lax.ppermute(ahead, "seq", [(i, i + count // 2) for i in range(count // 2)])
    high = inner(True, place)
    carries = call(
        functools.partial(middle_kernel, block),
        shape(poled_rows + RAW * groups, bf16),
        in_specs=[smem] + [vmem] * 6,
    )(place, line, arrived, ahead, prefix, *tables_in)
    carries = exchange(carries, lines)
    members = lax.axis_size("chan")
    summed, squares = call(
        outer_kernel,
        (
            jax.ShapeDtypeStruct((tokens, chans), bf16),
            jax.ShapeDtypeStruct((members, tokens), f32),
        ),
        room=11.5,
        in_specs=[smem] + [vmem] * 8 + [hbm] * 4,
        scratch=[
            hold(poled_rows),
            hold(RAW * groups),
            hold(poled_rows),
            hold(poled_rows),
            hold(tokens * groups),
            hold(tokens * groups),
            pltpu.SemaphoreType.DMA((8,)),
        ],
    )(
        place,
        carries,
        *tables_in,
        skip,
        low[2],
        low[3],
        high[2],
        high[3],
        low[0],
        low[1],
        high[0],
        high[1],
    )
    squares = lax.all_to_all(squares, "chan", 0, 0, tiled=True)
    whole = jax.ShapeDtypeStruct((tokens, chans), bf16)
    return call(
        norm_kernel,
        (whole, whole),
        in_specs=[vmem] * 3,
        out_specs=(hbm, hbm),
        scratch=[wide, pltpu.SemaphoreType.DMA((5,))],
    )(summed, squares, norm_gain.reshape(groups, LANES))


def solution(mesh):
    whole = P("seq", "chan")
    in_specs = (whole, whole, whole, whole, P(None, None, "chan"))
    in_specs += (P(None, "chan"), P(None, "chan"), P("chan"), P("chan"))
    return jax.shard_map(
        layer, mesh=mesh, in_specs=in_specs, out_specs=(whole, whole), check_vma=False
    )
```

```python
import functools

import jax
import jax.numpy as jnp
from jax import lax
from jax.experimental import pallas as pl
from jax.experimental.pallas import tpu as pltpu
from jax.sharding import PartitionSpec as P


D = 8192
EPSILON = 1e-06
LANES = 128
SUBLANES = 8
MINOR = 8
MIDDLE = 8
MAJOR = 2
STEP = 9
LONG_STEP = 18
HALO = 2
RAW = 8
EXTRA = 8

f32 = jnp.float32
bf16 = jnp.bfloat16

POLES = 16


def call(kernel, out_shape, scratch=(), room=50, **extra):
    limit = int((64 - room) * 1024) << 10
    return pl.pallas_call(
        kernel,
        out_shape=out_shape,
        scratch_shapes=scratch,
        compiler_params=pltpu.CompilerParams(vmem_limit_bytes=limit),
        **extra,
    )


def spread(source, target, first, columns, groups):
    items = source.shape[0]
    every = target.shape[0] // groups
    for g in columns:
        start = (g // SUBLANES * every + first) * SUBLANES + g % SUBLANES
        target[pl.ds(start, items, stride=SUBLANES), :] = source[
            :, g * LANES : (g + 1) * LANES
        ].astype(f32)


def at_tile(ref, item, half, groups):
    start = (half * (ref.shape[0] // groups) + item) * SUBLANES
    return pl.ds(start if isinstance(start, int) else pl.multiple_of(start, SUBLANES), SUBLANES)


def tile(ref, item, half, groups):
    return ref[at_tile(ref, item, half, groups), :]


def put(ref, item, half, groups, value):
    ref[at_tile(ref, item, half, groups), :] = value


def poled(item, half, stride=POLES):
    return pl.ds(half * SUBLANES * stride + item, SUBLANES, stride=stride)


def taps_of(taps, which, half):
    return [taps[poled(which * 3 + lag, half), :] for lag in range(3)]


def fir(taps, now, last, older):
    return taps[0] * now + taps[1] * last + taps[2] * older


def fill_tables(filters, decay, rates, taps):
    groups = decay.shape[1] // LANES
    for g in range(groups):
        columns = slice(g * LANES, (g + 1) * LANES)
        rates[g * POLES : (g + 1) * POLES, :] = decay[:, columns]
        for which in range(3):
            start = g * POLES + 3 * which
            taps[start : start + 3, :] = filters[which, :, columns]
        taps[g * POLES + 9 : (g + 1) * POLES, :] = jnp.zeros((POLES - 9, LANES), f32)


def first_kernel(
    query_in, key_in, value_in, filters_in, decay_in, parcel,
    key, value, query, filters, decay, keys, values, states, rates, taps, sem,
):
    tokens, chans = key.shape
    groups = chans // LANES
    halves = groups // SUBLANES
    width = SUBLANES * LANES

    def part(source, target, half, slot):
        columns = slice(half * width, (half + 1) * width)
        return pltpu.make_async_copy(source.at[:, columns], target.at[:, columns], sem.at[slot])

    small = [
        pltpu.make_async_copy(decay_in, decay, sem.at[0]),
        pltpu.make_async_copy(filters_in, filters, sem.at[1]),
        pltpu.make_async_copy(query_in.at[tokens - 8 : tokens, :], query, sem.at[2]),
    ]
    large = [
        (part(key_in, key, h, 3 + 2 * h), part(value_in, value, h, 4 + 2 * h))
        for h in range(halves)
    ]
    small[0].start()
    small[1].start()
    for pair in large:
        pair[0].start()
        pair[1].start()
    small[2].start()
    small[0].wait()
    small[1].wait()
    fill_tables(filters, decay, rates, taps)
    for half in range(halves):
        factor = [jnp.exp(-rates[poled(n, half), :]) for n in range(POLES)]
        key_taps = taps_of(taps, 1, half)
        value_taps = taps_of(taps, 2, half)
        for copy in large[half]:
            copy.wait()
        columns = range(half * SUBLANES, (half + 1) * SUBLANES)
        spread(key, keys, 0, columns, groups)
        spread(value, values, 0, columns, groups)

        def turn(i, carry):
            k1, k2, v1, v2, *state = carry
            for u in range(LONG_STEP):
                t = HALO + i * LONG_STEP + u
                k0 = tile(keys, t, half, groups)
                v0 = tile(values, t, half, groups)
                m = fir(key_taps, k0, k1, k2) * fir(value_taps, v0, v1, v2)
                state = [factor[n] * state[n] + m for n in range(POLES)]
                k1, k2, v1, v2 = k0, k1, v0, v1
            return (k1, k2, v1, v2, *state)

        begin = tuple(tile(x, t, half, groups) for x in (keys, values) for t in (1, 0))
        begin += (jnp.zeros((SUBLANES, LANES), f32),) * POLES
        end = lax.fori_loop(0, (tokens - HALO) // LONG_STEP, turn, begin)
        for n in range(POLES):
            states[poled(n, half), :] = end[4 + n]
    small[2].wait()
    ends = [(x[:16, :].astype(f32)[:2], x[tokens - 16 :, :].astype(f32)[-2:]) for x in (key, value)]
    raw = jnp.concatenate([*ends[0], *ends[1]], axis=0)
    last = query[...].astype(f32)[-2:]
    each = groups // MINOR
    rows = each * POLES
    size = rows + each * RAW + EXTRA
    for j in range(MINOR):
        lanes = [slice(g * LANES, (g + 1) * LANES) for g in range(each * j, each * (j + 1))]
        parcel[j * size : j * size + rows, :] = states[rows * j : rows * (j + 1), :].astype(bf16)
        pieces = [raw[:, x] for x in lanes] + [last[:, x] for x in lanes]
        pieces.append(jnp.zeros((EXTRA - 2 * each, LANES), f32))
        parcel[j * size + rows : (j + 1) * size, :] = jnp.concatenate(pieces, axis=0).astype(bf16)


def opening_of(tap, head, tail):
    result = [[], []]
    for g in range(head.shape[0] // RAW):
        pair = [[], []]
        for side in range(2):
            weight = [
                tap[g * POLES + 3 + 3 * side + lag : g * POLES + 4 + 3 * side + lag, :]
                for lag in range(3)
            ]
            at = g * RAW + 4 * side
            line = [tail[at + 2 + r : at + 3 + r, :] for r in range(2)]
            line += [head[at + r : at + 1 + r, :] for r in range(2)]
            for t in range(2):
                pair[t].append(fir(weight, line[t + 2], line[t + 1], line[t]))
        for t in range(2):
            m = pair[t][0] * pair[t][1]
            result[t].append(jnp.broadcast_to(m, (POLES, LANES)))
    return [jnp.concatenate(x, axis=0) for x in result]


def piece_of(place, filters, decay):
    chans = decay.shape[1] // MINOR
    start = pl.multiple_of((place[0] % MINOR) * chans, LANES)
    rates = decay[:, pl.ds(start, chans)]
    taps = jnp.concatenate([filters[which, :, pl.ds(start, chans)] for which in range(3)], axis=0)
    taps = jnp.concatenate([taps, jnp.zeros((POLES - 9, chans), f32)], axis=0)
    return [
        jnp.concatenate([x[:, g : g + LANES] for g in range(0, chans, LANES)], axis=0)
        for x in (rates, taps)
    ]


def is_head(shape):
    return (lax.broadcasted_iota(jnp.int32, shape, 0) & 2) == 0


def not_extra(shape):
    return lax.broadcasted_iota(jnp.int32, shape, 0) < shape[0] - EXTRA


def minor_kernel(block, place, arrived, filters, decay_rate, skip, sums, prefix):
    del skip
    rate, tap = piece_of(place, filters, decay_rate)
    size = arrived.shape[0] // MINOR
    rows = rate.shape[0]
    decay = jnp.exp(-rate * block)
    late = [jnp.exp(-rate * (block - 1.0)), jnp.exp(-rate * (block - 2.0))]
    total = jnp.zeros((rows, LANES), f32)
    raw = []
    for b in range(MINOR):
        prefix[b * rows : (b + 1) * rows, :] = total
        total = decay * total + arrived[b * size : b * size + rows, :].astype(f32)
        raw.append(arrived[b * size + rows : (b + 1) * size, :].astype(f32))
        if b:
            m = opening_of(tap, raw[b][:-EXTRA], raw[b - 1])
            total = total + (late[0] * m[0] + late[1] * m[1])
    head = is_head(raw[0].shape) & not_extra(raw[0].shape)
    ends = jnp.where(head, raw[0], raw[-1]).astype(bf16)
    total = total.astype(bf16)
    for other in range(MIDDLE):
        sums[other * size : other * size + rows, :] = total
        sums[other * size + rows : (other + 1) * size, :] = ends


def lines_of(block, rate, tap, arrived, state, tail):
    size = arrived.shape[0] // MIDDLE
    rows = rate.shape[0]
    line_decay = jnp.exp(-rate * (block * MINOR))
    rest_decay = jnp.exp(-rate * (block * (MINOR - 1)))
    late = [jnp.exp(-rate * (block - 1.0)), jnp.exp(-rate * (block - 2.0))]
    entering, openings, tails = [], [], []
    for line in range(MIDDLE):
        raw = arrived[line * size + rows : (line + 1) * size, :].astype(f32)
        m = opening_of(tap, raw[:-EXTRA], tail)
        tails.append(tail)
        openings.append(late[0] * m[0] + late[1] * m[1])
        entering.append(state)
        piece = arrived[line * size : line * size + rows, :].astype(f32)
        state = line_decay * state + (piece + rest_decay * openings[-1])
        tail = raw
    return entering, openings, tails, state, tail


def ahead_kernel(block, place, arrived, filters, decay_rate, ahead):
    rate, tap = piece_of(place, filters, decay_rate)
    rows = rate.shape[0]
    begin = jnp.zeros((rows, LANES), f32), jnp.zeros((ahead.shape[0] - rows, LANES), f32)
    *_, state, tail = lines_of(block, rate, tap, arrived, *begin)
    ahead[:rows, :] = state.astype(bf16)
    ahead[rows:, :] = tail.astype(bf16)


def tail_rows(raw):
    at = raw.shape[0] - EXTRA
    rows = []
    for g in range(at // RAW):
        rows += [raw[g * RAW + 2 : g * RAW + 4], raw[g * RAW + 6 : g * RAW + 8]]
        rows += [raw[at + 2 * g : at + 2 * g + 2], jnp.zeros((2, LANES), f32)]
    return jnp.concatenate(rows, axis=0)


def middle_kernel(block, place, line, arrived, ahead, prefix, filters, decay_rate, carries):
    rate, tap = piece_of(place, filters, decay_rate)
    rows = rate.shape[0]
    mine = (place[0] // MINOR) % MIDDLE
    begin = ahead[:rows, :].astype(f32), ahead[rows:, :].astype(f32)
    entering, openings, tails, *_ = lines_of(block, rate, tap, arrived, *begin)
    before, own, tail = entering[0], openings[0], tails[0]
    for other in range(1, MIDDLE):
        before = jnp.where(mine == other, entering[other], before)
        own = jnp.where(mine == other, openings[other], own)
        tail = jnp.where(mine == other, tails[other], tail)
    decay = jnp.exp(-rate * block)
    size = line.shape[0] // MINOR
    out = carries.shape[0] // MINOR
    for b in range(MINOR):
        here = before + prefix[b * rows : (b + 1) * rows, :]
        if b:
            here = here + own
            own = decay * own
            tail = line[(b - 1) * size + rows : b * size, :].astype(f32)
        carries[b * out : b * out + rows, :] = here.astype(bf16)
        carries[b * out + rows : (b + 1) * out, :] = tail_rows(tail).astype(bf16)
        before = decay * before


def inner_kernel(
    upper, place, query_hbm, key_hbm, value_hbm, residual_hbm, residue_hbm, skip_hbm, filters, decay,
    base_hbm, feature_hbm, heads, skip, query_in, key_in, value_in, residual, residue, queries, keys, values, streams, feature,
    weights, rates, taps, sem, out_sem,
):
    tokens, chans = query_in.shape
    groups = chans // LANES
    halves = groups // SUBLANES
    width = SUBLANES * LANES
    lanes = (
        (query_hbm, query_in, queries),
        (key_hbm, key_in, keys),
        (value_hbm, value_in, values),
        (residual_hbm, residual, streams),
    )
    parts = out_sem.shape[0] // (2 * halves)
    span = tokens * SUBLANES // parts

    @pl.when((place[0] >= MINOR * MIDDLE) == upper)
    def _():
        small = [
            pltpu.make_async_copy(residue_hbm, residue, sem.at[0]),
            pltpu.make_async_copy(skip_hbm, skip, sem.at[1]),
        ]
        for copy in small:
            copy.start()
        copies = []
        for half in range(halves):
            columns = slice(half * width, (half + 1) * width)
            for i, (source, target, _) in enumerate(lanes):
                copies.append(
                    pltpu.make_async_copy(
                        source.at[:, columns], target.at[:, columns], sem.at[2 + 4 * half + i]
                    )
                )
                copies[-1].start()
        fill_tables(filters, decay, rates, taps)
        for copy in small:
            copy.wait()
        for g in range(groups):
            weights[g * POLES : (g + 1) * POLES, :] = residue[:, g * LANES : (g + 1) * LANES]
        outward = []
        for half in range(halves):
            for i, (_, source, target) in enumerate(lanes):
                copies[4 * half + i].wait()
                columns = range(half * SUBLANES, (half + 1) * SUBLANES)
                spread(source, target, 0, columns, groups)
            for i in range(3):
                for t in range(HALO):
                    put(heads, HALO * i + t, half, groups, tile(lanes[i][2], t, half, groups))
            taps_here = [taps_of(taps, which, half) for which in range(3)]

            def filtered(i, carry):
                carry = list(carry)
                for u in range(STEP):
                    t = HALO + i * STEP + u
                    now = [tile(lanes[w][2], t, half, groups) for w in range(3)]
                    out = [
                        fir(taps_here[w], now[w], carry[2 * w], carry[2 * w + 1]) for w in range(3)
                    ]
                    put(feature, t, half, groups, out[0])
                    put(keys, t, half, groups, out[1] * out[2])
                    for w in range(3):
                        carry[2 * w + 1], carry[2 * w] = carry[2 * w], now[w]
                return tuple(carry)

            begin = tuple(tile(lanes[w][2], t, half, groups) for w in range(3) for t in (1, 0))
            lax.fori_loop(0, (tokens - HALO) // STEP, filtered, begin)
            for t in range(HALO):
                put(feature, t, half, groups, jnp.zeros((SUBLANES, LANES), f32))

            factor, weight = [], []
            for n in range(POLES):
                rate = rates[poled(n, half), :]
                factor.append(jnp.exp(-rate))
                weight.append(weights[poled(n, half), :] * jnp.sqrt(2.0 * rate))
            direct = tile(skip, 0, half, groups)

            def turn(i, state):
                for u in range(STEP):
                    t = HALO + i * STEP + u
                    m = tile(keys, t, half, groups)
                    state = [factor[n] * state[n] + m for n in range(POLES)]
                    sums = [direct * m, weight[0] * state[0]]
                    for n in range(1, POLES):
                        sums[n % 2] = sums[n % 2] + weight[n] * state[n]
                    gated = tile(feature, t, half, groups) * (sums[0] + sums[1])
                    put(streams, t, half, groups, tile(streams, t, half, groups) + gated)
                return tuple(state)

            state = (jnp.zeros((SUBLANES, LANES), f32),) * POLES
            turns = (tokens - HALO) // STEP
            done = 0
            for p in range(parts):
                last = min(turns, -((HALO - (p + 1) * tokens // parts) // STEP))
                state = lax.fori_loop(done, last, turn, state)
                done = last
                rows = slice(span * (parts * half + p), span * (parts * half + p + 1))
                for i, (source, target) in enumerate(
                    ((streams, base_hbm), (feature, feature_hbm))
                ):
                    slot = 2 * (parts * half + p) + i
                    outward.append(
                        pltpu.make_async_copy(
                            source.at[rows, :], target.at[rows, :], out_sem.at[slot]
                        )
                    )
                    outward[-1].start()
        for copy in outward:
            copy.wait()


def outer_kernel(
    place, carries, filters, decay, residue, skip, heads_low, heads_high,
    base_low, feature_low, base_high, feature_high, summed, squares,
    carried, before, rates, taps, weights, query, gated, sem,
):
    tokens, chans = summed.shape
    groups = chans // LANES
    lower = place[0] < MINOR * MIDDLE
    parts = sem.shape[0] // (2 * (groups // SUBLANES))
    span = tokens // parts

    def copies_from(feature, base):
        copies = []
        for p in range(sem.shape[0] // 2):
            part = slice(p * span * SUBLANES, (p + 1) * span * SUBLANES)
            for i, (source, target) in enumerate(((feature, query), (base, gated))):
                copies.append(
                    pltpu.make_async_copy(
                        source.at[part, :], target.at[part, :], sem.at[2 * p + i]
                    )
                )
        return copies

    copies = copies_from(feature_low, base_low)

    @pl.when(lower)
    def _():
        for copy in copies:
            copy.start()

    @pl.when(jnp.logical_not(lower))
    def _():
        for copy in copies_from(feature_high, base_high):
            copy.start()

    fill_tables(filters, decay, rates, taps)
    for g in range(groups):
        weights[g * POLES : (g + 1) * POLES, :] = residue[:, g * LANES : (g + 1) * LANES]
    size = carries.shape[0] // MINOR
    rows = groups // MINOR * POLES
    for j in range(MINOR):
        piece = carries[j * size : (j + 1) * size, :].astype(f32)
        carried[j * rows : (j + 1) * rows, :] = piece[:rows]
        before[j * (size - rows) : (j + 1) * (size - rows), :] = piece[rows:]

    def chosen(low, high, item, half):
        return jnp.where(lower, tile(low, item, half, groups), tile(high, item, half, groups))

    for half in range(groups // SUBLANES):
        opening = []
        for i, at in enumerate((4, 0, 2)):
            line = [before[poled(at + r, half, RAW), :] for r in range(2)]
            line += [chosen(heads_low, heads_high, HALO * i + r, half) for r in range(2)]
            weight = taps_of(taps, i, half)
            opening.append([fir(weight, line[t + 2], line[t + 1], line[t]) for t in range(2)])
        mixed = [opening[1][t] * opening[2][t] for t in range(2)]
        factor, state, weight = [], [], []
        for n in range(POLES):
            rate = rates[poled(n, half), :]
            factor.append(jnp.exp(-rate))
            weight.append(weights[poled(n, half), :] * jnp.sqrt(2.0 * rate))
            state.append(weight[n] * (factor[n] * carried[poled(n, half), :] + mixed[0]))
        direct = tile(skip, 0, half, groups)

        def total_of(state, first):
            sums = [state[0] if first is None else first + state[0], state[1]]
            for n in range(2, POLES):
                sums[n % 2] = sums[n % 2] + state[n]
            return sums[0] + sums[1]

        start = []
        for t in range(HALO):
            if t:
                state = [factor[n] * state[n] + weight[n] * mixed[t] for n in range(POLES)]
            start.append(opening[0][t] * total_of(state, direct * mixed[t]))
        state = tuple(factor[n] * state[n] for n in range(POLES))

        def turn(i, state):
            for u in range(STEP):
                t = HALO + i * STEP + u
                added = tile(query, t, half, groups) * total_of(state, None)
                put(gated, t, half, groups, tile(gated, t, half, groups) + added)
                state = tuple(factor[n] * state[n] for n in range(POLES))
            return state

        turns = (tokens - HALO) // STEP
        done = 0
        for p in range(parts):
            for copy in copies[2 * (parts * half + p) : 2 * (parts * half + p + 1)]:
                copy.wait()
            if p == 0:
                for t in range(HALO):
                    put(gated, t, half, groups, tile(gated, t, half, groups) + start[t])
            last = turns if p == parts - 1 else ((p + 1) * span - HALO) // STEP
            state = lax.fori_loop(done, last, turn, state)
            done = last
    total = jnp.zeros((tokens, LANES), f32)
    for g in range(groups):
        start = g // SUBLANES * tokens * SUBLANES + g % SUBLANES
        value = gated[pl.ds(start, tokens, stride=SUBLANES), :].astype(bf16)
        summed[:, g * LANES : (g + 1) * LANES] = value
        value = value.astype(f32)
        total = total + value * value
    squares[...] = jnp.broadcast_to(jnp.sum(total.T, axis=0, keepdims=True), squares.shape)


def norm_kernel(summed, squares, gain, stream_out, normed_out, normed, sem):
    tokens, chans = summed.shape
    parts = 4
    width = chans // parts
    stream = pltpu.make_async_copy(summed, stream_out, sem.at[parts])
    stream.start()
    mean = jnp.sum(squares[...], axis=0, keepdims=True) / D
    inverse = jnp.broadcast_to(lax.rsqrt(mean + EPSILON), (LANES, tokens)).T
    copies = []
    for part in range(parts):
        for g in range(part * width // LANES, (part + 1) * width // LANES):
            columns = slice(g * LANES, (g + 1) * LANES)
            normed[:, columns] = (
                summed[:, columns].astype(f32) * inverse * gain[g : g + 1, :]
            ).astype(bf16)
        columns = slice(part * width, (part + 1) * width)
        copies.append(
            pltpu.make_async_copy(normed.at[:, columns], normed_out.at[:, columns], sem.at[part])
        )
        copies[part].start()
    for copy in copies:
        copy.wait()
    stream.wait()


def layer(
    residual, query_in, key_in, value_in, short_filter, decay_rate, residue, skip_gain, norm_gain
):
    tokens, chans = residual.shape
    groups = chans // LANES
    count = MINOR * MIDDLE * MAJOR
    block = float(tokens)

    def shape(rows, kind=f32):
        return jax.ShapeDtypeStruct((rows, LANES), kind)

    def hold(rows):
        return pltpu.VMEM((rows, LANES), f32)

    smem = pl.BlockSpec(memory_space=pltpu.SMEM)
    vmem = pl.BlockSpec(memory_space=pltpu.VMEM)
    hbm = pl.BlockSpec(memory_space=pltpu.HBM)
    wide = pltpu.VMEM((tokens, chans), bf16)
    poled_rows = POLES * groups
    parcel_rows = (POLES + RAW) * groups + EXTRA * MINOR

    parcel = call(
        first_kernel,
        shape(parcel_rows, bf16),
        room=10.1,
        in_specs=[hbm] * 5,
        scratch=[
            wide,
            wide,
            pltpu.VMEM((8, chans), bf16),
            pltpu.VMEM(short_filter.shape, f32),
            pltpu.VMEM(decay_rate.shape, f32),
            hold(tokens * groups),
            hold(tokens * groups),
            hold(poled_rows),
            hold(poled_rows),
            hold(poled_rows),
            pltpu.SemaphoreType.DMA((3 + 2 * (groups // SUBLANES),)),
        ],
    )(query_in, key_in, value_in, short_filter, decay_rate)

    place = lax.axis_index("seq").astype(jnp.int32).reshape(1)
    lines = [[g * MINOR + j for j in range(MINOR)] for g in range(MIDDLE * MAJOR)]
    planes = [
        [(z * MIDDLE + y) * MINOR + j for y in range(MIDDLE)]
        for z in range(MAJOR)
        for j in range(MINOR)
    ]

    def exchange(x, members):
        return lax.all_to_all(x, "seq", 0, 0, axis_index_groups=members, tiled=True)

    tables_in = (short_filter, decay_rate)
    skip = skip_gain.reshape(groups, LANES)
    parcel, place = lax.optimization_barrier((parcel, place))
    arrived = exchange(parcel, lines)
    sums, prefix = call(
        functools.partial(minor_kernel, block),
        (shape(parcel_rows, bf16), shape(poled_rows)),
        in_specs=[smem, vmem, vmem, vmem, vmem],
    )(place, arrived, *tables_in, skip)
    line = arrived
    arrived = exchange(sums, planes)
    ahead = call(
        functools.partial(ahead_kernel, block),
        shape(parcel_rows // MINOR, bf16),
        in_specs=[smem, vmem, vmem, vmem],
    )(place, arrived, *tables_in)

    def inner(upper, place):
        return call(
            functools.partial(inner_kernel, upper),
            (
                shape(tokens * groups),
                shape(tokens * groups),
                shape(3 * HALO * groups),
            ),
            room=10.25,
            in_specs=[smem] + [hbm] * 6 + [vmem] * 2,
            out_specs=(hbm, hbm, vmem),
            scratch=[hold(groups)]
            + [wide] * 4
            + [pltpu.VMEM(residue.shape, f32)]
            + [hold(tokens * groups)] * 5
            + [hold(poled_rows)] * 3
            + [pltpu.SemaphoreType.DMA((2 + 4 * (groups // SUBLANES),))]
            + [pltpu.SemaphoreType.DMA((16,))],
        )(place, query_in, key_in, value_in, residual, residue, skip, *tables_in)

    place, ahead = lax.optimization_barrier((place, ahead))
    low = inner(False, place)
    *low, ahead = lax.optimization_barrier((*low, ahead))
    ahead = lax.ppermute(ahead, "seq", [(i, i + count // 2) for i in range(count // 2)])
    high = inner(True, place)
    carries = call(
        functools.partial(middle_kernel, block),
        shape(poled_rows + RAW * groups, bf16),
        in_specs=[smem] + [vmem] * 6,
    )(place, line, arrived, ahead, prefix, *tables_in)
    carries = exchange(carries, lines)
    members = lax.axis_size("chan")
    summed, squares = call(
        outer_kernel,
        (
            jax.ShapeDtypeStruct((tokens, chans), bf16),
            jax.ShapeDtypeStruct((members, tokens), f32),
        ),
        room=11.5,
        in_specs=[smem] + [vmem] * 7 + [hbm] * 4,
        scratch=[
            hold(poled_rows),
            hold(RAW * groups),
            hold(poled_rows),
            hold(poled_rows),
            hold(poled_rows),
            hold(tokens * groups),
            hold(tokens * groups),
            pltpu.SemaphoreType.DMA((16,)),
        ],
    )(
        place,
        carries,
        *tables_in,
        residue,
        skip,
        low[2],
        high[2],
        low[0],
        low[1],
        high[0],
        high[1],
    )
    squares = lax.all_to_all(squares, "chan", 0, 0, tiled=True)
    whole = jax.ShapeDtypeStruct((tokens, chans), bf16)
    return call(
        norm_kernel,
        (whole, whole),
        in_specs=[vmem] * 3,
        out_specs=(hbm, hbm),
        scratch=[wide, pltpu.SemaphoreType.DMA((5,))],
    )(summed, squares, norm_gain.reshape(groups, LANES))


def solution(mesh):
    whole = P("seq", "chan")
    in_specs = (whole, whole, whole, whole, P(None, None, "chan"))
    in_specs += (P(None, "chan"), P(None, "chan"), P("chan"), P("chan"))
    return jax.shard_map(
        layer, mesh=mesh, in_specs=in_specs, out_specs=(whole, whole), check_vma=False
    )
```

```python
import functools

import jax
import jax.numpy as jnp
from jax import lax
from jax.experimental import pallas as pl
from jax.experimental.pallas import tpu as pltpu
from jax.sharding import PartitionSpec as P


D = 8192
EPSILON = 1e-06
LANES = 128
SUBLANES = 8
MINOR = 8
MIDDLE = 8
MAJOR = 2
STEP = 9
LONG_STEP = 18
HALO = 2
RAW = 8
EXTRA = 8

f32 = jnp.float32
bf16 = jnp.bfloat16

POLES = 16


def call(kernel, out_shape, scratch=(), room=50, **extra):
    limit = int((64 - room) * 1024) << 10
    return pl.pallas_call(
        kernel,
        out_shape=out_shape,
        scratch_shapes=scratch,
        compiler_params=pltpu.CompilerParams(vmem_limit_bytes=limit),
        **extra,
    )


def spread(source, target, first, columns, groups):
    items = source.shape[0]
    every = target.shape[0] // groups
    for g in columns:
        start = (g // SUBLANES * every + first) * SUBLANES + g % SUBLANES
        target[pl.ds(start, items, stride=SUBLANES), :] = source[
            :, g * LANES : (g + 1) * LANES
        ].astype(f32)


def at_tile(ref, item, half, groups):
    start = (half * (ref.shape[0] // groups) + item) * SUBLANES
    return pl.ds(start if isinstance(start, int) else pl.multiple_of(start, SUBLANES), SUBLANES)


def tile(ref, item, half, groups):
    return ref[at_tile(ref, item, half, groups), :]


def put(ref, item, half, groups, value):
    ref[at_tile(ref, item, half, groups), :] = value


def poled(item, half, stride=POLES):
    return pl.ds(half * SUBLANES * stride + item, SUBLANES, stride=stride)


def taps_of(taps, which, half):
    return [taps[poled(which * 3 + lag, half), :] for lag in range(3)]


def fir(taps, now, last, older):
    return taps[0] * now + taps[1] * last + taps[2] * older


def fill_tables(filters, decay, rates, taps):
    groups = decay.shape[1] // LANES
    for g in range(groups):
        columns = slice(g * LANES, (g + 1) * LANES)
        rates[g * POLES : (g + 1) * POLES, :] = decay[:, columns]
        for which in range(3):
            start = g * POLES + 3 * which
            taps[start : start + 3, :] = filters[which, :, columns]
        taps[g * POLES + 9 : (g + 1) * POLES, :] = jnp.zeros((POLES - 9, LANES), f32)


def first_kernel(
    query_in, key_in, value_in, filters_in, decay_in, parcel,
    key, value, query, filters, decay, keys, values, states, rates, taps, sem,
):
    tokens, chans = key.shape
    groups = chans // LANES
    halves = groups // SUBLANES
    width = SUBLANES * LANES

    def part(source, target, half, slot):
        columns = slice(half * width, (half + 1) * width)
        return pltpu.make_async_copy(source.at[:, columns], target.at[:, columns], sem.at[slot])

    small = [
        pltpu.make_async_copy(decay_in, decay, sem.at[0]),
        pltpu.make_async_copy(filters_in, filters, sem.at[1]),
        pltpu.make_async_copy(query_in.at[tokens - 8 : tokens, :], query, sem.at[2]),
    ]
    large = [
        (part(key_in, key, h, 3 + 2 * h), part(value_in, value, h, 4 + 2 * h))
        for h in range(halves)
    ]
    small[0].start()
    small[1].start()
    for pair in large:
        pair[0].start()
        pair[1].start()
    small[2].start()
    small[0].wait()
    small[1].wait()
    fill_tables(filters, decay, rates, taps)
    for half in range(halves):
        factor = [jnp.exp(-rates[poled(n, half), :]) for n in range(POLES)]
        key_taps = taps_of(taps, 1, half)
        value_taps = taps_of(taps, 2, half)
        for copy in large[half]:
            copy.wait()
        columns = range(half * SUBLANES, (half + 1) * SUBLANES)
        spread(key, keys, 0, columns, groups)
        spread(value, values, 0, columns, groups)

        def turn(i, carry):
            k1, k2, v1, v2, *state = carry
            for u in range(LONG_STEP):
                t = HALO + i * LONG_STEP + u
                k0 = tile(keys, t, half, groups)
                v0 = tile(values, t, half, groups)
                m = fir(key_taps, k0, k1, k2) * fir(value_taps, v0, v1, v2)
                state = [factor[n] * state[n] + m for n in range(POLES)]
                k1, k2, v1, v2 = k0, k1, v0, v1
            return (k1, k2, v1, v2, *state)

        begin = tuple(tile(x, t, half, groups) for x in (keys, values) for t in (1, 0))
        begin += (jnp.zeros((SUBLANES, LANES), f32),) * POLES
        end = lax.fori_loop(0, (tokens - HALO) // LONG_STEP, turn, begin)
        for n in range(POLES):
            states[poled(n, half), :] = end[4 + n]
    small[2].wait()
    ends = [(x[:16, :].astype(f32)[:2], x[tokens - 16 :, :].astype(f32)[-2:]) for x in (key, value)]
    raw = jnp.concatenate([*ends[0], *ends[1]], axis=0)
    last = query[...].astype(f32)[-2:]
    each = groups // MINOR
    rows = each * POLES
    size = rows + each * RAW + EXTRA
    for j in range(MINOR):
        lanes = [slice(g * LANES, (g + 1) * LANES) for g in range(each * j, each * (j + 1))]
        parcel[j * size : j * size + rows, :] = states[rows * j : rows * (j + 1), :].astype(bf16)
        pieces = [raw[:, x] for x in lanes] + [last[:, x] for x in lanes]
        pieces.append(jnp.zeros((EXTRA - 2 * each, LANES), f32))
        parcel[j * size + rows : (j + 1) * size, :] = jnp.concatenate(pieces, axis=0).astype(bf16)


def opening_of(tap, head, tail):
    result = [[], []]
    for g in range(head.shape[0] // RAW):
        pair = [[], []]
        for side in range(2):
            weight = [
                tap[g * POLES + 3 + 3 * side + lag : g * POLES + 4 + 3 * side + lag, :]
                for lag in range(3)
            ]
            at = g * RAW + 4 * side
            line = [tail[at + 2 + r : at + 3 + r, :] for r in range(2)]
            line += [head[at + r : at + 1 + r, :] for r in range(2)]
            for t in range(2):
                pair[t].append(fir(weight, line[t + 2], line[t + 1], line[t]))
        for t in range(2):
            m = pair[t][0] * pair[t][1]
            result[t].append(jnp.broadcast_to(m, (POLES, LANES)))
    return [jnp.concatenate(x, axis=0) for x in result]


def piece_of(place, filters, decay):
    chans = decay.shape[1] // MINOR
    start = pl.multiple_of((place[0] % MINOR) * chans, LANES)
    rates = decay[:, pl.ds(start, chans)]
    taps = jnp.concatenate([filters[which, :, pl.ds(start, chans)] for which in range(3)], axis=0)
    taps = jnp.concatenate([taps, jnp.zeros((POLES - 9, chans), f32)], axis=0)
    return [
        jnp.concatenate([x[:, g : g + LANES] for g in range(0, chans, LANES)], axis=0)
        for x in (rates, taps)
    ]


def is_head(shape):
    return (lax.broadcasted_iota(jnp.int32, shape, 0) & 2) == 0


def not_extra(shape):
    return lax.broadcasted_iota(jnp.int32, shape, 0) < shape[0] - EXTRA


def minor_kernel(block, place, arrived, filters, decay_rate, skip, sums, prefix):
    del skip
    rate, tap = piece_of(place, filters, decay_rate)
    size = arrived.shape[0] // MINOR
    rows = rate.shape[0]
    decay = jnp.exp(-rate * block)
    late = [jnp.exp(-rate * (block - 1.0)), jnp.exp(-rate * (block - 2.0))]
    total = jnp.zeros((rows, LANES), f32)
    raw = []
    for b in range(MINOR):
        prefix[b * rows : (b + 1) * rows, :] = total
        total = decay * total + arrived[b * size : b * size + rows, :].astype(f32)
        raw.append(arrived[b * size + rows : (b + 1) * size, :].astype(f32))
        if b:
            m = opening_of(tap, raw[b][:-EXTRA], raw[b - 1])
            total = total + (late[0] * m[0] + late[1] * m[1])
    head = is_head(raw[0].shape) & not_extra(raw[0].shape)
    ends = jnp.where(head, raw[0], raw[-1]).astype(bf16)
    total = total.astype(bf16)
    for other in range(MIDDLE):
        sums[other * size : other * size + rows, :] = total
        sums[other * size + rows : (other + 1) * size, :] = ends


def lines_of(block, rate, tap, arrived, state, tail):
    size = arrived.shape[0] // MIDDLE
    rows = rate.shape[0]
    line_decay = jnp.exp(-rate * (block * MINOR))
    rest_decay = jnp.exp(-rate * (block * (MINOR - 1)))
    late = [jnp.exp(-rate * (block - 1.0)), jnp.exp(-rate * (block - 2.0))]
    entering, openings, tails = [], [], []
    for line in range(MIDDLE):
        raw = arrived[line * size + rows : (line + 1) * size, :].astype(f32)
        m = opening_of(tap, raw[:-EXTRA], tail)
        tails.append(tail)
        openings.append(late[0] * m[0] + late[1] * m[1])
        entering.append(state)
        piece = arrived[line * size : line * size + rows, :].astype(f32)
        state = line_decay * state + (piece + rest_decay * openings[-1])
        tail = raw
    return entering, openings, tails, state, tail


def ahead_kernel(block, place, arrived, filters, decay_rate, ahead):
    rate, tap = piece_of(place, filters, decay_rate)
    rows = rate.shape[0]
    begin = jnp.zeros((rows, LANES), f32), jnp.zeros((ahead.shape[0] - rows, LANES), f32)
    *_, state, tail = lines_of(block, rate, tap, arrived, *begin)
    ahead[:rows, :] = state.astype(bf16)
    ahead[rows:, :] = tail.astype(bf16)


def tail_rows(raw):
    at = raw.shape[0] - EXTRA
    rows = []
    for g in range(at // RAW):
        rows += [raw[g * RAW + 2 : g * RAW + 4], raw[g * RAW + 6 : g * RAW + 8]]
        rows += [raw[at + 2 * g : at + 2 * g + 2], jnp.zeros((2, LANES), f32)]
    return jnp.concatenate(rows, axis=0)


def middle_kernel(block, place, line, arrived, ahead, prefix, filters, decay_rate, carries):
    rate, tap = piece_of(place, filters, decay_rate)
    rows = rate.shape[0]
    mine = (place[0] // MINOR) % MIDDLE
    begin = ahead[:rows, :].astype(f32), ahead[rows:, :].astype(f32)
    entering, openings, tails, *_ = lines_of(block, rate, tap, arrived, *begin)
    before, own, tail = entering[0], openings[0], tails[0]
    for other in range(1, MIDDLE):
        before = jnp.where(mine == other, entering[other], before)
        own = jnp.where(mine == other, openings[other], own)
        tail = jnp.where(mine == other, tails[other], tail)
    decay = jnp.exp(-rate * block)
    size = line.shape[0] // MINOR
    out = carries.shape[0] // MINOR
    for b in range(MINOR):
        here = before + prefix[b * rows : (b + 1) * rows, :]
        if b:
            here = here + own
            own = decay * own
            tail = line[(b - 1) * size + rows : b * size, :].astype(f32)
        carries[b * out : b * out + rows, :] = here.astype(bf16)
        carries[b * out + rows : (b + 1) * out, :] = tail_rows(tail).astype(bf16)
        before = decay * before


def inner_kernel(
    upper, place, query_hbm, key_hbm, value_hbm, residual_hbm, residue_hbm, skip_hbm, filters_hbm,
    decay_hbm, base_hbm, feature_hbm, heads, skip, filters, decay, query_in, key_in, value_in, residual, residue, queries, keys, values, streams, feature,
    weights, rates, taps, sem, out_sem,
):
    tokens, chans = query_in.shape
    groups = chans // LANES
    halves = groups // SUBLANES
    width = SUBLANES * LANES
    lanes = (
        (query_hbm, query_in, queries),
        (key_hbm, key_in, keys),
        (value_hbm, value_in, values),
        (residual_hbm, residual, streams),
    )
    parts = out_sem.shape[0] // (2 * halves)
    span = tokens * SUBLANES // parts

    @pl.when((place[0] >= MINOR * MIDDLE) == upper)
    def _():
        small = [
            pltpu.make_async_copy(residue_hbm, residue, sem.at[0]),
            pltpu.make_async_copy(skip_hbm, skip, sem.at[1]),
            pltpu.make_async_copy(filters_hbm, filters, sem.at[2]),
            pltpu.make_async_copy(decay_hbm, decay, sem.at[3]),
        ]
        for copy in small:
            copy.start()
        copies = []
        for half in range(halves):
            columns = slice(half * width, (half + 1) * width)
            for i, (source, target, _) in enumerate(lanes):
                copies.append(
                    pltpu.make_async_copy(
                        source.at[:, columns], target.at[:, columns], sem.at[4 + 4 * half + i]
                    )
                )
                copies[-1].start()
        for copy in small:
            copy.wait()
        fill_tables(filters, decay, rates, taps)
        for g in range(groups):
            weights[g * POLES : (g + 1) * POLES, :] = residue[:, g * LANES : (g + 1) * LANES]
        outward = []
        for half in range(halves):
            for i, (_, source, target) in enumerate(lanes):
                copies[4 * half + i].wait()
                columns = range(half * SUBLANES, (half + 1) * SUBLANES)
                spread(source, target, 0, columns, groups)
            for i in range(3):
                for t in range(HALO):
                    put(heads, HALO * i + t, half, groups, tile(lanes[i][2], t, half, groups))
            taps_here = [taps_of(taps, which, half) for which in range(3)]

            def filtered(i, carry):
                carry = list(carry)
                for u in range(STEP):
                    t = HALO + i * STEP + u
                    now = [tile(lanes[w][2], t, half, groups) for w in range(3)]
                    out = [
                        fir(taps_here[w], now[w], carry[2 * w], carry[2 * w + 1]) for w in range(3)
                    ]
                    put(feature, t, half, groups, out[0])
                    put(keys, t, half, groups, out[1] * out[2])
                    for w in range(3):
                        carry[2 * w + 1], carry[2 * w] = carry[2 * w], now[w]
                return tuple(carry)

            begin = tuple(tile(lanes[w][2], t, half, groups) for w in range(3) for t in (1, 0))
            lax.fori_loop(0, (tokens - HALO) // STEP, filtered, begin)
            for t in range(HALO):
                put(feature, t, half, groups, jnp.zeros((SUBLANES, LANES), f32))

            factor, weight = [], []
            for n in range(POLES):
                rate = rates[poled(n, half), :]
                factor.append(jnp.exp(-rate))
                weight.append(weights[poled(n, half), :] * jnp.sqrt(2.0 * rate))
            direct = tile(skip, 0, half, groups)

            def turn(i, state):
                for u in range(STEP):
                    t = HALO + i * STEP + u
                    m = tile(keys, t, half, groups)
                    state = [factor[n] * state[n] + m for n in range(POLES)]
                    sums = [direct * m, weight[0] * state[0]]
                    for n in range(1, POLES):
                        sums[n % 2] = sums[n % 2] + weight[n] * state[n]
                    gated = tile(feature, t, half, groups) * (sums[0] + sums[1])
                    put(streams, t, half, groups, tile(streams, t, half, groups) + gated)
                return tuple(state)

            state = (jnp.zeros((SUBLANES, LANES), f32),) * POLES
            turns = (tokens - HALO) // STEP
            done = 0
            for p in range(parts):
                last = min(turns, -((HALO - (p + 1) * tokens // parts) // STEP))
                state = lax.fori_loop(done, last, turn, state)
                done = last
                rows = slice(span * (parts * half + p), span * (parts * half + p + 1))
                for i, (source, target) in enumerate(
                    ((streams, base_hbm), (feature, feature_hbm))
                ):
                    slot = 2 * (parts * half + p) + i
                    outward.append(
                        pltpu.make_async_copy(
                            source.at[rows, :], target.at[rows, :], out_sem.at[slot]
                        )
                    )
                    outward[-1].start()
        for copy in outward:
            copy.wait()


def outer_kernel(
    place, carries, filters, decay, residue, skip, heads_low, heads_high,
    base_low, feature_low, base_high, feature_high, summed, squares,
    carried, before, rates, taps, weights, query, gated, sem,
):
    tokens, chans = summed.shape
    groups = chans // LANES
    lower = place[0] < MINOR * MIDDLE
    parts = sem.shape[0] // (2 * (groups // SUBLANES))
    span = tokens // parts

    def copies_from(feature, base):
        copies = []
        for p in range(sem.shape[0] // 2):
            part = slice(p * span * SUBLANES, (p + 1) * span * SUBLANES)
            for i, (source, target) in enumerate(((feature, query), (base, gated))):
                copies.append(
                    pltpu.make_async_copy(
                        source.at[part, :], target.at[part, :], sem.at[2 * p + i]
                    )
                )
        return copies

    copies = copies_from(feature_low, base_low)

    @pl.when(lower)
    def _():
        for copy in copies:
            copy.start()

    @pl.when(jnp.logical_not(lower))
    def _():
        for copy in copies_from(feature_high, base_high):
            copy.start()

    fill_tables(filters, decay, rates, taps)
    for g in range(groups):
        weights[g * POLES : (g + 1) * POLES, :] = residue[:, g * LANES : (g + 1) * LANES]
    size = carries.shape[0] // MINOR
    rows = groups // MINOR * POLES
    for j in range(MINOR):
        piece = carries[j * size : (j + 1) * size, :].astype(f32)
        carried[j * rows : (j + 1) * rows, :] = piece[:rows]
        before[j * (size - rows) : (j + 1) * (size - rows), :] = piece[rows:]

    def chosen(low, high, item, half):
        return jnp.where(lower, tile(low, item, half, groups), tile(high, item, half, groups))

    for half in range(groups // SUBLANES):
        opening = []
        for i, at in enumerate((4, 0, 2)):
            line = [before[poled(at + r, half, RAW), :] for r in range(2)]
            line += [chosen(heads_low, heads_high, HALO * i + r, half) for r in range(2)]
            weight = taps_of(taps, i, half)
            opening.append([fir(weight, line[t + 2], line[t + 1], line[t]) for t in range(2)])
        mixed = [opening[1][t] * opening[2][t] for t in range(2)]
        factor, state, weight = [], [], []
        for n in range(POLES):
            rate = rates[poled(n, half), :]
            factor.append(jnp.exp(-rate))
            weight.append(weights[poled(n, half), :] * jnp.sqrt(2.0 * rate))
            state.append(weight[n] * (factor[n] * carried[poled(n, half), :] + mixed[0]))
        direct = tile(skip, 0, half, groups)

        def total_of(state, first):
            sums = [state[0] if first is None else first + state[0], state[1]]
            for n in range(2, POLES):
                sums[n % 2] = sums[n % 2] + state[n]
            return sums[0] + sums[1]

        start = []
        for t in range(HALO):
            if t:
                state = [factor[n] * state[n] + weight[n] * mixed[t] for n in range(POLES)]
            start.append(opening[0][t] * total_of(state, direct * mixed[t]))
        state = tuple(factor[n] * state[n] for n in range(POLES))

        def turn(i, state):
            for u in range(STEP):
                t = HALO + i * STEP + u
                added = tile(query, t, half, groups) * total_of(state, None)
                put(gated, t, half, groups, tile(gated, t, half, groups) + added)
                state = tuple(factor[n] * state[n] for n in range(POLES))
            return state

        turns = (tokens - HALO) // STEP
        done = 0
        for p in range(parts):
            for copy in copies[2 * (parts * half + p) : 2 * (parts * half + p + 1)]:
                copy.wait()
            if p == 0:
                for t in range(HALO):
                    put(gated, t, half, groups, tile(gated, t, half, groups) + start[t])
            last = turns if p == parts - 1 else ((p + 1) * span - HALO) // STEP
            state = lax.fori_loop(done, last, turn, state)
            done = last
    total = jnp.zeros((tokens, LANES), f32)
    for g in range(groups):
        start = g // SUBLANES * tokens * SUBLANES + g % SUBLANES
        value = gated[pl.ds(start, tokens, stride=SUBLANES), :].astype(bf16)
        summed[:, g * LANES : (g + 1) * LANES] = value
        value = value.astype(f32)
        total = total + value * value
    squares[...] = jnp.broadcast_to(jnp.sum(total.T, axis=0, keepdims=True), squares.shape)


def norm_kernel(summed, squares, gain, stream_out, normed_out, normed, sem):
    tokens, chans = summed.shape
    parts = 4
    width = chans // parts
    stream = pltpu.make_async_copy(summed, stream_out, sem.at[parts])
    stream.start()
    mean = jnp.sum(squares[...], axis=0, keepdims=True) / D
    inverse = jnp.broadcast_to(lax.rsqrt(mean + EPSILON), (LANES, tokens)).T
    copies = []
    for part in range(parts):
        for g in range(part * width // LANES, (part + 1) * width // LANES):
            columns = slice(g * LANES, (g + 1) * LANES)
            normed[:, columns] = (
                summed[:, columns].astype(f32) * inverse * gain[g : g + 1, :]
            ).astype(bf16)
        columns = slice(part * width, (part + 1) * width)
        copies.append(
            pltpu.make_async_copy(normed.at[:, columns], normed_out.at[:, columns], sem.at[part])
        )
        copies[part].start()
    for copy in copies:
        copy.wait()
    stream.wait()


def layer(
    residual, query_in, key_in, value_in, short_filter, decay_rate, residue, skip_gain, norm_gain
):
    tokens, chans = residual.shape
    groups = chans // LANES
    count = MINOR * MIDDLE * MAJOR
    block = float(tokens)

    def shape(rows, kind=f32):
        return jax.ShapeDtypeStruct((rows, LANES), kind)

    def hold(rows):
        return pltpu.VMEM((rows, LANES), f32)

    smem = pl.BlockSpec(memory_space=pltpu.SMEM)
    vmem = pl.BlockSpec(memory_space=pltpu.VMEM)
    hbm = pl.BlockSpec(memory_space=pltpu.HBM)
    wide = pltpu.VMEM((tokens, chans), bf16)
    poled_rows = POLES * groups
    parcel_rows = (POLES + RAW) * groups + EXTRA * MINOR

    parcel = call(
        first_kernel,
        shape(parcel_rows, bf16),
        room=10.1,
        in_specs=[hbm] * 5,
        scratch=[
            wide,
            wide,
            pltpu.VMEM((8, chans), bf16),
            pltpu.VMEM(short_filter.shape, f32),
            pltpu.VMEM(decay_rate.shape, f32),
            hold(tokens * groups),
            hold(tokens * groups),
            hold(poled_rows),
            hold(poled_rows),
            hold(poled_rows),
            pltpu.SemaphoreType.DMA((3 + 2 * (groups // SUBLANES),)),
        ],
    )(query_in, key_in, value_in, short_filter, decay_rate)

    place = lax.axis_index("seq").astype(jnp.int32).reshape(1)
    lines = [[g * MINOR + j for j in range(MINOR)] for g in range(MIDDLE * MAJOR)]
    planes = [
        [(z * MIDDLE + y) * MINOR + j for y in range(MIDDLE)]
        for z in range(MAJOR)
        for j in range(MINOR)
    ]

    def exchange(x, members):
        return lax.all_to_all(x, "seq", 0, 0, axis_index_groups=members, tiled=True)

    tables_in = (short_filter, decay_rate)
    skip = skip_gain.reshape(groups, LANES)
    parcel, place = lax.optimization_barrier((parcel, place))
    arrived = exchange(parcel, lines)
    sums, prefix = call(
        functools.partial(minor_kernel, block),
        (shape(parcel_rows, bf16), shape(poled_rows)),
        in_specs=[smem, vmem, vmem, vmem, vmem],
    )(place, arrived, *tables_in, skip)
    line = arrived
    arrived = exchange(sums, planes)
    ahead = call(
        functools.partial(ahead_kernel, block),
        shape(parcel_rows // MINOR, bf16),
        in_specs=[smem, vmem, vmem, vmem],
    )(place, arrived, *tables_in)

    def inner(upper, place):
        return call(
            functools.partial(inner_kernel, upper),
            (
                shape(tokens * groups),
                shape(tokens * groups),
                shape(3 * HALO * groups),
            ),
            room=10.25,
            in_specs=[smem] + [hbm] * 8,
            out_specs=(hbm, hbm, vmem),
            scratch=[hold(groups)]
            + [pltpu.VMEM(short_filter.shape, f32), pltpu.VMEM(decay_rate.shape, f32)]
            + [wide] * 4
            + [pltpu.VMEM(residue.shape, f32)]
            + [hold(tokens * groups)] * 5
            + [hold(poled_rows)] * 3
            + [pltpu.SemaphoreType.DMA((4 + 4 * (groups // SUBLANES),))]
            + [pltpu.SemaphoreType.DMA((16,))],
        )(place, query_in, key_in, value_in, residual, residue, skip, *tables_in)

    place, ahead = lax.optimization_barrier((place, ahead))
    low = inner(False, place)
    *low, ahead = lax.optimization_barrier((*low, ahead))
    ahead = lax.ppermute(ahead, "seq", [(i, i + count // 2) for i in range(count // 2)])
    high = inner(True, place)
    carries = call(
        functools.partial(middle_kernel, block),
        shape(poled_rows + RAW * groups, bf16),
        in_specs=[smem] + [vmem] * 6,
    )(place, line, arrived, ahead, prefix, *tables_in)
    carries = exchange(carries, lines)
    members = lax.axis_size("chan")
    summed, squares = call(
        outer_kernel,
        (
            jax.ShapeDtypeStruct((tokens, chans), bf16),
            jax.ShapeDtypeStruct((members, tokens), f32),
        ),
        room=11.5,
        in_specs=[smem] + [vmem] * 7 + [hbm] * 4,
        scratch=[
            hold(poled_rows),
            hold(RAW * groups),
            hold(poled_rows),
            hold(poled_rows),
            hold(poled_rows),
            hold(tokens * groups),
            hold(tokens * groups),
            pltpu.SemaphoreType.DMA((16,)),
        ],
    )(
        place,
        carries,
        *tables_in,
        residue,
        skip,
        low[2],
        high[2],
        low[0],
        low[1],
        high[0],
        high[1],
    )
    squares = lax.all_to_all(squares, "chan", 0, 0, tiled=True)
    whole = jax.ShapeDtypeStruct((tokens, chans), bf16)
    return call(
        norm_kernel,
        (whole, whole),
        in_specs=[vmem] * 3,
        out_specs=(hbm, hbm),
        scratch=[wide, pltpu.SemaphoreType.DMA((5,))],
    )(summed, squares, norm_gain.reshape(groups, LANES))


def solution(mesh):
    whole = P("seq", "chan")
    in_specs = (whole, whole, whole, whole, P(None, None, "chan"))
    in_specs += (P(None, "chan"), P(None, "chan"), P("chan"), P("chan"))
    return jax.shard_map(
        layer, mesh=mesh, in_specs=in_specs, out_specs=(whole, whole), check_vma=False
    )
```

```python
import functools

import jax
import jax.numpy as jnp
from jax import lax
from jax.experimental import pallas as pl
from jax.experimental.pallas import tpu as pltpu
from jax.sharding import PartitionSpec as P


D = 8192
EPSILON = 1e-06
LANES = 128
SUBLANES = 8
MINOR = 8
MIDDLE = 8
MAJOR = 2
STEP = 9
LONG_STEP = 18
HALO = 2
RAW = 8
EXTRA = 8

f32 = jnp.float32
bf16 = jnp.bfloat16

POLES = 16


def call(kernel, out_shape, scratch=(), room=50, **extra):
    limit = int((64 - room) * 1024) << 10
    return pl.pallas_call(
        kernel,
        out_shape=out_shape,
        scratch_shapes=scratch,
        compiler_params=pltpu.CompilerParams(vmem_limit_bytes=limit),
        **extra,
    )


def spread(source, target, first, columns, groups):
    items = source.shape[0]
    every = target.shape[0] // groups
    for g in columns:
        start = (g // SUBLANES * every + first) * SUBLANES + g % SUBLANES
        target[pl.ds(start, items, stride=SUBLANES), :] = source[
            :, g * LANES : (g + 1) * LANES
        ].astype(f32)


def at_tile(ref, item, half, groups):
    start = (half * (ref.shape[0] // groups) + item) * SUBLANES
    return pl.ds(start if isinstance(start, int) else pl.multiple_of(start, SUBLANES), SUBLANES)


def tile(ref, item, half, groups):
    return ref[at_tile(ref, item, half, groups), :]


def put(ref, item, half, groups, value):
    ref[at_tile(ref, item, half, groups), :] = value


def poled(item, half, stride=POLES):
    return pl.ds(half * SUBLANES * stride + item, SUBLANES, stride=stride)


def taps_of(taps, which, half):
    return [taps[poled(which * 3 + lag, half), :] for lag in range(3)]


def fir(taps, now, last, older):
    return taps[0] * now + taps[1] * last + taps[2] * older


def fill_tables(filters, decay, rates, taps):
    groups = decay.shape[1] // LANES
    for g in range(groups):
        columns = slice(g * LANES, (g + 1) * LANES)
        rates[g * POLES : (g + 1) * POLES, :] = decay[:, columns]
        for which in range(3):
            start = g * POLES + 3 * which
            taps[start : start + 3, :] = filters[which, :, columns]
        taps[g * POLES + 9 : (g + 1) * POLES, :] = jnp.zeros((POLES - 9, LANES), f32)


def first_kernel(
    query_in, key_in, value_in, filters_in, decay_in, parcel,
    key, value, query, filters, decay, keys, values, states, rates, taps, sem,
):
    tokens, chans = key.shape
    groups = chans // LANES
    halves = groups // SUBLANES
    width = SUBLANES * LANES

    def part(source, target, half, slot):
        columns = slice(half * width, (half + 1) * width)
        return pltpu.make_async_copy(source.at[:, columns], target.at[:, columns], sem.at[slot])

    small = [
        pltpu.make_async_copy(decay_in, decay, sem.at[0]),
        pltpu.make_async_copy(filters_in, filters, sem.at[1]),
        pltpu.make_async_copy(query_in.at[tokens - 8 : tokens, :], query, sem.at[2]),
    ]
    large = [
        (part(key_in, key, h, 3 + 2 * h), part(value_in, value, h, 4 + 2 * h))
        for h in range(halves)
    ]
    small[0].start()
    small[1].start()
    for copy in large[0]:
        copy.start()
    small[0].wait()
    small[1].wait()
    fill_tables(filters, decay, rates, taps)
    for half in range(halves):
        factor = [jnp.exp(-rates[poled(n, half), :]) for n in range(POLES)]
        key_taps = taps_of(taps, 1, half)
        value_taps = taps_of(taps, 2, half)
        for copy in large[half]:
            copy.wait()
        for copy in large[half + 1] if half + 1 < halves else small[2:]:
            copy.start()
        columns = range(half * SUBLANES, (half + 1) * SUBLANES)
        spread(key, keys, 0, columns, groups)
        spread(value, values, 0, columns, groups)

        def turn(i, carry):
            k1, k2, v1, v2, *state = carry
            for u in range(LONG_STEP):
                t = HALO + i * LONG_STEP + u
                k0 = tile(keys, t, half, groups)
                v0 = tile(values, t, half, groups)
                m = fir(key_taps, k0, k1, k2) * fir(value_taps, v0, v1, v2)
                state = [factor[n] * state[n] + m for n in range(POLES)]
                k1, k2, v1, v2 = k0, k1, v0, v1
            return (k1, k2, v1, v2, *state)

        begin = tuple(tile(x, t, half, groups) for x in (keys, values) for t in (1, 0))
        begin += (jnp.zeros((SUBLANES, LANES), f32),) * POLES
        end = lax.fori_loop(0, (tokens - HALO) // LONG_STEP, turn, begin)
        for n in range(POLES):
            states[poled(n, half), :] = end[4 + n]
    small[2].wait()
    ends = [(x[:16, :].astype(f32)[:2], x[tokens - 16 :, :].astype(f32)[-2:]) for x in (key, value)]
    raw = jnp.concatenate([*ends[0], *ends[1]], axis=0)
    last = query[...].astype(f32)[-2:]
    each = groups // MINOR
    rows = each * POLES
    size = rows + each * RAW + EXTRA
    for j in range(MINOR):
        lanes = [slice(g * LANES, (g + 1) * LANES) for g in range(each * j, each * (j + 1))]
        parcel[j * size : j * size + rows, :] = states[rows * j : rows * (j + 1), :].astype(bf16)
        pieces = [raw[:, x] for x in lanes] + [last[:, x] for x in lanes]
        pieces.append(jnp.zeros((EXTRA - 2 * each, LANES), f32))
        parcel[j * size + rows : (j + 1) * size, :] = jnp.concatenate(pieces, axis=0).astype(bf16)


def opening_of(tap, head, tail):
    result = [[], []]
    for g in range(head.shape[0] // RAW):
        pair = [[], []]
        for side in range(2):
            weight = [
                tap[g * POLES + 3 + 3 * side + lag : g * POLES + 4 + 3 * side + lag, :]
                for lag in range(3)
            ]
            at = g * RAW + 4 * side
            line = [tail[at + 2 + r : at + 3 + r, :] for r in range(2)]
            line += [head[at + r : at + 1 + r, :] for r in range(2)]
            for t in range(2):
                pair[t].append(fir(weight, line[t + 2], line[t + 1], line[t]))
        for t in range(2):
            m = pair[t][0] * pair[t][1]
            result[t].append(jnp.broadcast_to(m, (POLES, LANES)))
    return [jnp.concatenate(x, axis=0) for x in result]


def piece_of(place, filters, decay):
    chans = decay.shape[1] // MINOR
    start = pl.multiple_of((place[0] % MINOR) * chans, LANES)
    rates = decay[:, pl.ds(start, chans)]
    taps = jnp.concatenate([filters[which, :, pl.ds(start, chans)] for which in range(3)], axis=0)
    taps = jnp.concatenate([taps, jnp.zeros((POLES - 9, chans), f32)], axis=0)
    return [
        jnp.concatenate([x[:, g : g + LANES] for g in range(0, chans, LANES)], axis=0)
        for x in (rates, taps)
    ]


def is_head(shape):
    return (lax.broadcasted_iota(jnp.int32, shape, 0) & 2) == 0


def not_extra(shape):
    return lax.broadcasted_iota(jnp.int32, shape, 0) < shape[0] - EXTRA


def minor_kernel(block, place, arrived, filters, decay_rate, skip, sums, prefix):
    del skip
    rate, tap = piece_of(place, filters, decay_rate)
    size = arrived.shape[0] // MINOR
    rows = rate.shape[0]
    decay = jnp.exp(-rate * block)
    late = [jnp.exp(-rate * (block - 1.0)), jnp.exp(-rate * (block - 2.0))]
    total = jnp.zeros((rows, LANES), f32)
    raw = []
    for b in range(MINOR):
        prefix[b * rows : (b + 1) * rows, :] = total
        total = decay * total + arrived[b * size : b * size + rows, :].astype(f32)
        raw.append(arrived[b * size + rows : (b + 1) * size, :].astype(f32))
        if b:
            m = opening_of(tap, raw[b][:-EXTRA], raw[b - 1])
            total = total + (late[0] * m[0] + late[1] * m[1])
    head = is_head(raw[0].shape) & not_extra(raw[0].shape)
    ends = jnp.where(head, raw[0], raw[-1]).astype(bf16)
    total = total.astype(bf16)
    for other in range(MIDDLE):
        sums[other * size : other * size + rows, :] = total
        sums[other * size + rows : (other + 1) * size, :] = ends


def lines_of(block, rate, tap, arrived, state, tail):
    size = arrived.shape[0] // MIDDLE
    rows = rate.shape[0]
    line_decay = jnp.exp(-rate * (block * MINOR))
    rest_decay = jnp.exp(-rate * (block * (MINOR - 1)))
    late = [jnp.exp(-rate * (block - 1.0)), jnp.exp(-rate * (block - 2.0))]
    entering, openings, tails = [], [], []
    for line in range(MIDDLE):
        raw = arrived[line * size + rows : (line + 1) * size, :].astype(f32)
        m = opening_of(tap, raw[:-EXTRA], tail)
        tails.append(tail)
        openings.append(late[0] * m[0] + late[1] * m[1])
        entering.append(state)
        piece = arrived[line * size : line * size + rows, :].astype(f32)
        state = line_decay * state + (piece + rest_decay * openings[-1])
        tail = raw
    return entering, openings, tails, state, tail


def ahead_kernel(block, place, arrived, filters, decay_rate, ahead):
    rate, tap = piece_of(place, filters, decay_rate)
    rows = rate.shape[0]
    begin = jnp.zeros((rows, LANES), f32), jnp.zeros((ahead.shape[0] - rows, LANES), f32)
    *_, state, tail = lines_of(block, rate, tap, arrived, *begin)
    ahead[:rows, :] = state.astype(bf16)
    ahead[rows:, :] = tail.astype(bf16)


def tail_rows(raw):
    at = raw.shape[0] - EXTRA
    rows = []
    for g in range(at // RAW):
        rows += [raw[g * RAW + 2 : g * RAW + 4], raw[g * RAW + 6 : g * RAW + 8]]
        rows += [raw[at + 2 * g : at + 2 * g + 2], jnp.zeros((2, LANES), f32)]
    return jnp.concatenate(rows, axis=0)


def middle_kernel(block, place, line, arrived, ahead, prefix, filters, decay_rate, carries):
    rate, tap = piece_of(place, filters, decay_rate)
    rows = rate.shape[0]
    mine = (place[0] // MINOR) % MIDDLE
    begin = ahead[:rows, :].astype(f32), ahead[rows:, :].astype(f32)
    entering, openings, tails, *_ = lines_of(block, rate, tap, arrived, *begin)
    before, own, tail = entering[0], openings[0], tails[0]
    for other in range(1, MIDDLE):
        before = jnp.where(mine == other, entering[other], before)
        own = jnp.where(mine == other, openings[other], own)
        tail = jnp.where(mine == other, tails[other], tail)
    decay = jnp.exp(-rate * block)
    size = line.shape[0] // MINOR
    out = carries.shape[0] // MINOR
    for b in range(MINOR):
        here = before + prefix[b * rows : (b + 1) * rows, :]
        if b:
            here = here + own
            own = decay * own
            tail = line[(b - 1) * size + rows : b * size, :].astype(f32)
        carries[b * out : b * out + rows, :] = here.astype(bf16)
        carries[b * out + rows : (b + 1) * out, :] = tail_rows(tail).astype(bf16)
        before = decay * before


def inner_kernel(
    upper, place, query_hbm, key_hbm, value_hbm, residual_hbm, residue_hbm, skip_hbm, filters_hbm,
    decay_hbm, base_hbm, feature_hbm, heads, skip, filters, decay, query_in, key_in, value_in, residual, residue, queries, keys, values, streams, feature,
    weights, rates, taps, sem, out_sem,
):
    tokens, chans = query_in.shape
    groups = chans // LANES
    halves = groups // SUBLANES
    width = SUBLANES * LANES
    lanes = (
        (query_hbm, query_in, queries),
        (key_hbm, key_in, keys),
        (value_hbm, value_in, values),
        (residual_hbm, residual, streams),
    )
    parts = out_sem.shape[0] // (2 * halves)
    span = tokens * SUBLANES // parts

    @pl.when((place[0] >= MINOR * MIDDLE) == upper)
    def _():
        small = [
            pltpu.make_async_copy(residue_hbm, residue, sem.at[0]),
            pltpu.make_async_copy(skip_hbm, skip, sem.at[1]),
            pltpu.make_async_copy(filters_hbm, filters, sem.at[2]),
            pltpu.make_async_copy(decay_hbm, decay, sem.at[3]),
        ]
        for copy in small:
            copy.start()
        copies = []
        for half in range(halves):
            columns = slice(half * width, (half + 1) * width)
            for i, (source, target, _) in enumerate(lanes):
                copies.append(
                    pltpu.make_async_copy(
                        source.at[:, columns], target.at[:, columns], sem.at[4 + 4 * half + i]
                    )
                )
                copies[-1].start()
        for copy in small:
            copy.wait()
        fill_tables(filters, decay, rates, taps)
        for g in range(groups):
            weights[g * POLES : (g + 1) * POLES, :] = residue[:, g * LANES : (g + 1) * LANES]
        outward = []
        for half in range(halves):
            for i, (_, source, target) in enumerate(lanes):
                copies[4 * half + i].wait()
                columns = range(half * SUBLANES, (half + 1) * SUBLANES)
                spread(source, target, 0, columns, groups)
            for i in range(3):
                for t in range(HALO):
                    put(heads, HALO * i + t, half, groups, tile(lanes[i][2], t, half, groups))
            taps_here = [taps_of(taps, which, half) for which in range(3)]

            def filtered(i, carry):
                carry = list(carry)
                for u in range(STEP):
                    t = HALO + i * STEP + u
                    now = [tile(lanes[w][2], t, half, groups) for w in range(3)]
                    out = [
                        fir(taps_here[w], now[w], carry[2 * w], carry[2 * w + 1]) for w in range(3)
                    ]
                    put(feature, t, half, groups, out[0])
                    put(keys, t, half, groups, out[1] * out[2])
                    for w in range(3):
                        carry[2 * w + 1], carry[2 * w] = carry[2 * w], now[w]
                return tuple(carry)

            begin = tuple(tile(lanes[w][2], t, half, groups) for w in range(3) for t in (1, 0))
            lax.fori_loop(0, (tokens - HALO) // STEP, filtered, begin)
            for t in range(HALO):
                put(feature, t, half, groups, jnp.zeros((SUBLANES, LANES), f32))

            factor, weight = [], []
            for n in range(POLES):
                rate = rates[poled(n, half), :]
                factor.append(jnp.exp(-rate))
                weight.append(weights[poled(n, half), :] * jnp.sqrt(2.0 * rate))
            direct = tile(skip, 0, half, groups)

            def turn(i, state):
                for u in range(STEP):
                    t = HALO + i * STEP + u
                    m = tile(keys, t, half, groups)
                    state = [factor[n] * state[n] + m for n in range(POLES)]
                    sums = [direct * m, weight[0] * state[0]]
                    for n in range(1, POLES):
                        sums[n % 2] = sums[n % 2] + weight[n] * state[n]
                    gated = tile(feature, t, half, groups) * (sums[0] + sums[1])
                    put(streams, t, half, groups, tile(streams, t, half, groups) + gated)
                return tuple(state)

            state = (jnp.zeros((SUBLANES, LANES), f32),) * POLES
            turns = (tokens - HALO) // STEP
            done = 0
            for p in range(parts):
                last = min(turns, -((HALO - (p + 1) * tokens // parts) // STEP))
                state = lax.fori_loop(done, last, turn, state)
                done = last
                rows = slice(span * (parts * half + p), span * (parts * half + p + 1))
                for i, (source, target) in enumerate(
                    ((streams, base_hbm), (feature, feature_hbm))
                ):
                    slot = 2 * (parts * half + p) + i
                    outward.append(
                        pltpu.make_async_copy(
                            source.at[rows, :], target.at[rows, :], out_sem.at[slot]
                        )
                    )
                    outward[-1].start()
        for copy in outward:
            copy.wait()


def outer_kernel(
    place, carries, filters, decay, residue, skip, heads_low, heads_high,
    base_low, feature_low, base_high, feature_high, summed, squares,
    carried, before, rates, taps, weights, query, gated, sem,
):
    tokens, chans = summed.shape
    groups = chans // LANES
    lower = place[0] < MINOR * MIDDLE
    parts = sem.shape[0] // (2 * (groups // SUBLANES))
    span = tokens // parts

    def copies_from(feature, base):
        copies = []
        for p in range(sem.shape[0] // 2):
            part = slice(p * span * SUBLANES, (p + 1) * span * SUBLANES)
            for i, (source, target) in enumerate(((feature, query), (base, gated))):
                copies.append(
                    pltpu.make_async_copy(
                        source.at[part, :], target.at[part, :], sem.at[2 * p + i]
                    )
                )
        return copies

    copies = copies_from(feature_low, base_low)
    others = copies_from(feature_high, base_high)

    def begin(parts):
        @pl.when(lower)
        def _():
            for copy in copies[parts]:
                copy.start()

        @pl.when(jnp.logical_not(lower))
        def _():
            for copy in others[parts]:
                copy.start()

    ahead = 4
    begin(slice(0, ahead))
    fill_tables(filters, decay, rates, taps)
    for g in range(groups):
        weights[g * POLES : (g + 1) * POLES, :] = residue[:, g * LANES : (g + 1) * LANES]
    size = carries.shape[0] // MINOR
    rows = groups // MINOR * POLES
    for j in range(MINOR):
        piece = carries[j * size : (j + 1) * size, :].astype(f32)
        carried[j * rows : (j + 1) * rows, :] = piece[:rows]
        before[j * (size - rows) : (j + 1) * (size - rows), :] = piece[rows:]

    def chosen(low, high, item, half):
        return jnp.where(lower, tile(low, item, half, groups), tile(high, item, half, groups))

    for half in range(groups // SUBLANES):
        opening = []
        for i, at in enumerate((4, 0, 2)):
            line = [before[poled(at + r, half, RAW), :] for r in range(2)]
            line += [chosen(heads_low, heads_high, HALO * i + r, half) for r in range(2)]
            weight = taps_of(taps, i, half)
            opening.append([fir(weight, line[t + 2], line[t + 1], line[t]) for t in range(2)])
        mixed = [opening[1][t] * opening[2][t] for t in range(2)]
        factor, state, weight = [], [], []
        for n in range(POLES):
            rate = rates[poled(n, half), :]
            factor.append(jnp.exp(-rate))
            weight.append(weights[poled(n, half), :] * jnp.sqrt(2.0 * rate))
            state.append(weight[n] * (factor[n] * carried[poled(n, half), :] + mixed[0]))
        direct = tile(skip, 0, half, groups)

        def total_of(state, first):
            sums = [state[0] if first is None else first + state[0], state[1]]
            for n in range(2, POLES):
                sums[n % 2] = sums[n % 2] + state[n]
            return sums[0] + sums[1]

        start = []
        for t in range(HALO):
            if t:
                state = [factor[n] * state[n] + weight[n] * mixed[t] for n in range(POLES)]
            start.append(opening[0][t] * total_of(state, direct * mixed[t]))
        state = tuple(factor[n] * state[n] for n in range(POLES))

        def turn(i, state):
            for u in range(STEP):
                t = HALO + i * STEP + u
                added = tile(query, t, half, groups) * total_of(state, None)
                put(gated, t, half, groups, tile(gated, t, half, groups) + added)
                state = tuple(factor[n] * state[n] for n in range(POLES))
            return state

        turns = (tokens - HALO) // STEP
        done = 0
        for p in range(parts):
            now = 2 * (parts * half + p)
            for copy in copies[now : now + 2]:
                copy.wait()
            if now + ahead < len(copies):
                begin(slice(now + ahead, now + ahead + 2))
            if p == 0:
                for t in range(HALO):
                    put(gated, t, half, groups, tile(gated, t, half, groups) + start[t])
            last = turns if p == parts - 1 else ((p + 1) * span - HALO) // STEP
            state = lax.fori_loop(done, last, turn, state)
            done = last
    total = jnp.zeros((tokens, LANES), f32)
    for g in range(groups):
        start = g // SUBLANES * tokens * SUBLANES + g % SUBLANES
        value = gated[pl.ds(start, tokens, stride=SUBLANES), :].astype(bf16)
        summed[:, g * LANES : (g + 1) * LANES] = value
        value = value.astype(f32)
        total = total + value * value
    squares[...] = jnp.broadcast_to(jnp.sum(total.T, axis=0, keepdims=True), squares.shape)


def norm_kernel(summed, squares, gain, stream_out, normed_out, normed, sem):
    tokens, chans = summed.shape
    parts = 4
    width = chans // parts
    stream = pltpu.make_async_copy(summed, stream_out, sem.at[parts])
    stream.start()
    mean = jnp.sum(squares[...], axis=0, keepdims=True) / D
    inverse = jnp.broadcast_to(lax.rsqrt(mean + EPSILON), (LANES, tokens)).T
    copies = []
    for part in range(parts):
        for g in range(part * width // LANES, (part + 1) * width // LANES):
            columns = slice(g * LANES, (g + 1) * LANES)
            normed[:, columns] = (
                summed[:, columns].astype(f32) * inverse * gain[g : g + 1, :]
            ).astype(bf16)
        columns = slice(part * width, (part + 1) * width)
        copies.append(
            pltpu.make_async_copy(normed.at[:, columns], normed_out.at[:, columns], sem.at[part])
        )
        copies[part].start()
    for copy in copies:
        copy.wait()
    stream.wait()


def layer(
    residual, query_in, key_in, value_in, short_filter, decay_rate, residue, skip_gain, norm_gain
):
    tokens, chans = residual.shape
    groups = chans // LANES
    count = MINOR * MIDDLE * MAJOR
    block = float(tokens)

    def shape(rows, kind=f32):
        return jax.ShapeDtypeStruct((rows, LANES), kind)

    def hold(rows):
        return pltpu.VMEM((rows, LANES), f32)

    smem = pl.BlockSpec(memory_space=pltpu.SMEM)
    vmem = pl.BlockSpec(memory_space=pltpu.VMEM)
    hbm = pl.BlockSpec(memory_space=pltpu.HBM)
    wide = pltpu.VMEM((tokens, chans), bf16)
    poled_rows = POLES * groups
    parcel_rows = (POLES + RAW) * groups + EXTRA * MINOR

    parcel = call(
        first_kernel,
        shape(parcel_rows, bf16),
        room=10.1,
        in_specs=[hbm] * 5,
        scratch=[
            wide,
            wide,
            pltpu.VMEM((8, chans), bf16),
            pltpu.VMEM(short_filter.shape, f32),
            pltpu.VMEM(decay_rate.shape, f32),
            hold(tokens * groups),
            hold(tokens * groups),
            hold(poled_rows),
            hold(poled_rows),
            hold(poled_rows),
            pltpu.SemaphoreType.DMA((3 + 2 * (groups // SUBLANES),)),
        ],
    )(query_in, key_in, value_in, short_filter, decay_rate)

    place = lax.axis_index("seq").astype(jnp.int32).reshape(1)
    lines = [[g * MINOR + j for j in range(MINOR)] for g in range(MIDDLE * MAJOR)]
    planes = [
        [(z * MIDDLE + y) * MINOR + j for y in range(MIDDLE)]
        for z in range(MAJOR)
        for j in range(MINOR)
    ]

    def exchange(x, members):
        return lax.all_to_all(x, "seq", 0, 0, axis_index_groups=members, tiled=True)

    tables_in = (short_filter, decay_rate)
    skip = skip_gain.reshape(groups, LANES)
    parcel, place = lax.optimization_barrier((parcel, place))
    arrived = exchange(parcel, lines)
    sums, prefix = call(
        functools.partial(minor_kernel, block),
        (shape(parcel_rows, bf16), shape(poled_rows)),
        in_specs=[smem, vmem, vmem, vmem, vmem],
    )(place, arrived, *tables_in, skip)
    line = arrived
    arrived = exchange(sums, planes)
    ahead = call(
        functools.partial(ahead_kernel, block),
        shape(parcel_rows // MINOR, bf16),
        in_specs=[smem, vmem, vmem, vmem],
    )(place, arrived, *tables_in)

    def inner(upper, place):
        return call(
            functools.partial(inner_kernel, upper),
            (
                shape(tokens * groups),
                shape(tokens * groups),
                shape(3 * HALO * groups),
            ),
            room=10.25,
            in_specs=[smem] + [hbm] * 8,
            out_specs=(hbm, hbm, vmem),
            scratch=[hold(groups)]
            + [pltpu.VMEM(short_filter.shape, f32), pltpu.VMEM(decay_rate.shape, f32)]
            + [wide] * 4
            + [pltpu.VMEM(residue.shape, f32)]
            + [hold(tokens * groups)] * 5
            + [hold(poled_rows)] * 3
            + [pltpu.SemaphoreType.DMA((4 + 4 * (groups // SUBLANES),))]
            + [pltpu.SemaphoreType.DMA((16,))],
        )(place, query_in, key_in, value_in, residual, residue, skip, *tables_in)

    place, ahead = lax.optimization_barrier((place, ahead))
    low = inner(False, place)
    *low, ahead = lax.optimization_barrier((*low, ahead))
    ahead = lax.ppermute(ahead, "seq", [(i, i + count // 2) for i in range(count // 2)])
    high = inner(True, place)
    carries = call(
        functools.partial(middle_kernel, block),
        shape(poled_rows + RAW * groups, bf16),
        in_specs=[smem] + [vmem] * 6,
    )(place, line, arrived, ahead, prefix, *tables_in)
    carries = exchange(carries, lines)
    members = lax.axis_size("chan")
    summed, squares = call(
        outer_kernel,
        (
            jax.ShapeDtypeStruct((tokens, chans), bf16),
            jax.ShapeDtypeStruct((members, tokens), f32),
        ),
        room=11.5,
        in_specs=[smem] + [vmem] * 7 + [hbm] * 4,
        scratch=[
            hold(poled_rows),
            hold(RAW * groups),
            hold(poled_rows),
            hold(poled_rows),
            hold(poled_rows),
            hold(tokens * groups),
            hold(tokens * groups),
            pltpu.SemaphoreType.DMA((16,)),
        ],
    )(
        place,
        carries,
        *tables_in,
        residue,
        skip,
        low[2],
        high[2],
        low[0],
        low[1],
        high[0],
        high[1],
    )
    squares = lax.all_to_all(squares, "chan", 0, 0, tiled=True)
    whole = jax.ShapeDtypeStruct((tokens, chans), bf16)
    return call(
        norm_kernel,
        (whole, whole),
        in_specs=[vmem] * 3,
        out_specs=(hbm, hbm),
        scratch=[wide, pltpu.SemaphoreType.DMA((5,))],
    )(summed, squares, norm_gain.reshape(groups, LANES))


def solution(mesh):
    whole = P("seq", "chan")
    in_specs = (whole, whole, whole, whole, P(None, None, "chan"))
    in_specs += (P(None, "chan"), P(None, "chan"), P("chan"), P("chan"))
    return jax.shard_map(
        layer, mesh=mesh, in_specs=in_specs, out_specs=(whole, whole), check_vma=False
    )
```

```python
import functools

import jax
import jax.numpy as jnp
from jax import lax
from jax.experimental import pallas as pl
from jax.experimental.pallas import tpu as pltpu
from jax.sharding import PartitionSpec as P


D = 8192
EPSILON = 1e-06
LANES = 128
SUBLANES = 8
MINOR = 8
MIDDLE = 8
MAJOR = 2
STEP = 9
LONG_STEP = 18
HALO = 2
RAW = 8
EXTRA = 8

f32 = jnp.float32
bf16 = jnp.bfloat16

POLES = 16


def call(kernel, out_shape, scratch=(), room=50, **extra):
    limit = int((64 - room) * 1024) << 10
    return pl.pallas_call(
        kernel,
        out_shape=out_shape,
        scratch_shapes=scratch,
        compiler_params=pltpu.CompilerParams(vmem_limit_bytes=limit),
        **extra,
    )


def spread(source, target, first, columns, groups):
    items = source.shape[0]
    every = target.shape[0] // groups
    for g in columns:
        start = (g // SUBLANES * every + first) * SUBLANES + g % SUBLANES
        target[pl.ds(start, items, stride=SUBLANES), :] = source[
            :, g * LANES : (g + 1) * LANES
        ].astype(f32)


def at_tile(ref, item, half, groups):
    start = (half * (ref.shape[0] // groups) + item) * SUBLANES
    return pl.ds(start if isinstance(start, int) else pl.multiple_of(start, SUBLANES), SUBLANES)


def tile(ref, item, half, groups):
    return ref[at_tile(ref, item, half, groups), :]


def put(ref, item, half, groups, value):
    ref[at_tile(ref, item, half, groups), :] = value


def poled(item, half, stride=POLES):
    return pl.ds(half * SUBLANES * stride + item, SUBLANES, stride=stride)


def taps_of(taps, which, half):
    return [taps[poled(which * 3 + lag, half), :] for lag in range(3)]


def fir(taps, now, last, older):
    return taps[0] * now + taps[1] * last + taps[2] * older


def fill_tables(filters, decay, rates, taps):
    groups = decay.shape[1] // LANES
    for g in range(groups):
        columns = slice(g * LANES, (g + 1) * LANES)
        rates[g * POLES : (g + 1) * POLES, :] = decay[:, columns]
        for which in range(3):
            start = g * POLES + 3 * which
            taps[start : start + 3, :] = filters[which, :, columns]
        taps[g * POLES + 9 : (g + 1) * POLES, :] = jnp.zeros((POLES - 9, LANES), f32)


def first_kernel(
    query_in, key_in, value_in, filters_in, decay_in, parcel,
    key, value, query, filters, decay, keys, values, states, rates, taps, sem,
):
    tokens, chans = key.shape
    groups = chans // LANES
    halves = groups // SUBLANES
    width = SUBLANES * LANES

    pieces = 4
    span = tokens // pieces

    def part(source, target, half, slot):
        columns = slice(half * width, (half + 1) * width)
        return [
            pltpu.make_async_copy(
                source.at[p * span : (p + 1) * span, columns],
                target.at[p * span : (p + 1) * span, columns],
                sem.at[3 + slot * pieces + p],
            )
            for p in range(pieces)
        ]

    small = [
        pltpu.make_async_copy(decay_in, decay, sem.at[0]),
        pltpu.make_async_copy(filters_in, filters, sem.at[1]),
        pltpu.make_async_copy(query_in.at[tokens - 8 : tokens, :], query, sem.at[2]),
    ]
    large = [
        part(key_in, key, h, 2 * h) + part(value_in, value, h, 2 * h + 1) for h in range(halves)
    ]
    small[0].start()
    small[1].start()
    for group in large:
        for copy in group:
            copy.start()
    small[2].start()
    small[0].wait()
    small[1].wait()
    fill_tables(filters, decay, rates, taps)
    for half in range(halves):
        factor = [jnp.exp(-rates[poled(n, half), :]) for n in range(POLES)]
        key_taps = taps_of(taps, 1, half)
        value_taps = taps_of(taps, 2, half)
        for copy in large[half]:
            copy.wait()
        columns = range(half * SUBLANES, (half + 1) * SUBLANES)
        spread(key, keys, 0, columns, groups)
        spread(value, values, 0, columns, groups)

        def turn(i, carry):
            k1, k2, v1, v2, *state = carry
            for u in range(LONG_STEP):
                t = HALO + i * LONG_STEP + u
                k0 = tile(keys, t, half, groups)
                v0 = tile(values, t, half, groups)
                m = fir(key_taps, k0, k1, k2) * fir(value_taps, v0, v1, v2)
                state = [factor[n] * state[n] + m for n in range(POLES)]
                k1, k2, v1, v2 = k0, k1, v0, v1
            return (k1, k2, v1, v2, *state)

        begin = tuple(tile(x, t, half, groups) for x in (keys, values) for t in (1, 0))
        begin += (jnp.zeros((SUBLANES, LANES), f32),) * POLES
        end = lax.fori_loop(0, (tokens - HALO) // LONG_STEP, turn, begin)
        for n in range(POLES):
            states[poled(n, half), :] = end[4 + n]
    small[2].wait()
    ends = [(x[:16, :].astype(f32)[:2], x[tokens - 16 :, :].astype(f32)[-2:]) for x in (key, value)]
    raw = jnp.concatenate([*ends[0], *ends[1]], axis=0)
    last = query[...].astype(f32)[-2:]
    each = groups // MINOR
    rows = each * POLES
    size = rows + each * RAW + EXTRA
    for j in range(MINOR):
        lanes = [slice(g * LANES, (g + 1) * LANES) for g in range(each * j, each * (j + 1))]
        parcel[j * size : j * size + rows, :] = states[rows * j : rows * (j + 1), :].astype(bf16)
        pieces = [raw[:, x] for x in lanes] + [last[:, x] for x in lanes]
        pieces.append(jnp.zeros((EXTRA - 2 * each, LANES), f32))
        parcel[j * size + rows : (j + 1) * size, :] = jnp.concatenate(pieces, axis=0).astype(bf16)


def opening_of(tap, head, tail):
    result = [[], []]
    for g in range(head.shape[0] // RAW):
        pair = [[], []]
        for side in range(2):
            weight = [
                tap[g * POLES + 3 + 3 * side + lag : g * POLES + 4 + 3 * side + lag, :]
                for lag in range(3)
            ]
            at = g * RAW + 4 * side
            line = [tail[at + 2 + r : at + 3 + r, :] for r in range(2)]
            line += [head[at + r : at + 1 + r, :] for r in range(2)]
            for t in range(2):
                pair[t].append(fir(weight, line[t + 2], line[t + 1], line[t]))
        for t in range(2):
            m = pair[t][0] * pair[t][1]
            result[t].append(jnp.broadcast_to(m, (POLES, LANES)))
    return [jnp.concatenate(x, axis=0) for x in result]


def piece_of(place, filters, decay):
    chans = decay.shape[1] // MINOR
    start = pl.multiple_of((place[0] % MINOR) * chans, LANES)
    rates = decay[:, pl.ds(start, chans)]
    taps = jnp.concatenate([filters[which, :, pl.ds(start, chans)] for which in range(3)], axis=0)
    taps = jnp.concatenate([taps, jnp.zeros((POLES - 9, chans), f32)], axis=0)
    return [
        jnp.concatenate([x[:, g : g + LANES] for g in range(0, chans, LANES)], axis=0)
        for x in (rates, taps)
    ]


def is_head(shape):
    return (lax.broadcasted_iota(jnp.int32, shape, 0) & 2) == 0


def not_extra(shape):
    return lax.broadcasted_iota(jnp.int32, shape, 0) < shape[0] - EXTRA


def minor_kernel(block, place, arrived, filters, decay_rate, skip, sums, prefix):
    del skip
    rate, tap = piece_of(place, filters, decay_rate)
    size = arrived.shape[0] // MINOR
    rows = rate.shape[0]
    decay = jnp.exp(-rate * block)
    late = [jnp.exp(-rate * (block - 1.0)), jnp.exp(-rate * (block - 2.0))]
    total = jnp.zeros((rows, LANES), f32)
    raw = []
    for b in range(MINOR):
        prefix[b * rows : (b + 1) * rows, :] = total
        total = decay * total + arrived[b * size : b * size + rows, :].astype(f32)
        raw.append(arrived[b * size + rows : (b + 1) * size, :].astype(f32))
        if b:
            m = opening_of(tap, raw[b][:-EXTRA], raw[b - 1])
            total = total + (late[0] * m[0] + late[1] * m[1])
    head = is_head(raw[0].shape) & not_extra(raw[0].shape)
    ends = jnp.where(head, raw[0], raw[-1]).astype(bf16)
    total = total.astype(bf16)
    for other in range(MIDDLE):
        sums[other * size : other * size + rows, :] = total
        sums[other * size + rows : (other + 1) * size, :] = ends


def lines_of(block, rate, tap, arrived, state, tail):
    size = arrived.shape[0] // MIDDLE
    rows = rate.shape[0]
    line_decay = jnp.exp(-rate * (block * MINOR))
    rest_decay = jnp.exp(-rate * (block * (MINOR - 1)))
    late = [jnp.exp(-rate * (block - 1.0)), jnp.exp(-rate * (block - 2.0))]
    entering, openings, tails = [], [], []
    for line in range(MIDDLE):
        raw = arrived[line * size + rows : (line + 1) * size, :].astype(f32)
        m = opening_of(tap, raw[:-EXTRA], tail)
        tails.append(tail)
        openings.append(late[0] * m[0] + late[1] * m[1])
        entering.append(state)
        piece = arrived[line * size : line * size + rows, :].astype(f32)
        state = line_decay * state + (piece + rest_decay * openings[-1])
        tail = raw
    return entering, openings, tails, state, tail


def ahead_kernel(block, place, arrived, filters, decay_rate, ahead):
    rate, tap = piece_of(place, filters, decay_rate)
    rows = rate.shape[0]
    begin = jnp.zeros((rows, LANES), f32), jnp.zeros((ahead.shape[0] - rows, LANES), f32)
    *_, state, tail = lines_of(block, rate, tap, arrived, *begin)
    ahead[:rows, :] = state.astype(bf16)
    ahead[rows:, :] = tail.astype(bf16)


def tail_rows(raw):
    at = raw.shape[0] - EXTRA
    rows = []
    for g in range(at // RAW):
        rows += [raw[g * RAW + 2 : g * RAW + 4], raw[g * RAW + 6 : g * RAW + 8]]
        rows += [raw[at + 2 * g : at + 2 * g + 2], jnp.zeros((2, LANES), f32)]
    return jnp.concatenate(rows, axis=0)


def middle_kernel(block, place, line, arrived, ahead, prefix, filters, decay_rate, carries):
    rate, tap = piece_of(place, filters, decay_rate)
    rows = rate.shape[0]
    mine = (place[0] // MINOR) % MIDDLE
    begin = ahead[:rows, :].astype(f32), ahead[rows:, :].astype(f32)
    entering, openings, tails, *_ = lines_of(block, rate, tap, arrived, *begin)
    before, own, tail = entering[0], openings[0], tails[0]
    for other in range(1, MIDDLE):
        before = jnp.where(mine == other, entering[other], before)
        own = jnp.where(mine == other, openings[other], own)
        tail = jnp.where(mine == other, tails[other], tail)
    decay = jnp.exp(-rate * block)
    size = line.shape[0] // MINOR
    out = carries.shape[0] // MINOR
    for b in range(MINOR):
        here = before + prefix[b * rows : (b + 1) * rows, :]
        if b:
            here = here + own
            own = decay * own
            tail = line[(b - 1) * size + rows : b * size, :].astype(f32)
        carries[b * out : b * out + rows, :] = here.astype(bf16)
        carries[b * out + rows : (b + 1) * out, :] = tail_rows(tail).astype(bf16)
        before = decay * before


def inner_kernel(
    upper, place, query_hbm, key_hbm, value_hbm, residual_hbm, residue_hbm, skip_hbm, filters_hbm,
    decay_hbm, base_hbm, feature_hbm, heads, skip, filters, decay, query_in, key_in, value_in, residual, residue, queries, keys, values, streams, feature,
    weights, rates, taps, sem, out_sem,
):
    tokens, chans = query_in.shape
    groups = chans // LANES
    halves = groups // SUBLANES
    width = SUBLANES * LANES
    lanes = (
        (query_hbm, query_in, queries),
        (key_hbm, key_in, keys),
        (value_hbm, value_in, values),
        (residual_hbm, residual, streams),
    )
    parts = out_sem.shape[0] // (2 * halves)
    span = tokens * SUBLANES // parts

    @pl.when((place[0] >= MINOR * MIDDLE) == upper)
    def _():
        small = [
            pltpu.make_async_copy(residue_hbm, residue, sem.at[0]),
            pltpu.make_async_copy(skip_hbm, skip, sem.at[1]),
            pltpu.make_async_copy(filters_hbm, filters, sem.at[2]),
            pltpu.make_async_copy(decay_hbm, decay, sem.at[3]),
        ]
        for copy in small:
            copy.start()
        copies = []
        for half in range(halves):
            columns = slice(half * width, (half + 1) * width)
            for i, (source, target, _) in enumerate(lanes):
                copies.append(
                    pltpu.make_async_copy(
                        source.at[:, columns], target.at[:, columns], sem.at[4 + 4 * half + i]
                    )
                )
                copies[-1].start()
        for copy in small:
            copy.wait()
        fill_tables(filters, decay, rates, taps)
        for g in range(groups):
            weights[g * POLES : (g + 1) * POLES, :] = residue[:, g * LANES : (g + 1) * LANES]
        outward = []
        for half in range(halves):
            for i, (_, source, target) in enumerate(lanes):
                copies[4 * half + i].wait()
                columns = range(half * SUBLANES, (half + 1) * SUBLANES)
                spread(source, target, 0, columns, groups)
            for i in range(3):
                for t in range(HALO):
                    put(heads, HALO * i + t, half, groups, tile(lanes[i][2], t, half, groups))
            taps_here = [taps_of(taps, which, half) for which in range(3)]

            def filtered(i, carry):
                carry = list(carry)
                for u in range(STEP):
                    t = HALO + i * STEP + u
                    now = [tile(lanes[w][2], t, half, groups) for w in range(3)]
                    out = [
                        fir(taps_here[w], now[w], carry[2 * w], carry[2 * w + 1]) for w in range(3)
                    ]
                    put(feature, t, half, groups, out[0])
                    put(keys, t, half, groups, out[1] * out[2])
                    for w in range(3):
                        carry[2 * w + 1], carry[2 * w] = carry[2 * w], now[w]
                return tuple(carry)

            begin = tuple(tile(lanes[w][2], t, half, groups) for w in range(3) for t in (1, 0))
            lax.fori_loop(0, (tokens - HALO) // STEP, filtered, begin)
            for t in range(HALO):
                put(feature, t, half, groups, jnp.zeros((SUBLANES, LANES), f32))

            factor, weight = [], []
            for n in range(POLES):
                rate = rates[poled(n, half), :]
                factor.append(jnp.exp(-rate))
                weight.append(weights[poled(n, half), :] * jnp.sqrt(2.0 * rate))
            direct = tile(skip, 0, half, groups)

            def turn(i, state):
                for u in range(STEP):
                    t = HALO + i * STEP + u
                    m = tile(keys, t, half, groups)
                    state = [factor[n] * state[n] + m for n in range(POLES)]
                    sums = [direct * m, weight[0] * state[0]]
                    for n in range(1, POLES):
                        sums[n % 2] = sums[n % 2] + weight[n] * state[n]
                    gated = tile(feature, t, half, groups) * (sums[0] + sums[1])
                    put(streams, t, half, groups, tile(streams, t, half, groups) + gated)
                return tuple(state)

            state = (jnp.zeros((SUBLANES, LANES), f32),) * POLES
            turns = (tokens - HALO) // STEP
            done = 0
            for p in range(parts):
                last = min(turns, -((HALO - (p + 1) * tokens // parts) // STEP))
                state = lax.fori_loop(done, last, turn, state)
                done = last
                rows = slice(span * (parts * half + p), span * (parts * half + p + 1))
                for i, (source, target) in enumerate(
                    ((streams, base_hbm), (feature, feature_hbm))
                ):
                    slot = 2 * (parts * half + p) + i
                    outward.append(
                        pltpu.make_async_copy(
                            source.at[rows, :], target.at[rows, :], out_sem.at[slot]
                        )
                    )
                    outward[-1].start()
        for copy in outward:
            copy.wait()


def outer_kernel(
    place, carries, filters, decay, residue, skip, heads_low, heads_high,
    base_low, feature_low, base_high, feature_high, summed, squares,
    carried, before, rates, taps, weights, query, gated, sem,
):
    tokens, chans = summed.shape
    groups = chans // LANES
    lower = place[0] < MINOR * MIDDLE
    parts = 4
    pieces = 4
    every = 2 * pieces
    span = tokens // parts

    def copies_from(feature, base):
        copies = []
        piece = span // pieces
        for p in range(sem.shape[0] // 2):
            part = slice(p * piece * SUBLANES, (p + 1) * piece * SUBLANES)
            for i, (source, target) in enumerate(((feature, query), (base, gated))):
                copies.append(
                    pltpu.make_async_copy(
                        source.at[part, :], target.at[part, :], sem.at[2 * p + i]
                    )
                )
        return copies

    copies = copies_from(feature_low, base_low)

    @pl.when(lower)
    def _():
        for copy in copies:
            copy.start()

    @pl.when(jnp.logical_not(lower))
    def _():
        for copy in copies_from(feature_high, base_high):
            copy.start()

    fill_tables(filters, decay, rates, taps)
    for g in range(groups):
        weights[g * POLES : (g + 1) * POLES, :] = residue[:, g * LANES : (g + 1) * LANES]
    size = carries.shape[0] // MINOR
    rows = groups // MINOR * POLES
    for j in range(MINOR):
        piece = carries[j * size : (j + 1) * size, :].astype(f32)
        carried[j * rows : (j + 1) * rows, :] = piece[:rows]
        before[j * (size - rows) : (j + 1) * (size - rows), :] = piece[rows:]

    def chosen(low, high, item, half):
        return jnp.where(lower, tile(low, item, half, groups), tile(high, item, half, groups))

    for half in range(groups // SUBLANES):
        opening = []
        for i, at in enumerate((4, 0, 2)):
            line = [before[poled(at + r, half, RAW), :] for r in range(2)]
            line += [chosen(heads_low, heads_high, HALO * i + r, half) for r in range(2)]
            weight = taps_of(taps, i, half)
            opening.append([fir(weight, line[t + 2], line[t + 1], line[t]) for t in range(2)])
        mixed = [opening[1][t] * opening[2][t] for t in range(2)]
        factor, state, weight = [], [], []
        for n in range(POLES):
            rate = rates[poled(n, half), :]
            factor.append(jnp.exp(-rate))
            weight.append(weights[poled(n, half), :] * jnp.sqrt(2.0 * rate))
            state.append(weight[n] * (factor[n] * carried[poled(n, half), :] + mixed[0]))
        direct = tile(skip, 0, half, groups)

        def total_of(state, first):
            sums = [state[0] if first is None else first + state[0], state[1]]
            for n in range(2, POLES):
                sums[n % 2] = sums[n % 2] + state[n]
            return sums[0] + sums[1]

        start = []
        for t in range(HALO):
            if t:
                state = [factor[n] * state[n] + weight[n] * mixed[t] for n in range(POLES)]
            start.append(opening[0][t] * total_of(state, direct * mixed[t]))
        state = tuple(factor[n] * state[n] for n in range(POLES))

        def turn(i, state):
            for u in range(STEP):
                t = HALO + i * STEP + u
                added = tile(query, t, half, groups) * total_of(state, None)
                put(gated, t, half, groups, tile(gated, t, half, groups) + added)
                state = tuple(factor[n] * state[n] for n in range(POLES))
            return state

        turns = (tokens - HALO) // STEP
        done = 0
        for p in range(parts):
            for copy in copies[every * (parts * half + p) : every * (parts * half + p + 1)]:
                copy.wait()
            if p == 0:
                for t in range(HALO):
                    put(gated, t, half, groups, tile(gated, t, half, groups) + start[t])
            last = turns if p == parts - 1 else ((p + 1) * span - HALO) // STEP
            state = lax.fori_loop(done, last, turn, state)
            done = last
    total = jnp.zeros((tokens, LANES), f32)
    for g in range(groups):
        start = g // SUBLANES * tokens * SUBLANES + g % SUBLANES
        value = gated[pl.ds(start, tokens, stride=SUBLANES), :].astype(bf16)
        summed[:, g * LANES : (g + 1) * LANES] = value
        value = value.astype(f32)
        total = total + value * value
    squares[...] = jnp.broadcast_to(jnp.sum(total.T, axis=0, keepdims=True), squares.shape)


def norm_kernel(summed, squares, gain, stream_out, normed_out, normed, sem):
    tokens, chans = summed.shape
    parts = 4
    width = chans // parts
    stream = pltpu.make_async_copy(summed, stream_out, sem.at[parts])
    stream.start()
    mean = jnp.sum(squares[...], axis=0, keepdims=True) / D
    inverse = jnp.broadcast_to(lax.rsqrt(mean + EPSILON), (LANES, tokens)).T
    copies = []
    for part in range(parts):
        for g in range(part * width // LANES, (part + 1) * width // LANES):
            columns = slice(g * LANES, (g + 1) * LANES)
            normed[:, columns] = (
                summed[:, columns].astype(f32) * inverse * gain[g : g + 1, :]
            ).astype(bf16)
        columns = slice(part * width, (part + 1) * width)
        copies.append(
            pltpu.make_async_copy(normed.at[:, columns], normed_out.at[:, columns], sem.at[part])
        )
        copies[part].start()
    for copy in copies:
        copy.wait()
    stream.wait()


def layer(
    residual, query_in, key_in, value_in, short_filter, decay_rate, residue, skip_gain, norm_gain
):
    tokens, chans = residual.shape
    groups = chans // LANES
    count = MINOR * MIDDLE * MAJOR
    block = float(tokens)

    def shape(rows, kind=f32):
        return jax.ShapeDtypeStruct((rows, LANES), kind)

    def hold(rows):
        return pltpu.VMEM((rows, LANES), f32)

    smem = pl.BlockSpec(memory_space=pltpu.SMEM)
    vmem = pl.BlockSpec(memory_space=pltpu.VMEM)
    hbm = pl.BlockSpec(memory_space=pltpu.HBM)
    wide = pltpu.VMEM((tokens, chans), bf16)
    poled_rows = POLES * groups
    parcel_rows = (POLES + RAW) * groups + EXTRA * MINOR

    parcel = call(
        first_kernel,
        shape(parcel_rows, bf16),
        room=10.1,
        in_specs=[hbm] * 5,
        scratch=[
            wide,
            wide,
            pltpu.VMEM((8, chans), bf16),
            pltpu.VMEM(short_filter.shape, f32),
            pltpu.VMEM(decay_rate.shape, f32),
            hold(tokens * groups),
            hold(tokens * groups),
            hold(poled_rows),
            hold(poled_rows),
            hold(poled_rows),
            pltpu.SemaphoreType.DMA((3 + 8 * (groups // SUBLANES),)),
        ],
    )(query_in, key_in, value_in, short_filter, decay_rate)

    place = lax.axis_index("seq").astype(jnp.int32).reshape(1)
    lines = [[g * MINOR + j for j in range(MINOR)] for g in range(MIDDLE * MAJOR)]
    planes = [
        [(z * MIDDLE + y) * MINOR + j for y in range(MIDDLE)]
        for z in range(MAJOR)
        for j in range(MINOR)
    ]

    def exchange(x, members):
        return lax.all_to_all(x, "seq", 0, 0, axis_index_groups=members, tiled=True)

    tables_in = (short_filter, decay_rate)
    skip = skip_gain.reshape(groups, LANES)
    parcel, place = lax.optimization_barrier((parcel, place))
    arrived = exchange(parcel, lines)
    sums, prefix = call(
        functools.partial(minor_kernel, block),
        (shape(parcel_rows, bf16), shape(poled_rows)),
        in_specs=[smem, vmem, vmem, vmem, vmem],
    )(place, arrived, *tables_in, skip)
    line = arrived
    arrived = exchange(sums, planes)
    ahead = call(
        functools.partial(ahead_kernel, block),
        shape(parcel_rows // MINOR, bf16),
        in_specs=[smem, vmem, vmem, vmem],
    )(place, arrived, *tables_in)

    def inner(upper, place):
        return call(
            functools.partial(inner_kernel, upper),
            (
                shape(tokens * groups),
                shape(tokens * groups),
                shape(3 * HALO * groups),
            ),
            room=10.25,
            in_specs=[smem] + [hbm] * 8,
            out_specs=(hbm, hbm, vmem),
            scratch=[hold(groups)]
            + [pltpu.VMEM(short_filter.shape, f32), pltpu.VMEM(decay_rate.shape, f32)]
            + [wide] * 4
            + [pltpu.VMEM(residue.shape, f32)]
            + [hold(tokens * groups)] * 5
            + [hold(poled_rows)] * 3
            + [pltpu.SemaphoreType.DMA((4 + 4 * (groups // SUBLANES),))]
            + [pltpu.SemaphoreType.DMA((16,))],
        )(place, query_in, key_in, value_in, residual, residue, skip, *tables_in)

    place, ahead = lax.optimization_barrier((place, ahead))
    low = inner(False, place)
    *low, ahead = lax.optimization_barrier((*low, ahead))
    ahead = lax.ppermute(ahead, "seq", [(i, i + count // 2) for i in range(count // 2)])
    high = inner(True, place)
    carries = call(
        functools.partial(middle_kernel, block),
        shape(poled_rows + RAW * groups, bf16),
        in_specs=[smem] + [vmem] * 6,
    )(place, line, arrived, ahead, prefix, *tables_in)
    carries = exchange(carries, lines)
    members = lax.axis_size("chan")
    summed, squares = call(
        outer_kernel,
        (
            jax.ShapeDtypeStruct((tokens, chans), bf16),
            jax.ShapeDtypeStruct((members, tokens), f32),
        ),
        room=11.5,
        in_specs=[smem] + [vmem] * 7 + [hbm] * 4,
        scratch=[
            hold(poled_rows),
            hold(RAW * groups),
            hold(poled_rows),
            hold(poled_rows),
            hold(poled_rows),
            hold(tokens * groups),
            hold(tokens * groups),
            pltpu.SemaphoreType.DMA((64,)),
        ],
    )(
        place,
        carries,
        *tables_in,
        residue,
        skip,
        low[2],
        high[2],
        low[0],
        low[1],
        high[0],
        high[1],
    )
    squares = lax.all_to_all(squares, "chan", 0, 0, tiled=True)
    whole = jax.ShapeDtypeStruct((tokens, chans), bf16)
    return call(
        norm_kernel,
        (whole, whole),
        in_specs=[vmem] * 3,
        out_specs=(hbm, hbm),
        scratch=[wide, pltpu.SemaphoreType.DMA((5,))],
    )(summed, squares, norm_gain.reshape(groups, LANES))


def solution(mesh):
    whole = P("seq", "chan")
    in_specs = (whole, whole, whole, whole, P(None, None, "chan"))
    in_specs += (P(None, "chan"), P(None, "chan"), P("chan"), P("chan"))
    return jax.shard_map(
        layer, mesh=mesh, in_specs=in_specs, out_specs=(whole, whole), check_vma=False
    )
```
